128 devices in a mesh: space: 64 (over y, z, x), dp: 2 (over core).
Axes of the slice: x: 4, y: 4, z: 4, core: 2. Of those that a mesh axis runs over, the one named last changes fastest.
Arguments:
- states: bfloat16 [2, 32768, 512], P('dp', 'space'), may hold values from -6 to 6
- cotangent: bfloat16 [2, 32768, 512], P('dp', 'space'), may hold values from -6 to 6
- send_owner: int32 [4096], P('space'), may hold values from 0 to 63, as said below
- line_place: int32 [4096], P('space'), may hold values from 0 to 191, as said below
- gain_attn: float32 [512], replicated, may hold values from 0.1 to 1.9
- w_qkv: bfloat16 [512, 1536], replicated, may hold values from -0.25 to 0.25
- w_out: bfloat16 [512, 512], replicated, may hold values from -0.25 to 0.25
- gain_mlp: float32 [512], replicated, may hold values from 0.1 to 1.9
- w_up: bfloat16 [512, 2048], replicated, may hold values from -0.25 to 0.25
- w_down: bfloat16 [2048, 512], replicated, may hold values from -0.125 to 0.125
Outputs:
- output: bfloat16 [2, 32768, 512], P('dp', 'space')
- grad_states: bfloat16 [2, 32768, 512], P('dp', 'space')
- grad_gain_attn: float32 [512], replicated
- grad_qkv: float32 [512, 1536], replicated
- grad_out: float32 [512, 512], replicated
- grad_gain_mlp: float32 [512], replicated
- grad_up: float32 [512, 2048], replicated
- grad_down: float32 [2048, 512], replicated
The draws below stay inside these ranges and needn't reach their ends.
Inputs may be any that keep to these rules, and one draw needn't show every extreme that they name: `send_owner`: each block's owner is a space index. Owners' loads are skewed: the busiest attend 3 times the mean number of lines, some over none. Every device sends the same number of blocks to a given owner, at most 3; the busiest owners receive 3 blocks from every device. `line_place`: A block's place is its line's slot at the owner times 4 plus its position in the line. The places of the blocks that one owner receives are 0 to their number less one, each once; the 4 blocks of a line share owner and line slot.
All inputs are finite; a program needn't handle non-finite values.
Results may differ from the reference program's by a relative error of at most 0.017.
Values may be sent and summed in bfloat16 or wider, within the bound.
A program may use at most 128 MiB of HBM per device.

```python
import math
import jax
import jax.numpy as jnp
from jax import lax

D = 512
FF = 2048
HEADS = 8
SEG = 8
FRAG = 4
PAIR = 1
TOKENS = 32768
SNAPS = 2
N_SPACE = 64


def permute_lines(subkey):
    return jax.random.permutation(subkey, N_SPACE * PAIR)


def swap_into(load, target, candidates):
    other = jnp.argmax(candidates).astype(jnp.int32)
    needed = load[target] == 0
    first = load[target]
    second = load[other]
    load = load.at[other].set(jnp.where(needed, first, second))
    return load.at[target].set(jnp.where(needed, second, first))


def routing_tables(key):
    lines_group = N_SPACE * PAIR
    pattern = jnp.tile(jnp.array([3, 2, 1, 1, 1, 0, 0, 0], jnp.int32), N_SPACE // 8)
    shuffle = jax.random.permutation(jax.random.fold_in(key, 11), N_SPACE)
    load = pattern[shuffle]
    indices = jnp.arange(N_SPACE, dtype=jnp.int32)
    load = swap_into(load, 0, load > 0)
    load = swap_into(load, N_SPACE - 1, (load > 0) & (indices > 0))
    per_group = load * PAIR
    line_owner = jnp.repeat(jnp.arange(N_SPACE, dtype=jnp.int32), per_group, total_repeat_length=lines_group)
    subkeys = jax.random.split(jax.random.fold_in(key, 12), N_SPACE)
    orders = jax.vmap(permute_lines)(subkeys)
    owner = line_owner[orders].reshape(-1).astype(jnp.int32)
    total = N_SPACE * lines_group
    scores = jax.random.permutation(jax.random.fold_in(key, 13), total).astype(jnp.int32)
    combined = owner * total + scores
    ranking = jnp.argsort(combined, stable=True).astype(jnp.int32)
    position = jnp.zeros((total,), jnp.int32).at[ranking].set(jnp.arange(total, dtype=jnp.int32))
    received = N_SPACE * per_group
    offsets = (jnp.cumsum(received) - received).astype(jnp.int32)
    place = position - offsets[owner]
    return (owner, place.astype(jnp.int32))


def draw_send_owner(key, part):
    return routing_tables(key)[0]


def draw_line_place(key, part):
    return routing_tables(key)[1]


def shard_levels(key, extent, pieces, smallest, largest):
    level = 1.0
    for dim, shards_of in pieces:
        draws = jax.random.uniform(jax.random.fold_in(jax.random.fold_in(key, 6), dim), (shards_of,), jnp.float32, smallest / len(pieces), largest / len(pieces))
        level = level * jnp.repeat(jnp.exp(draws), extent[dim] // shards_of).reshape((-1,) + (1,) * (len(extent) - 1 - dim))
    return level


def centred(own_key, dims, scale, reach, pieces=(), held_as=jnp.bfloat16):
    level = shard_levels(own_key, dims, pieces, -0.22, 0.18) if pieces else 1.0
    values = jax.random.normal(own_key, dims, jnp.float32) * scale * level
    return jnp.minimum(jnp.maximum(values, -reach), reach).astype(held_as)


def setup_inputs(seed: int = 0) -> dict:
    seeds = jax.random.split(jax.random.key(seed), 11)
    return {
        "states": centred(seeds[0], (SNAPS, TOKENS, D), 1.0, 6.0, ((0, 2), (1, 64))),
        "cotangent": centred(seeds[1], (SNAPS, TOKENS, D), 1.0, 6.0, ((0, 2), (1, 64))),
        "send_owner": draw_send_owner(jax.random.fold_in(seeds[10], 71), 0),
        "line_place": draw_line_place(jax.random.fold_in(seeds[10], 71), 0),
        "gain_attn": jnp.clip(1.0 + 0.18 * jax.random.normal(seeds[4], (D,), jnp.float32), 0.1, 1.9),
        "w_qkv": centred(seeds[5], (D, 3 * D), D ** -0.5, 0.25),
        "w_out": centred(seeds[6], (D, D), D ** -0.5, 0.25),
        "gain_mlp": jnp.clip(1.0 + 0.18 * jax.random.normal(seeds[7], (D,), jnp.float32), 0.1, 1.9),
        "w_up": centred(seeds[8], (D, FF), D ** -0.5, 0.25),
        "w_down": centred(seeds[9], (FF, D), FF ** -0.5, 0.125),
    }


EPSILON = 1e-05

def norm_rows(values, gain):
    center = values - lax.optimization_barrier(jnp.mean(values, axis=-1, keepdims=True))
    spread = lax.optimization_barrier(jnp.mean(center * center, axis=-1, keepdims=True))
    return center * lax.rsqrt(spread + EPSILON) * gain

def gelu_back(pre_act, upstream):
    _, pullback = jax.vjp(jax.nn.gelu, pre_act)
    return pullback(upstream)[0]

def norm_back(values, gain, upstream):
    _, pullback = jax.vjp(norm_rows, values, gain)
    return pullback(upstream)

def contract_rows(left, right):
    return lax.dot_general(left, right, (((0,), (0,)), ((), ())), preferred_element_type=jnp.float32)

def line_weights(queries, keys_in):
    scale = queries.shape[-1] ** (-0.5)
    scores = jnp.einsum('nqhd,nkhd->nhqk', queries.astype(jnp.float32), keys_in.astype(jnp.float32)) * scale
    expo = jnp.exp(scores)
    return expo / lax.optimization_barrier(jnp.sum(expo, axis=-1, keepdims=True))

def attend_forward(packed):
    queries, keys_in, values_in = packed
    probs = line_weights(queries, keys_in)
    rounded = probs.astype(jnp.bfloat16)
    return jnp.einsum('nhqk,nkhd->nqhd', rounded.astype(jnp.float32), values_in.astype(jnp.float32)).astype(jnp.bfloat16)

def attend_backward(packed):
    queries, keys_in, values_in, upstream = packed
    scale = queries.shape[-1] ** (-0.5)
    probs = line_weights(queries, keys_in)
    rounded = probs.astype(jnp.bfloat16)
    upstream32 = upstream.astype(jnp.float32)
    dprob = jnp.einsum('nqhd,nkhd->nhqk', upstream32, values_in.astype(jnp.float32))
    dscore = probs * (dprob - lax.optimization_barrier(jnp.sum(dprob * probs, axis=-1, keepdims=True)))
    dscore_b = (dscore * scale).astype(jnp.bfloat16).astype(jnp.float32)
    dquery = jnp.einsum('nhqk,nkhd->nqhd', dscore_b, keys_in.astype(jnp.float32)).astype(jnp.bfloat16)
    dkey = jnp.einsum('nhqk,nqhd->nkhd', dscore_b, queries.astype(jnp.float32)).astype(jnp.bfloat16)
    dvalue = jnp.einsum('nhqk,nqhd->nkhd', rounded.astype(jnp.float32), upstream32).astype(jnp.bfloat16)
    return (dquery, dkey, dvalue)

def reference(states, cotangent, send_owner, line_place, gain_attn, w_qkv, w_out, gain_mlp, w_up, w_down):
    snaps, tokens, width = states.shape
    head_dim = width // HEADS
    nblocks = send_owner.shape[0]
    counts = jnp.zeros((N_SPACE,), jnp.int32).at[send_owner].add(1)
    offsets = jnp.cumsum(counts) - counts
    position = (offsets[send_owner] + line_place).astype(jnp.int32)
    order = jnp.zeros((nblocks,), jnp.int32).at[position].set(jnp.arange(nblocks, dtype=jnp.int32))
    line_count = snaps * nblocks // FRAG
    group = N_SPACE * N_SPACE // 8

    def to_lines(rows_arr):
        blocks = rows_arr.reshape(snaps, nblocks, SEG, -1)[:, order]
        return blocks.reshape(line_count // group, group, FRAG * SEG, -1)

    def from_lines(lines):
        blocks = lines.reshape(snaps, nblocks, SEG, -1)[:, position]
        return blocks.reshape(snaps * tokens, -1)
    rows = snaps * tokens
    flat = states.reshape(rows, width).astype(jnp.float32)
    normed = norm_rows(flat, gain_attn).astype(jnp.bfloat16)
    projected = jnp.dot(normed, w_qkv, preferred_element_type=jnp.float32).astype(jnp.bfloat16)
    lines = to_lines(projected)
    heads_shape = lines.shape[:3] + (HEADS, head_dim)
    queries = lines[..., :width].reshape(heads_shape)
    keys_in = lines[..., width:2 * width].reshape(heads_shape)
    values_in = lines[..., 2 * width:].reshape(heads_shape)
    attended = lax.map(attend_forward, (queries, keys_in, values_in))
    mixed = from_lines(attended.reshape(lines.shape[:3] + (width,)))
    hidden = (flat + jnp.dot(mixed, w_out, preferred_element_type=jnp.float32)).astype(jnp.bfloat16)
    hidden32 = hidden.astype(jnp.float32)
    normed_mlp = norm_rows(hidden32, gain_mlp).astype(jnp.bfloat16)
    pre_act = jnp.dot(normed_mlp, w_up, preferred_element_type=jnp.float32)
    activated = jax.nn.gelu(pre_act).astype(jnp.bfloat16)
    output = (hidden32 + jnp.dot(activated, w_down, preferred_element_type=jnp.float32)).astype(jnp.bfloat16)
    upstream = cotangent.reshape(rows, width)
    grad_down = contract_rows(activated, upstream)
    dpre = gelu_back(pre_act, jnp.dot(upstream, w_down.T, preferred_element_type=jnp.float32)).astype(jnp.bfloat16)
    grad_up = contract_rows(normed_mlp, dpre)
    dnormed_mlp = jnp.dot(dpre, w_up.T, preferred_element_type=jnp.float32)
    dhid_norm, grad_gain_mlp = norm_back(hidden32, gain_mlp, dnormed_mlp)
    dhidden = upstream.astype(jnp.float32) + dhid_norm
    dhidden_b = dhidden.astype(jnp.bfloat16)
    grad_out = contract_rows(mixed, dhidden_b)
    dmixed = jnp.dot(dhidden_b, w_out.T, preferred_element_type=jnp.float32).astype(jnp.bfloat16)
    dmixed_lines = to_lines(dmixed).reshape(heads_shape)
    dquery, dkey, dvalue = lax.map(attend_backward, (queries, keys_in, values_in, dmixed_lines))
    line_shape = lines.shape[:3] + (width,)
    dlines = jnp.concatenate([dquery.reshape(line_shape), dkey.reshape(line_shape), dvalue.reshape(line_shape)], axis=-1)
    dprojected = from_lines(dlines)
    grad_qkv = contract_rows(normed, dprojected)
    dnormed = jnp.dot(dprojected, w_qkv.T, preferred_element_type=jnp.float32).astype(jnp.bfloat16)
    dflat_norm, grad_gain_attn = norm_back(flat, gain_attn, dnormed.astype(jnp.float32))
    grad_states = (dhidden + dflat_norm).astype(jnp.bfloat16).reshape(states.shape)
    factor = 1.0 / math.sqrt(rows)
    return (output.reshape(states.shape), grad_states, grad_gain_attn * factor, grad_qkv * factor, grad_out * factor, grad_gain_mlp * factor, grad_up * factor, grad_down * factor)
```

```python
import math

import jax
import jax.numpy as jnp
from jax import lax
from jax.sharding import PartitionSpec as P

HEADS = 8
SEG = 8
FRAG = 4
BINS = 16
PAIRS = 4
CAP = 6

EPSILON = 1e-05
F32 = jnp.float32
BF16 = jnp.bfloat16


def dot(a, b, dims):
    return lax.dot_general(a, b, (dims, ((), ())), preferred_element_type=F32)


NN = ((1,), (0,))
NT = ((1,), (1,))
TN = ((0,), (0,))


def norm_stats(v):
    center = v - jnp.mean(v, axis=-1, keepdims=True)
    inv = lax.rsqrt(jnp.mean(center * center, axis=-1, keepdims=True) + EPSILON)
    return center * inv, inv


def norm_back(unit, inv, gain, upstream):
    g = upstream * gain
    m1 = jnp.mean(g, axis=-1, keepdims=True)
    m2 = jnp.mean(g * unit, axis=-1, keepdims=True)
    return inv * (g - m1 - unit * m2)


GELU_C = math.sqrt(2.0 / math.pi)


def gelu_parts(v):
    t = jnp.tanh(GELU_C * (v + 0.044715 * (v * v * v)))
    value = 0.5 * v * (1.0 + t)
    slope = 0.5 * (1.0 + t) + 0.5 * v * (1.0 - t * t) * (GELU_C * (1.0 + 3 * 0.044715 * (v * v)))
    return value, slope


def routing(owner, place, cap):
    n = owner.shape[0]
    ids = jnp.arange(n, dtype=jnp.int32)
    same = owner[:, None] == owner[None, :]
    rank = jnp.sum(same & (ids[None, :] < ids[:, None]), axis=1, dtype=jnp.int32)
    load = jnp.sum(same, axis=1, dtype=jnp.int32)
    first = rank == 0
    ahead = first[None, :] & (load[None, :] == load[:, None]) & (owner[None, :] < owner[:, None])
    index = jnp.sum(ahead, axis=1, dtype=jnp.int32)
    n3 = jnp.sum(first & (load == 3), dtype=jnp.int32)
    n2 = jnp.sum(first & (load == 2), dtype=jnp.int32)
    odd = (n3 % 2) == 1
    base3 = 3 * index
    base2 = 3 * n3 + 2 * index + jnp.where(odd & (index >= 1), 1, 0)
    base1 = 3 * n3 + 2 * n2 + jnp.where(odd & (n2 >= 2), 1, 0) + index
    base = jnp.where(load == 3, base3, jnp.where(load == 2, base2, base1))
    return base + rank, (base % cap) * n + place


def exchange(x):
    return lax.all_to_all(x, "space", split_axis=0, concat_axis=0, tiled=True)


def per_device(
    states, cotangent, send_owner, line_place, gain_attn, w_qkv, w_out, gain_mlp, w_up, w_down
):
    width = states.shape[2]
    rows = states.shape[1]
    nspace = lax.axis_size("space")
    total_rows = rows * nspace * lax.axis_size("dp")
    nblocks = send_owner.shape[0]
    cap = CAP
    slots = BINS * cap
    wide = 2 * (width // HEADS)
    head_dim = width // HEADS
    scale = head_dim ** (-0.5)
    slot, tag = routing(send_owner, line_place, cap)
    tags = jnp.sum(
        jnp.where(slot[None, :] == jnp.arange(slots, dtype=jnp.int32)[:, None], tag[None, :] + 1, 0), axis=1
    ) - 1
    tags = jnp.broadcast_to(tags.reshape(BINS, 1, cap), (BINS, PAIRS, cap)).reshape(nspace, cap)
    tags = exchange(tags).reshape(nspace * cap)
    nsorted = cap * nspace
    sorter = (jnp.arange(nsorted, dtype=jnp.int32)[:, None] == tags[None, :]).astype(BF16)
    target = (slot[:, None] * SEG + jnp.arange(SEG, dtype=jnp.int32)[None, :]).reshape(rows)
    pack = (jnp.arange(slots * SEG, dtype=jnp.int32)[:, None] == target[None, :]).astype(BF16)

    def to_lines(x, columns):
        x = x.reshape(BINS, cap * SEG, columns // wide // PAIRS, PAIRS, wide)
        x = x.transpose(0, 3, 1, 2, 4).reshape(nspace, cap * SEG, columns // PAIRS)
        got = exchange(x).reshape(nspace * cap, SEG * (columns // PAIRS))
        got = dot(sorter, got, NN).astype(BF16)
        return got.reshape(nsorted // FRAG, FRAG * SEG, columns // PAIRS)

    def from_lines(x):
        columns = x.shape[-1]
        back = dot(sorter, x.reshape(nsorted, SEG * columns), TN).astype(BF16)
        back = exchange(back.reshape(nspace, cap * SEG, columns))
        back = back.reshape(BINS, PAIRS, cap * SEG, columns // wide, wide).transpose(0, 2, 3, 1, 4)
        return back.reshape(slots * SEG, columns * PAIRS)

    flat_b = dot(pack, states[0], NN).astype(BF16)
    upstream = dot(pack, cotangent[0], NN).astype(BF16)
    flat = flat_b.astype(F32)
    unit_a, inv_a = norm_stats(flat)
    normed = (unit_a * gain_attn).astype(BF16)
    projected = dot(normed, w_qkv, NN).astype(BF16)
    lines = to_lines(projected, 3 * width)
    heads = (lines.shape[0], FRAG * SEG, 2, head_dim)
    queries = lines[..., :wide].reshape(heads)
    keys_in = lines[..., wide : 2 * wide].reshape(heads)
    values_in = lines[..., 2 * wide :].reshape(heads)
    expo = jnp.exp(jnp.einsum("nqhd,nkhd->nhqk", queries, keys_in, preferred_element_type=F32) * scale)
    probs = expo / jnp.sum(expo, axis=-1, keepdims=True)
    rounded = probs.astype(BF16)
    attended = jnp.einsum("nhqk,nkhd->nqhd", rounded, values_in, preferred_element_type=F32)
    attended = attended.astype(BF16).reshape(lines.shape[0], FRAG * SEG, wide)
    mixed = from_lines(attended)

    hidden = (flat + dot(mixed, w_out, NN)).astype(BF16)
    hidden32 = hidden.astype(F32)
    unit_m, inv_m = norm_stats(hidden32)
    normed_mlp = (unit_m * gain_mlp).astype(BF16)
    act32, slope = gelu_parts(dot(normed_mlp, w_up, NN))
    activated = act32.astype(BF16)
    output = (hidden32 + dot(activated, w_down, NN)).astype(BF16)
    dpre = (slope * dot(upstream, w_down, NT)).astype(BF16)
    dnormed_mlp = dot(dpre, w_up, NT)
    grad_gain_mlp = jnp.sum(unit_m * dnormed_mlp, axis=0)
    dhidden = upstream.astype(F32) + norm_back(unit_m, inv_m, gain_mlp, dnormed_mlp)
    dhidden_b = dhidden.astype(BF16)
    dmixed = dot(dhidden_b, w_out, NT).astype(BF16)
    grad_down = dot(activated, upstream, TN).astype(BF16)
    grad_up = dot(normed_mlp, dpre, TN).astype(BF16)
    grad_out = dot(mixed, dhidden_b, TN).astype(BF16)
    grad_down, grad_up, grad_out = lax.psum((grad_down, grad_up, grad_out), ("space", "dp"))

    dattended = to_lines(dmixed, width).reshape(heads)
    dprob = jnp.einsum("nqhd,nkhd->nhqk", dattended, values_in, preferred_element_type=F32)
    dscore = probs * (dprob - jnp.sum(dprob * probs, axis=-1, keepdims=True))
    dscore = (dscore * scale).astype(BF16)
    dquery = jnp.einsum("nhqk,nkhd->nqhd", dscore, keys_in, preferred_element_type=F32)
    dkey = jnp.einsum("nhqk,nqhd->nkhd", dscore, queries, preferred_element_type=F32)
    dvalue = jnp.einsum("nhqk,nqhd->nkhd", rounded, dattended, preferred_element_type=F32)
    parts = [v.astype(BF16).reshape(lines.shape[0], FRAG * SEG, wide) for v in (dquery, dkey, dvalue)]
    dprojected = from_lines(jnp.concatenate(parts, axis=-1))
    grad_qkv = dot(normed, dprojected, TN).astype(BF16)
    dnormed = dot(dprojected, w_qkv, NT).astype(BF16).astype(F32)
    grad_gain_attn = jnp.sum(unit_a * dnormed, axis=0)
    grad_states = (dhidden + norm_back(unit_a, inv_a, gain_attn, dnormed)).astype(BF16)
    output = dot(pack, output, TN).astype(BF16)
    grad_states = dot(pack, grad_states, TN).astype(BF16)
    grad_qkv, grad_gains = lax.psum((grad_qkv, jnp.stack([grad_gain_attn, grad_gain_mlp])), ("space", "dp"))
    factor = 1.0 / math.sqrt(total_rows)
    return (
        output[None],
        grad_states[None],
        grad_gains[0] * factor,
        grad_qkv.astype(F32) * factor,
        grad_out.astype(F32) * factor,
        grad_gains[1] * factor,
        grad_up.astype(F32) * factor,
        grad_down.astype(F32) * factor,
    )


def solution(mesh):
    placed = (
        P("dp", "space", None),
        P("dp", "space", None),
        P("space"),
        P("space"),
        P(),
        P(),
        P(),
        P(),
        P(),
        P(),
    )
    return jax.shard_map(
        per_device,
        mesh=mesh,
        in_specs=placed,
        out_specs=(P("dp", "space", None), P("dp", "space", None), P(), P(), P(), P(), P(), P()),
        check_vma=False,
    )
```

```python
import functools
import math

import jax
import jax.numpy as jnp
from jax import lax
from jax.experimental import pallas as pl
from jax.experimental.pallas import tpu as pltpu
from jax.sharding import PartitionSpec as P

HEADS = 8
SEG = 8
FRAG = 4
BINS = 16
PAIRS = 4
CAP = 6

EPSILON = 1e-05
F32 = jnp.float32
BF16 = jnp.bfloat16
MESH = pl.DeviceIdType.MESH


def dot(a, b, dims):
    return lax.dot_general(a, b, (dims, ((), ())), preferred_element_type=F32)


NN = ((1,), (0,))
NT = ((1,), (1,))
TN = ((0,), (0,))


def norm_stats(v):
    center = v - jnp.mean(v, axis=-1, keepdims=True)
    inv = lax.rsqrt(jnp.mean(center * center, axis=-1, keepdims=True) + EPSILON)
    return center * inv, inv


def norm_back(unit, inv, gain, upstream):
    g = upstream * gain
    m1 = jnp.mean(g, axis=-1, keepdims=True)
    m2 = jnp.mean(g * unit, axis=-1, keepdims=True)
    return inv * (g - m1 - unit * m2)


GELU_C = math.sqrt(2.0 / math.pi)


def gelu_parts(v):
    t = jnp.tanh(GELU_C * (v + 0.044715 * (v * v * v)))
    value = 0.5 * v * (1.0 + t)
    slope = 0.5 * (1.0 + t) + 0.5 * v * (1.0 - t * t) * (GELU_C * (1.0 + 3 * 0.044715 * (v * v)))
    return value, slope


def routing(owner, place, cap):
    n = owner.shape[0]
    ids = jnp.arange(n, dtype=jnp.int32)
    same = owner[:, None] == owner[None, :]
    rank = jnp.sum(same & (ids[None, :] < ids[:, None]), axis=1, dtype=jnp.int32)
    load = jnp.sum(same, axis=1, dtype=jnp.int32)
    first = rank == 0
    ahead = first[None, :] & (load[None, :] == load[:, None]) & (owner[None, :] < owner[:, None])
    index = jnp.sum(ahead, axis=1, dtype=jnp.int32)
    n3 = jnp.sum(first & (load == 3), dtype=jnp.int32)
    n2 = jnp.sum(first & (load == 2), dtype=jnp.int32)
    odd = (n3 % 2) == 1
    base3 = 3 * index
    base2 = 3 * n3 + 2 * index + jnp.where(odd & (index >= 1), 1, 0)
    base1 = 3 * n3 + 2 * n2 + jnp.where(odd & (n2 >= 2), 1, 0) + index
    base = jnp.where(load == 3, base3, jnp.where(load == 2, base2, base1))
    return base + rank, (base % cap) * n + place


def partner_of(me, k):
    ys = lax.rem(lax.div(me, 16) + lax.div(k, 16), 4)
    zs = lax.rem(lax.div(lax.rem(me, 16), 4) + lax.div(lax.rem(k, 16), 4), 4)
    xs = lax.rem(lax.rem(me, 4) + lax.rem(k, 4), 4)
    return ys * 16 + zs * 4 + xs


def greet_all(me, count):
    barrier = pltpu.get_barrier_semaphore()

    def greet(k, carry):
        pl.semaphore_signal(barrier, inc=1, device_id={"space": partner_of(me, k)}, device_id_type=MESH)
        return carry

    lax.fori_loop(1, count, greet, 0)
    pl.semaphore_wait(barrier, count - 1)


def remote(src, dst, send_sem, recv_sem, device):
    return pltpu.make_async_remote_copy(
        src_ref=src, dst_ref=dst, send_sem=send_sem, recv_sem=recv_sem,
        device_id={"space": device}, device_id_type=MESH,
    )


def lanes(j, pair):
    return pl.ds(pl.multiple_of(j * 512 + pair * 128, 128), 128)


def send_to_lines(me, count, pieces, src, recv, send_sem, recv_sem, extra=None):
    def send(k, carry):
        to = partner_of(me, k)
        for j in range(pieces):
            remote(src.at[lax.div(to, PAIRS), :, lanes(j, lax.rem(to, PAIRS))],
                   recv.at[me, :, pl.ds(128 * j, 128)], send_sem, recv_sem, to).start()
        if extra is not None:
            remote(extra[0].at[lax.div(to, PAIRS)], extra[1].at[me], extra[2], extra[3], to).start()
        return carry

    for j in range(pieces):
        pltpu.make_async_copy(src.at[lax.div(me, PAIRS), :, lanes(j, lax.rem(me, PAIRS))],
                              recv.at[me, :, pl.ds(128 * j, 128)], recv_sem).start()
    if extra is not None:
        pltpu.make_async_copy(extra[0].at[lax.div(me, PAIRS)], extra[1].at[me], extra[3]).start()
    lax.fori_loop(1, count, send, 0)


def send_home(me, count, pieces, src, home, send_sem, recv_sem):
    mine = lax.div(me, PAIRS)
    pair = lax.rem(me, PAIRS)

    def send(k, carry):
        to = partner_of(me, k)
        for j in range(pieces):
            remote(src.at[to, :, pl.ds(128 * j, 128)], home.at[mine, :, lanes(j, pair)],
                   send_sem, recv_sem, to).start()
        return carry

    for j in range(pieces):
        pltpu.make_async_copy(src.at[me, :, pl.ds(128 * j, 128)], home.at[mine, :, lanes(j, pair)], recv_sem).start()
    lax.fori_loop(1, count, send, 0)


def await_bytes(ref, sem):
    pltpu.make_async_copy(ref, ref, sem).wait()


def build_sorter(table, sorter):
    n = sorter.shape[0]
    for c in range(n // 128):
        ids = lax.broadcasted_iota(jnp.int32, (n, 128), 0)
        sorter[:, pl.ds(128 * c, 128)] = jnp.where(ids == table[c : c + 1, :] - 1, 1.0, 0.0).astype(BF16)


def sort_blocks(cap, recv, wide32, gathered, sorter, out):
    count = recv.shape[0]
    span = cap * SEG

    def widen(d, carry):
        for j in range(wide32.shape[0]):
            part = recv[d, :, pl.ds(128 * j, 128)]
            wide32[j, pl.ds(pl.multiple_of(d * span, 8), span), :] = part.astype(F32)
        return carry

    lax.fori_loop(0, count, widen, 0)

    for r in range(SEG):
        for s in range(cap):
            for j in range(wide32.shape[0]):
                part = wide32[j, pl.ds(s * SEG + r, count, stride=span), :]
                gathered[pl.ds(s * count, count), pl.ds(128 * j, 128)] = part.astype(BF16)
        out[r] = dot(sorter[...], gathered[...], NN).astype(BF16)


def unsort_blocks(cap, src, wide32, sorter, out):
    count = out.shape[0]
    span = cap * SEG
    for r in range(SEG):
        back = dot(sorter[...], src[r], TN)
        for s in range(cap):
            for j in range(wide32.shape[0]):
                part = back[s * count : (s + 1) * count, 128 * j : 128 * (j + 1)]
                wide32[j, pl.ds(s * SEG + r, count, stride=span), :] = part

    def narrow(d, carry):
        for j in range(wide32.shape[0]):
            part = wide32[j, pl.ds(pl.multiple_of(d * span, 8), span), :]
            out[d, :, pl.ds(128 * j, 128)] = part.astype(BF16)
        return carry

    lax.fori_loop(0, count, narrow, 0)


TILE = 32


def same_line():
    n = TILE * SEG
    a = lax.div(lax.rem(lax.broadcasted_iota(jnp.int32, (n, n), 0), TILE), FRAG)
    b = lax.div(lax.rem(lax.broadcasted_iota(jnp.int32, (n, n), 1), TILE), FRAG)
    return a == b


def head_probs(q, k, first, mask, scale):
    q = jnp.where(first, q, jnp.zeros_like(q))
    expo = jnp.where(mask, jnp.exp(dot(q, k, NT) * scale), 0.0)
    return expo / jnp.sum(expo, axis=-1, keepdims=True)


def forward_kernel(cap, scale, proj, tagt, mixed, lines, table, recv, trecv, wide32, gathered, sorter,
                   attended, wide128, back, sems):
    me = lax.axis_index("space")
    count = recv.shape[0]
    greet_all(me, count)
    send_to_lines(me, count, 3, proj, recv, sems.at[0], sems.at[1], (tagt, trecv, sems.at[2], sems.at[3]))
    await_bytes(trecv, sems.at[3])
    table[...] = jnp.sum(trecv[...], axis=0)
    build_sorter(table[...], sorter)
    await_bytes(recv, sems.at[1])
    sort_blocks(cap, recv, wide32, gathered, sorter, lines)
    n = TILE * SEG
    mask = same_line()
    low = lax.broadcasted_iota(jnp.int32, (n, 128), 1) < 64

    def attend(t, carry):
        part = pl.ds(pl.multiple_of(t * TILE, TILE), TILE)
        x = lines[:, part, :].reshape(n, 384)
        q, k, v = x[:, :128], x[:, 128:256], x[:, 256:]
        outs = []
        for first in (low, ~low):
            w = head_probs(q, k, first, mask, scale).astype(BF16)
            outs.append(dot(w, v, NN))
        attended[:, part, :] = jnp.where(low, outs[0], outs[1]).astype(BF16).reshape(SEG, TILE, 128)
        return carry

    lax.fori_loop(0, cap * count // TILE, attend, 0)
    unsort_blocks(cap, attended, wide128, sorter, back)
    send_home(me, count, 1, back, mixed, sems.at[4], sems.at[5])
    await_bytes(recv.at[pl.ds(0, count - 1)], sems.at[0])
    await_bytes(trecv.at[pl.ds(0, count - 1)], sems.at[2])
    await_bytes(back.at[pl.ds(0, count - 1)], sems.at[4])
    await_bytes(mixed, sems.at[5])


def backward_kernel(cap, scale, dmixed, lines, table, dproj, recv, wide128, gathered, sorter, dlines_in,
                    dlines, wide32, back, sems):
    me = lax.axis_index("space")
    count = recv.shape[0]
    greet_all(me, count)
    send_to_lines(me, count, 1, dmixed, recv, sems.at[0], sems.at[1])
    build_sorter(table[...], sorter)
    await_bytes(recv, sems.at[1])
    sort_blocks(cap, recv, wide128, gathered, sorter, dlines_in)
    n = TILE * SEG
    mask = same_line()
    low = lax.broadcasted_iota(jnp.int32, (n, 128), 1) < 64

    def attend(t, carry):
        part = pl.ds(pl.multiple_of(t * TILE, TILE), TILE)
        x = lines[:, part, :].reshape(n, 384)
        up = dlines_in[:, part, :].reshape(n, 128)
        q, k, v = x[:, :128], x[:, 128:256], x[:, 256:]
        outs = []
        for first in (low, ~low):
            p = head_probs(q, k, first, mask, scale)
            g = dot(jnp.where(first, up, jnp.zeros_like(up)), v, NT)
            ds = (p * (g - jnp.sum(g * p, axis=-1, keepdims=True)) * scale).astype(BF16)
            outs.append((dot(ds, k, NN), dot(ds, q, TN), dot(p.astype(BF16), up, TN)))
        for j in range(3):
            dlines[:, part, pl.ds(128 * j, 128)] = (
                jnp.where(low, outs[0][j], outs[1][j]).astype(BF16).reshape(SEG, TILE, 128)
            )
        return carry

    lax.fori_loop(0, cap * count // TILE, attend, 0)
    unsort_blocks(cap, dlines, wide32, sorter, back)
    send_home(me, count, 3, back, dproj, sems.at[2], sems.at[3])
    await_bytes(recv.at[pl.ds(0, count - 1)], sems.at[0])
    await_bytes(back.at[pl.ds(0, count - 1)], sems.at[2])
    await_bytes(dproj, sems.at[3])


VM = pl.BlockSpec(memory_space=pltpu.VMEM)


def forward_lines(proj, tagt, cap, count, scale):
    n = cap * count
    span = cap * SEG
    return pl.pallas_call(
        functools.partial(forward_kernel, cap, scale),
        out_shape=(
            jax.ShapeDtypeStruct((BINS, span, 512), BF16),
            jax.ShapeDtypeStruct((SEG, n, 384), BF16),
            jax.ShapeDtypeStruct((8, 128), jnp.int32),
        ),
        in_specs=[VM] * 2,
        out_specs=(VM,) * 3,
        scratch_shapes=[
            pltpu.VMEM((count, span, 384), BF16),
            pltpu.VMEM((count, 8, 128), jnp.int32),
            pltpu.VMEM((3, count * span, 128), F32),
            pltpu.VMEM((n, 384), BF16),
            pltpu.VMEM((n, n), BF16),
            pltpu.VMEM((SEG, n, 128), BF16),
            pltpu.VMEM((1, count * span, 128), F32),
            pltpu.VMEM((count, span, 128), BF16),
            pltpu.SemaphoreType.DMA((6,)),
        ],
        compiler_params=pltpu.CompilerParams(collective_id=1, has_side_effects=True, vmem_limit_bytes=60 << 20),
        name="forward_lines",
    )(proj, tagt)


def backward_lines(dmixed, lines, table, cap, count, scale):
    n = cap * count
    span = cap * SEG
    return pl.pallas_call(
        functools.partial(backward_kernel, cap, scale),
        out_shape=jax.ShapeDtypeStruct((BINS, span, 1536), BF16),
        in_specs=[VM] * 3,
        out_specs=VM,
        scratch_shapes=[
            pltpu.VMEM((count, span, 128), BF16),
            pltpu.VMEM((1, count * span, 128), F32),
            pltpu.VMEM((n, 128), BF16),
            pltpu.VMEM((n, n), BF16),
            pltpu.VMEM((SEG, n, 128), BF16),
            pltpu.VMEM((SEG, n, 384), BF16),
            pltpu.VMEM((3, count * span, 128), F32),
            pltpu.VMEM((count, span, 384), BF16),
            pltpu.SemaphoreType.DMA((4,)),
        ],
        compiler_params=pltpu.CompilerParams(collective_id=2, has_side_effects=True, vmem_limit_bytes=60 << 20),
        name="backward_lines",
    )(dmixed, lines, table)


def per_device(
    states, cotangent, send_owner, line_place, gain_attn, w_qkv, w_out, gain_mlp, w_up, w_down
):
    width = states.shape[2]
    rows = states.shape[1]
    nspace = lax.axis_size("space")
    total_rows = rows * nspace * lax.axis_size("dp")
    nblocks = send_owner.shape[0]
    cap = CAP
    slots = BINS * cap
    wide = 2 * (width // HEADS)
    head_dim = width // HEADS
    scale = head_dim ** (-0.5)
    slot, tag = routing(send_owner, line_place, cap)
    me = lax.axis_index("space")
    hit = slot[None, :] == jnp.arange(slots, dtype=jnp.int32)[:, None]
    tags = jnp.sum(jnp.where(hit, tag[None, :] + 1, 0), axis=1).reshape(BINS, cap // 2, 2)
    tags = jnp.pad(tags, ((0, 0), (0, 8 - cap // 2), (0, 0)))
    at_me = jnp.arange(nspace, dtype=jnp.int32) == me
    tagt = jnp.where(at_me[None, None, None, :], tags[..., None], 0).reshape(BINS, 8, 2 * nspace)
    target = (slot[:, None] * SEG + jnp.arange(SEG, dtype=jnp.int32)[None, :]).reshape(rows)
    pack = (jnp.arange(slots * SEG, dtype=jnp.int32)[:, None] == target[None, :]).astype(BF16)

    flat_b = dot(pack, states[0], NN).astype(BF16)
    upstream = dot(pack, cotangent[0], NN).astype(BF16)
    flat = flat_b.astype(F32)
    unit_a, inv_a = norm_stats(flat)
    normed = (unit_a * gain_attn).astype(BF16)
    projected = dot(normed, w_qkv, NN).astype(BF16)
    span = cap * SEG
    mixed, lines, table = forward_lines(projected.reshape(BINS, span, 3 * width), tagt, cap, nspace, scale)
    mixed = mixed.reshape(BINS * span, width)

    hidden = (flat + dot(mixed, w_out, NN)).astype(BF16)
    hidden32 = hidden.astype(F32)
    unit_m, inv_m = norm_stats(hidden32)
    normed_mlp = (unit_m * gain_mlp).astype(BF16)
    act32, slope = gelu_parts(dot(normed_mlp, w_up, NN))
    activated = act32.astype(BF16)
    output = (hidden32 + dot(activated, w_down, NN)).astype(BF16)
    dpre = (slope * dot(upstream, w_down, NT)).astype(BF16)
    dnormed_mlp = dot(dpre, w_up, NT)
    grad_gain_mlp = jnp.sum(unit_m * dnormed_mlp, axis=0)
    dhidden = upstream.astype(F32) + norm_back(unit_m, inv_m, gain_mlp, dnormed_mlp)
    dhidden_b = dhidden.astype(BF16)
    dmixed = dot(dhidden_b, w_out, NT).astype(BF16)
    grad_down = dot(activated, upstream, TN).astype(BF16)
    grad_up = dot(normed_mlp, dpre, TN).astype(BF16)
    grad_out = dot(mixed, dhidden_b, TN).astype(BF16)
    grad_down, grad_up, grad_out = lax.psum((grad_down, grad_up, grad_out), ("space", "dp"))

    dprojected = backward_lines(dmixed.reshape(BINS, span, width), lines, table, cap, nspace, scale)
    dprojected = dprojected.reshape(BINS * span, 3 * width)
    grad_qkv = dot(normed, dprojected, TN).astype(BF16)
    dnormed = dot(dprojected, w_qkv, NT).astype(BF16).astype(F32)
    grad_gain_attn = jnp.sum(unit_a * dnormed, axis=0)
    grad_states = (dhidden + norm_back(unit_a, inv_a, gain_attn, dnormed)).astype(BF16)
    output = dot(pack, output, TN).astype(BF16)
    grad_states = dot(pack, grad_states, TN).astype(BF16)
    grad_qkv, grad_gains = lax.psum((grad_qkv, jnp.stack([grad_gain_attn, grad_gain_mlp])), ("space", "dp"))
    factor = 1.0 / math.sqrt(total_rows)
    return (
        output[None],
        grad_states[None],
        grad_gains[0] * factor,
        grad_qkv.astype(F32) * factor,
        grad_out.astype(F32) * factor,
        grad_gains[1] * factor,
        grad_up.astype(F32) * factor,
        grad_down.astype(F32) * factor,
    )


def solution(mesh):
    placed = (
        P("dp", "space", None),
        P("dp", "space", None),
        P("space"),
        P("space"),
        P(),
        P(),
        P(),
        P(),
        P(),
        P(),
    )
    return jax.shard_map(
        per_device,
        mesh=mesh,
        in_specs=placed,
        out_specs=(P("dp", "space", None), P("dp", "space", None), P(), P(), P(), P(), P(), P()),
        check_vma=False,
    )
```

```python
import functools
import math

import jax
import jax.numpy as jnp
from jax import lax
from jax.experimental import pallas as pl
from jax.experimental.pallas import tpu as pltpu
from jax.sharding import PartitionSpec as P

HEADS = 8
SEG = 8
FRAG = 4
BINS = 16
PAIRS = 4
CAP = 6

EPSILON = 1e-05
F32 = jnp.float32
BF16 = jnp.bfloat16
MESH = pl.DeviceIdType.MESH


def dot(a, b, dims):
    return lax.dot_general(a, b, (dims, ((), ())), preferred_element_type=F32)


NN = ((1,), (0,))
NT = ((1,), (1,))
TN = ((0,), (0,))


def norm_stats(v):
    center = v - jnp.mean(v, axis=-1, keepdims=True)
    inv = lax.rsqrt(jnp.mean(center * center, axis=-1, keepdims=True) + EPSILON)
    return center * inv, inv


def norm_back(unit, inv, gain, upstream):
    g = upstream * gain
    m1 = jnp.mean(g, axis=-1, keepdims=True)
    m2 = jnp.mean(g * unit, axis=-1, keepdims=True)
    return inv * (g - m1 - unit * m2)


GELU_C = math.sqrt(2.0 / math.pi)


def gelu_parts(v):
    t = jnp.tanh(GELU_C * (v + 0.044715 * (v * v * v)))
    value = 0.5 * v * (1.0 + t)
    slope = 0.5 * (1.0 + t) + 0.5 * v * (1.0 - t * t) * (GELU_C * (1.0 + 3 * 0.044715 * (v * v)))
    return value, slope


def routing(owner, place, cap):
    n = owner.shape[0]
    ids = jnp.arange(n, dtype=jnp.int32)
    same = owner[:, None] == owner[None, :]
    rank = jnp.sum(same & (ids[None, :] < ids[:, None]), axis=1, dtype=jnp.int32)
    load = jnp.sum(same, axis=1, dtype=jnp.int32)
    first = rank == 0
    ahead = first[None, :] & (load[None, :] == load[:, None]) & (owner[None, :] < owner[:, None])
    index = jnp.sum(ahead, axis=1, dtype=jnp.int32)
    n3 = jnp.sum(first & (load == 3), dtype=jnp.int32)
    n2 = jnp.sum(first & (load == 2), dtype=jnp.int32)
    odd = (n3 % 2) == 1
    base3 = 3 * index
    base2 = 3 * n3 + 2 * index + jnp.where(odd & (index >= 1), 1, 0)
    base1 = 3 * n3 + 2 * n2 + jnp.where(odd & (n2 >= 2), 1, 0) + index
    base = jnp.where(load == 3, base3, jnp.where(load == 2, base2, base1))
    return base + rank, (base % cap) * n + place


def partner_of(me, k):
    ys = lax.rem(lax.div(me, 16) + lax.div(k, 16), 4)
    zs = lax.rem(lax.div(lax.rem(me, 16), 4) + lax.div(lax.rem(k, 16), 4), 4)
    xs = lax.rem(lax.rem(me, 4) + lax.rem(k, 4), 4)
    return ys * 16 + zs * 4 + xs


def greet_all(me, count, pair=False):
    barrier = pltpu.get_barrier_semaphore()

    def greet(k, carry):
        pl.semaphore_signal(barrier, inc=1, device_id={"space": partner_of(me, k)}, device_id_type=MESH)
        return carry

    lax.fori_loop(1, count, greet, 0)
    if pair:
        pl.semaphore_signal(barrier, inc=1, device_id={"dp": 1 - lax.axis_index("dp")}, device_id_type=MESH)
    pl.semaphore_wait(barrier, count if pair else count - 1)


def remote(src, dst, send_sem, recv_sem, device):
    return pltpu.make_async_remote_copy(
        src_ref=src, dst_ref=dst, send_sem=send_sem, recv_sem=recv_sem,
        device_id={"space": device}, device_id_type=MESH,
    )


def lanes(j, pair):
    return pl.ds(pl.multiple_of(j * 512 + pair * 128, 128), 128)


def send_to_lines(me, count, pieces, src, recv, send_sem, recv_sem, extra=None):
    def send(k, carry):
        to = partner_of(me, k)
        for j in range(pieces):
            remote(src.at[lax.div(to, PAIRS), :, lanes(j, lax.rem(to, PAIRS))],
                   recv.at[me, :, pl.ds(128 * j, 128)], send_sem, recv_sem, to).start()
        if extra is not None:
            remote(extra[0].at[lax.div(to, PAIRS)], extra[1].at[me], extra[2], extra[3], to).start()
        return carry

    for j in range(pieces):
        pltpu.make_async_copy(src.at[lax.div(me, PAIRS), :, lanes(j, lax.rem(me, PAIRS))],
                              recv.at[me, :, pl.ds(128 * j, 128)], recv_sem).start()
    if extra is not None:
        pltpu.make_async_copy(extra[0].at[lax.div(me, PAIRS)], extra[1].at[me], extra[3]).start()
    lax.fori_loop(1, count, send, 0)


def send_home(me, count, pieces, src, home, send_sem, recv_sem):
    mine = lax.div(me, PAIRS)
    pair = lax.rem(me, PAIRS)

    def send(k, carry):
        to = partner_of(me, k)
        for j in range(pieces):
            remote(src.at[to, :, pl.ds(128 * j, 128)], home.at[mine, :, lanes(j, pair)],
                   send_sem, recv_sem, to).start()
        return carry

    for j in range(pieces):
        pltpu.make_async_copy(src.at[me, :, pl.ds(128 * j, 128)], home.at[mine, :, lanes(j, pair)], recv_sem).start()
    lax.fori_loop(1, count, send, 0)


def await_bytes(ref, sem):
    pltpu.make_async_copy(ref, ref, sem).wait()


def build_sorter(table, sorter):
    n = sorter.shape[0]
    for c in range(n // 128):
        ids = lax.broadcasted_iota(jnp.int32, (n, 128), 0)
        sorter[:, pl.ds(128 * c, 128)] = jnp.where(ids == table[c : c + 1, :] - 1, 1.0, 0.0).astype(BF16)


def sort_blocks(cap, recv, wide32, gathered, sorter, out):
    count = recv.shape[0]
    span = cap * SEG

    def widen(d, carry):
        for j in range(wide32.shape[0]):
            part = recv[d, :, pl.ds(128 * j, 128)]
            wide32[j, pl.ds(pl.multiple_of(d * span, 8), span), :] = part.astype(F32)
        return carry

    lax.fori_loop(0, count, widen, 0)

    for r in range(SEG):
        for s in range(cap):
            for j in range(wide32.shape[0]):
                part = wide32[j, pl.ds(s * SEG + r, count, stride=span), :]
                gathered[pl.ds(s * count, count), pl.ds(128 * j, 128)] = part.astype(BF16)
        out[r] = dot(sorter[...], gathered[...], NN).astype(BF16)


def unsort_blocks(cap, src, wide32, sorter, out):
    count = out.shape[0]
    span = cap * SEG
    for r in range(SEG):
        back = dot(sorter[...], src[r], TN)
        for s in range(cap):
            for j in range(wide32.shape[0]):
                part = back[s * count : (s + 1) * count, 128 * j : 128 * (j + 1)]
                wide32[j, pl.ds(s * SEG + r, count, stride=span), :] = part

    def narrow(d, carry):
        for j in range(wide32.shape[0]):
            part = wide32[j, pl.ds(pl.multiple_of(d * span, 8), span), :]
            out[d, :, pl.ds(128 * j, 128)] = part.astype(BF16)
        return carry

    lax.fori_loop(0, count, narrow, 0)


TILE = 32


def same_line():
    n = TILE * SEG
    a = lax.div(lax.rem(lax.broadcasted_iota(jnp.int32, (n, n), 0), TILE), FRAG)
    b = lax.div(lax.rem(lax.broadcasted_iota(jnp.int32, (n, n), 1), TILE), FRAG)
    return a == b


def head_probs(q, k, first, mask, scale):
    q = jnp.where(first, q, jnp.zeros_like(q))
    expo = jnp.where(mask, jnp.exp(dot(q, k, NT) * scale), 0.0)
    return expo / jnp.sum(expo, axis=-1, keepdims=True)


def forward_kernel(cap, scale, proj, tagt, mixed, lines, table, recv, trecv, wide32, gathered, sorter,
                   attended, wide128, back, sems):
    me = lax.axis_index("space")
    count = recv.shape[0]
    greet_all(me, count)
    send_to_lines(me, count, 3, proj, recv, sems.at[0], sems.at[1], (tagt, trecv, sems.at[2], sems.at[3]))
    await_bytes(trecv, sems.at[3])
    table[...] = jnp.sum(trecv[...], axis=0)
    build_sorter(table[...], sorter)
    await_bytes(recv, sems.at[1])
    sort_blocks(cap, recv, wide32, gathered, sorter, lines)
    n = TILE * SEG
    mask = same_line()
    low = lax.broadcasted_iota(jnp.int32, (n, 128), 1) < 64

    def attend(t, carry):
        part = pl.ds(pl.multiple_of(t * TILE, TILE), TILE)
        x = lines[:, part, :].reshape(n, 384)
        q, k, v = x[:, :128], x[:, 128:256], x[:, 256:]
        outs = []
        for first in (low, ~low):
            w = head_probs(q, k, first, mask, scale).astype(BF16)
            outs.append(dot(w, v, NN))
        attended[:, part, :] = jnp.where(low, outs[0], outs[1]).astype(BF16).reshape(SEG, TILE, 128)
        return carry

    lax.fori_loop(0, cap * count // TILE, attend, 0)
    unsort_blocks(cap, attended, wide128, sorter, back)
    send_home(me, count, 1, back, mixed, sems.at[4], sems.at[5])
    await_bytes(recv.at[pl.ds(0, count - 1)], sems.at[0])
    await_bytes(trecv.at[pl.ds(0, count - 1)], sems.at[2])
    await_bytes(back.at[pl.ds(0, count - 1)], sems.at[4])
    await_bytes(mixed, sems.at[5])


VM = pl.BlockSpec(memory_space=pltpu.VMEM)


class Reducer:
    def __init__(self, me, g, out, pair, s0, r1, s1, r2, s2, r3, send, recv):
        self.me, self.g, self.out, self.pair, self.s0, self.r1, self.s1 = me, g, out, pair, s0, r1, s1
        self.r2, self.s2, self.r3, self.send, self.recv = r2, s2, r3, send, recv
        self.core = lax.axis_index("dp")
        self.place = (lax.div(me, 16), lax.rem(lax.div(me, 4), 4), lax.rem(me, 4))

    def peers(self, axis):
        step = (16, 4, 1)[axis]
        mine = self.place[axis]
        for k in (1, 2, 3):
            there = lax.rem(mine + k, 4)
            yield k - 1, there, self.me + (there - mine) * step

    def copy(self, stage, p, src, dst, device):
        pltpu.make_async_remote_copy(
            src_ref=src, dst_ref=dst, send_sem=self.send.at[stage, p], recv_sem=self.recv.at[stage, p],
            device_id=device, device_id_type=MESH,
        ).start()

    def wait(self, stage, p):
        await_bytes(self.sized(stage, p), self.recv.at[stage, p])

    def sized(self, stage, p):
        return (self.pair, self.r1, self.r2, self.r3, self.r3, self.r2, self.r1, self.pair)[stage].at[p]

    def start(self):
        for p in range(3):
            self.copy(0, p, self.g.at[1 - self.core, p], self.pair.at[p], {"dp": 1 - self.core})

    def step(self, stage):
        for p in range(3):
            self.wait(stage, p)
            a, b, c = p, (p + 1) % 3, (p + 2) % 3
            ia, ib, ic = self.place[a], self.place[b], self.place[c]
            shard = pl.ds(pl.multiple_of(ic * 128, 128), 128)
            own = self.out.at[self.core, p]
            if stage == 0:

                def add(i, carry):
                    u, v = lax.div(i, 4), lax.rem(i, 4)
                    self.s0[p, u, v] = (self.g[self.core, p, u, v].astype(F32) + self.pair[p, u, v].astype(F32)).astype(BF16)
                    return carry

                lax.fori_loop(0, 16, add, 0)
                for k, there, device in self.peers(a):
                    self.copy(1, p, self.s0.at[p, there], self.r1.at[p, k], {"space": device})
            elif stage == 1:

                def add4(u, carry):
                    total = self.s0[p, ia, u].astype(F32)
                    for k in range(3):
                        total += self.r1[p, k, u].astype(F32)
                    self.s1[p, u] = total.astype(BF16)
                    return carry

                lax.fori_loop(0, 4, add4, 0)
                for k, there, device in self.peers(b):
                    self.copy(2, p, self.s1.at[p, there], self.r2.at[p, k], {"space": device})
            elif stage == 2:
                total = self.s1[p, ib].astype(F32)
                for k in range(3):
                    total += self.r2[p, k].astype(F32)
                self.s2[p] = total.astype(BF16)
                for k, there, device in self.peers(c):
                    part = pl.ds(pl.multiple_of(there * 128, 128), 128)
                    self.copy(3, p, self.s2.at[p, :, part], self.r3.at[p, k], {"space": device})
            elif stage == 3:
                total = self.s2[p, :, shard].astype(F32)
                for k in range(3):
                    total += self.r3[p, k].astype(F32)
                own[ia, ib, :, shard] = total.astype(BF16)
                for k, there, device in self.peers(c):
                    piece = own.at[ia, ib, :, shard]
                    self.copy(4, p, piece, piece, {"space": device})
            elif stage == 4:
                for k, there, device in self.peers(b):
                    self.copy(5, p, own.at[ia, ib], own.at[ia, ib], {"space": device})
            elif stage == 5:
                for k, there, device in self.peers(a):
                    self.copy(6, p, own.at[ia], own.at[ia], {"space": device})
            elif stage == 6:
                self.copy(7, p, own, own, {"dp": 1 - self.core})

    def finish(self):
        for stage in range(8):
            for p in range(3):
                await_bytes(self.sized(stage, p), self.send.at[stage, p])


def reducer_scratch(q):
    return [
        pltpu.VMEM((3, 4, 4, q, 512), BF16),
        pltpu.VMEM((3, 4, 4, q, 512), BF16),
        pltpu.VMEM((3, 3, 4, q, 512), BF16),
        pltpu.VMEM((3, 4, q, 512), BF16),
        pltpu.VMEM((3, 3, q, 512), BF16),
        pltpu.VMEM((3, q, 512), BF16),
        pltpu.VMEM((3, 3, q, 128), BF16),
        pltpu.SemaphoreType.DMA((8, 3)),
        pltpu.SemaphoreType.DMA((8, 3)),
    ]


def sum_gains(stage, reducer, got, sems):
    slots, held, send, recv = got, sems[0], sems[1], sems[2]
    count = 2 if stage == 0 else 4
    mine = reducer.core if stage == 0 else reducer.place[stage - 1]
    slots[stage, mine] = held[stage]
    if stage == 0:
        pltpu.make_async_remote_copy(
            src_ref=held.at[0], dst_ref=slots.at[0, mine], send_sem=send.at[0], recv_sem=recv.at[0],
            device_id={"dp": 1 - mine}, device_id_type=MESH,
        ).start()
    else:
        for k, there, device in reducer.peers(stage - 1):
            remote(held.at[stage], slots.at[stage, mine], send.at[stage], recv.at[stage], device).start()


def gather_gains(stage, got, sems):
    slots, held, send, recv = got, sems[0], sems[1], sems[2]
    count = 2 if stage == 0 else 4
    await_bytes(slots.at[stage, pl.ds(0, count - 1)], recv.at[stage])
    total = slots[stage, 0]
    for k in range(1, count):
        total += slots[stage, k]
    return total


def tail_kernel(g, gains, out, gains_out, *scratch):
    me = lax.axis_index("space")
    red = Reducer(me, g, out, *scratch[:9])
    slots, held, gsend, grecv = scratch[9:]
    sems = (held, gsend, grecv)
    barrier = pltpu.get_barrier_semaphore()
    pl.semaphore_signal(barrier, inc=1, device_id={"dp": 1 - red.core}, device_id_type=MESH)
    for axis in range(3):
        for k, there, device in red.peers(axis):
            pl.semaphore_signal(barrier, inc=1, device_id={"space": device}, device_id_type=MESH)
    pl.semaphore_wait(barrier, 10)
    red.start()
    held[0] = gains[...]
    sum_gains(0, red, slots, sems)
    for stage in range(7):
        red.step(stage)
        if stage < 4:
            total = gather_gains(stage, slots, sems)
            if stage < 3:
                held[stage + 1] = total
                sum_gains(stage + 1, red, slots, sems)
            else:
                gains_out[...] = total
    for p in range(3):
        red.wait(7, p)
    red.finish()
    for stage in range(4):
        await_bytes(slots.at[stage, pl.ds(0, 1 if stage == 0 else 3)], gsend.at[stage])


def reduce_tail(g, gains):
    q = g.shape[0] // 96
    out, gains = pl.pallas_call(
        tail_kernel,
        out_shape=(
            jax.ShapeDtypeStruct((2, 3, 4, 4, q, 512), BF16),
            jax.ShapeDtypeStruct((8, 128), F32),
        ),
        in_specs=[VM] * 2,
        out_specs=(VM,) * 2,
        scratch_shapes=reducer_scratch(q)
        + [
            pltpu.VMEM((4, 4, 8, 128), F32),
            pltpu.VMEM((4, 8, 128), F32),
            pltpu.SemaphoreType.DMA((4,)),
            pltpu.SemaphoreType.DMA((4,)),
        ],
        compiler_params=pltpu.CompilerParams(collective_id=3, has_side_effects=True, vmem_limit_bytes=60 << 20),
        name="reduce_tail",
    )(g.reshape(2, 3, 4, 4, q, 512), gains)
    return out.reshape(g.shape), gains


def backward_kernel(cap, scale, dmixed, lines, table, g, dproj, out, recv, wide128, gathered, sorter, dlines_in,
                    dlines, wide32, back, sems, *scratch):
    me = lax.axis_index("space")
    count = recv.shape[0]
    red = Reducer(me, g, out, *scratch)
    greet_all(me, count, True)
    send_to_lines(me, count, 1, dmixed, recv, sems.at[0], sems.at[1])
    red.start()
    build_sorter(table[...], sorter)
    await_bytes(recv, sems.at[1])
    red.step(0)
    sort_blocks(cap, recv, wide128, gathered, sorter, dlines_in)
    n = TILE * SEG
    mask = same_line()
    low = lax.broadcasted_iota(jnp.int32, (n, 128), 1) < 64

    def attend(t, carry):
        part = pl.ds(pl.multiple_of(t * TILE, TILE), TILE)
        x = lines[:, part, :].reshape(n, 384)
        up = dlines_in[:, part, :].reshape(n, 128)
        q, k, v = x[:, :128], x[:, 128:256], x[:, 256:]
        outs = []
        for first in (low, ~low):
            p = head_probs(q, k, first, mask, scale)
            g = dot(jnp.where(first, up, jnp.zeros_like(up)), v, NT)
            ds = (p * (g - jnp.sum(g * p, axis=-1, keepdims=True)) * scale).astype(BF16)
            outs.append((dot(ds, k, NN), dot(ds, q, TN), dot(p.astype(BF16), up, TN)))
        for j in range(3):
            dlines[:, part, pl.ds(128 * j, 128)] = (
                jnp.where(low, outs[0][j], outs[1][j]).astype(BF16).reshape(SEG, TILE, 128)
            )
        return carry

    tiles = cap * count // TILE
    lax.fori_loop(0, tiles // 2, attend, 0)
    red.step(1)
    lax.fori_loop(tiles // 2, tiles, attend, 0)
    red.step(2)
    unsort_blocks(cap, dlines, wide32, sorter, back)
    send_home(me, count, 3, back, dproj, sems.at[2], sems.at[3])
    for stage in range(3, 7):
        red.step(stage)
    await_bytes(recv.at[pl.ds(0, count - 1)], sems.at[0])
    await_bytes(back.at[pl.ds(0, count - 1)], sems.at[2])
    await_bytes(dproj, sems.at[3])
    for p in range(3):
        red.wait(7, p)
    red.finish()


def forward_lines(proj, tagt, cap, count, scale):
    n = cap * count
    span = cap * SEG
    return pl.pallas_call(
        functools.partial(forward_kernel, cap, scale),
        out_shape=(
            jax.ShapeDtypeStruct((BINS, span, 512), BF16),
            jax.ShapeDtypeStruct((SEG, n, 384), BF16),
            jax.ShapeDtypeStruct((8, 128), jnp.int32),
        ),
        in_specs=[VM] * 2,
        out_specs=(VM,) * 3,
        scratch_shapes=[
            pltpu.VMEM((count, span, 384), BF16),
            pltpu.VMEM((count, 8, 128), jnp.int32),
            pltpu.VMEM((3, count * span, 128), F32),
            pltpu.VMEM((n, 384), BF16),
            pltpu.VMEM((n, n), BF16),
            pltpu.VMEM((SEG, n, 128), BF16),
            pltpu.VMEM((1, count * span, 128), F32),
            pltpu.VMEM((count, span, 128), BF16),
            pltpu.SemaphoreType.DMA((6,)),
        ],
        compiler_params=pltpu.CompilerParams(collective_id=1, has_side_effects=True, vmem_limit_bytes=60 << 20),
        name="forward_lines",
    )(proj, tagt)


def backward_lines(dmixed, lines, table, g, cap, count, scale):
    q = g.shape[0] // 96
    n = cap * count
    span = cap * SEG
    dproj, out = pl.pallas_call(
        functools.partial(backward_kernel, cap, scale),
        out_shape=(
            jax.ShapeDtypeStruct((BINS, span, 1536), BF16),
            jax.ShapeDtypeStruct((2, 3, 4, 4, q, 512), BF16),
        ),
        in_specs=[VM] * 4,
        out_specs=(VM,) * 2,
        scratch_shapes=[
            pltpu.VMEM((count, span, 128), BF16),
            pltpu.VMEM((1, count * span, 128), F32),
            pltpu.VMEM((n, 128), BF16),
            pltpu.VMEM((n, n), BF16),
            pltpu.VMEM((SEG, n, 128), BF16),
            pltpu.VMEM((SEG, n, 384), BF16),
            pltpu.VMEM((3, count * span, 128), F32),
            pltpu.VMEM((count, span, 384), BF16),
            pltpu.SemaphoreType.DMA((4,)),
        ]
        + reducer_scratch(q),
        compiler_params=pltpu.CompilerParams(collective_id=2, has_side_effects=True, vmem_limit_bytes=60 << 20),
        name="backward_lines",
    )(dmixed, lines, table, g.reshape(2, 3, 4, 4, q, 512))
    return dproj, out.reshape(g.shape)


def per_device(
    states, cotangent, send_owner, line_place, gain_attn, w_qkv, w_out, gain_mlp, w_up, w_down
):
    width = states.shape[2]
    rows = states.shape[1]
    nspace = lax.axis_size("space")
    total_rows = rows * nspace * lax.axis_size("dp")
    nblocks = send_owner.shape[0]
    cap = CAP
    slots = BINS * cap
    wide = 2 * (width // HEADS)
    head_dim = width // HEADS
    scale = head_dim ** (-0.5)
    slot, tag = routing(send_owner, line_place, cap)
    me = lax.axis_index("space")
    hit = slot[None, :] == jnp.arange(slots, dtype=jnp.int32)[:, None]
    tags = jnp.sum(jnp.where(hit, tag[None, :] + 1, 0), axis=1).reshape(BINS, cap // 2, 2)
    tags = jnp.pad(tags, ((0, 0), (0, 8 - cap // 2), (0, 0)))
    at_me = jnp.arange(nspace, dtype=jnp.int32) == me
    tagt = jnp.where(at_me[None, None, None, :], tags[..., None], 0).reshape(BINS, 8, 2 * nspace)
    target = (slot[:, None] * SEG + jnp.arange(SEG, dtype=jnp.int32)[None, :]).reshape(rows)
    pack = (jnp.arange(slots * SEG, dtype=jnp.int32)[:, None] == target[None, :]).astype(BF16)

    flat_b = dot(pack, states[0], NN).astype(BF16)
    upstream = dot(pack, cotangent[0], NN).astype(BF16)
    flat = flat_b.astype(F32)
    unit_a, inv_a = norm_stats(flat)
    normed = (unit_a * gain_attn).astype(BF16)
    projected = dot(normed, w_qkv, NN).astype(BF16)
    span = cap * SEG
    mixed, lines, table = forward_lines(projected.reshape(BINS, span, 3 * width), tagt, cap, nspace, scale)
    mixed = mixed.reshape(BINS * span, width)

    hidden = (flat + dot(mixed, w_out, NN)).astype(BF16)
    hidden32 = hidden.astype(F32)
    unit_m, inv_m = norm_stats(hidden32)
    normed_mlp = (unit_m * gain_mlp).astype(BF16)
    act32, slope = gelu_parts(dot(normed_mlp, w_up, NN))
    activated = act32.astype(BF16)
    output = (hidden32 + dot(activated, w_down, NN)).astype(BF16)
    dpre = (slope * dot(upstream, w_down, NT)).astype(BF16)
    dnormed_mlp = dot(dpre, w_up, NT)
    grad_gain_mlp = jnp.sum(unit_m * dnormed_mlp, axis=0)
    dhidden = upstream.astype(F32) + norm_back(unit_m, inv_m, gain_mlp, dnormed_mlp)
    dhidden_b = dhidden.astype(BF16)
    dmixed = dot(dhidden_b, w_out, NT).astype(BF16)
    early = [dot(activated, upstream, TN)]
    early += [dot(normed_mlp, dpre[:, j * width : (j + 1) * width], TN) for j in range(4)]
    early += [dot(mixed, dhidden_b, TN)]
    early = jnp.concatenate([v.astype(BF16) for v in early], axis=0)

    dprojected, early = backward_lines(dmixed.reshape(BINS, span, width), lines, table, early, cap, nspace, scale)
    dprojected = dprojected.reshape(BINS * span, 3 * width)
    late = [dot(normed, dprojected[:, j * width : (j + 1) * width], TN) for j in range(3)]
    late = jnp.concatenate([v.astype(BF16) for v in late], axis=0)
    dnormed = dot(dprojected, w_qkv, NT).astype(BF16).astype(F32)
    grad_gain_attn = jnp.sum(unit_a * dnormed, axis=0)
    grad_states = (dhidden + norm_back(unit_a, inv_a, gain_attn, dnormed)).astype(BF16)
    output = dot(pack, output, TN).astype(BF16)
    grad_states = dot(pack, grad_states, TN).astype(BF16)
    late, gains = reduce_tail(late, jnp.concatenate([grad_gain_attn, grad_gain_mlp]).reshape(8, 128))
    factor = 1.0 / math.sqrt(total_rows)
    gains = gains.reshape(2, width) * factor
    hidden_units = w_up.shape[1]

    def columns(blocks):
        blocks = blocks.reshape(-1, width, width)
        return jnp.concatenate([blocks[j].astype(F32) * factor for j in range(blocks.shape[0])], axis=1)

    return (
        output[None],
        grad_states[None],
        gains[0],
        columns(late),
        early[2 * hidden_units :].astype(F32) * factor,
        gains[1],
        columns(early[hidden_units : 2 * hidden_units]),
        early[:hidden_units].astype(F32) * factor,
    )


def solution(mesh):
    placed = (
        P("dp", "space", None),
        P("dp", "space", None),
        P("space"),
        P("space"),
        P(),
        P(),
        P(),
        P(),
        P(),
        P(),
    )
    return jax.shard_map(
        per_device,
        mesh=mesh,
        in_specs=placed,
        out_specs=(P("dp", "space", None), P("dp", "space", None), P(), P(), P(), P(), P(), P()),
        check_vma=False,
    )
```

```python
import functools
import math

import jax
import jax.numpy as jnp
from jax import lax
from jax.experimental import pallas as pl
from jax.experimental.pallas import tpu as pltpu
from jax.sharding import PartitionSpec as P

HEADS = 8
SEG = 8
FRAG = 4
BINS = 16
PAIRS = 4

EPSILON = 1e-05
F32 = jnp.float32
BF16 = jnp.bfloat16
MESH = pl.DeviceIdType.MESH


def dot(a, b, dims):
    return lax.dot_general(a, b, (dims, ((), ())), preferred_element_type=F32)


NN = ((1,), (0,))
NT = ((1,), (1,))
TN = ((0,), (0,))


def norm_stats(v):
    center = v - jnp.mean(v, axis=-1, keepdims=True)
    inv = lax.rsqrt(jnp.mean(center * center, axis=-1, keepdims=True) + EPSILON)
    return center * inv, inv


def norm_back(unit, inv, gain, upstream):
    g = upstream * gain
    m1 = jnp.mean(g, axis=-1, keepdims=True)
    m2 = jnp.mean(g * unit, axis=-1, keepdims=True)
    return inv * (g - m1 - unit * m2)


GELU_C = math.sqrt(2.0 / math.pi)


def gelu_parts(v):
    t = jnp.tanh(GELU_C * (v + 0.044715 * (v * v * v)))
    value = 0.5 * v * (1.0 + t)
    slope = 0.5 * (1.0 + t) + 0.5 * v * (1.0 - t * t) * (GELU_C * (1.0 + 3 * 0.044715 * (v * v)))
    return value, slope


def routing(owner, place, cap):
    n = owner.shape[0]
    ids = jnp.arange(n, dtype=jnp.int32)
    same = owner[:, None] == owner[None, :]
    rank = jnp.sum(same & (ids[None, :] < ids[:, None]), axis=1, dtype=jnp.int32)
    load = jnp.sum(same, axis=1, dtype=jnp.int32)
    first = rank == 0
    ahead = first[None, :] & (load[None, :] == load[:, None]) & (owner[None, :] < owner[:, None])
    index = jnp.sum(ahead, axis=1, dtype=jnp.int32)
    n3 = jnp.sum(first & (load == 3), dtype=jnp.int32)
    n2 = jnp.sum(first & (load == 2), dtype=jnp.int32)
    if cap == 4:
        spare = index < n3
        base1 = jnp.where(spare, 4 * index + 3, 3 * n3 + 2 * n2 + index)
        base = jnp.where(load == 3, 4 * index, jnp.where(load == 2, 4 * n3 + 2 * index, base1))
        return base + rank, (base % cap) * n + place
    odd = (n3 % 2) == 1
    base3 = 3 * index
    base2 = 3 * n3 + 2 * index + jnp.where(odd & (index >= 1), 1, 0)
    base1 = 3 * n3 + 2 * n2 + jnp.where(odd & (n2 >= 2), 1, 0) + index
    base = jnp.where(load == 3, base3, jnp.where(load == 2, base2, base1))
    return base + rank, (base % cap) * n + place


def partner_of(me, k):
    ys = lax.rem(lax.div(me, 16) + lax.div(k, 16), 4)
    zs = lax.rem(lax.div(lax.rem(me, 16), 4) + lax.div(lax.rem(k, 16), 4), 4)
    xs = lax.rem(lax.rem(me, 4) + lax.rem(k, 4), 4)
    return ys * 16 + zs * 4 + xs


def greet_all(me, count, pair=False):
    barrier = pltpu.get_barrier_semaphore()

    def greet(k, carry):
        pl.semaphore_signal(barrier, inc=1, device_id={"space": partner_of(me, k)}, device_id_type=MESH)
        return carry

    lax.fori_loop(1, count, greet, 0)
    if pair:
        pl.semaphore_signal(barrier, inc=1, device_id={"dp": 1 - lax.axis_index("dp")}, device_id_type=MESH)
    pl.semaphore_wait(barrier, count if pair else count - 1)


def remote(src, dst, send_sem, recv_sem, device):
    return pltpu.make_async_remote_copy(
        src_ref=src, dst_ref=dst, send_sem=send_sem, recv_sem=recv_sem,
        device_id={"space": device}, device_id_type=MESH,
    )


def lanes(j, pair):
    return pl.ds(pl.multiple_of(j * 512 + pair * 128, 128), 128)


def send_to_lines(me, count, pieces, src, recv, send_sem, recv_sem, extra=None):
    def send(k, carry):
        to = partner_of(me, k)
        for j in range(pieces):
            remote(src.at[lax.div(to, PAIRS), :, lanes(j, lax.rem(to, PAIRS))],
                   recv.at[me, :, pl.ds(128 * j, 128)], send_sem, recv_sem, to).start()
        if extra is not None:
            remote(extra[0].at[lax.div(to, PAIRS)], extra[1].at[me], extra[2], extra[3], to).start()
        return carry

    for j in range(pieces):
        pltpu.make_async_copy(src.at[lax.div(me, PAIRS), :, lanes(j, lax.rem(me, PAIRS))],
                              recv.at[me, :, pl.ds(128 * j, 128)], recv_sem).start()
    if extra is not None:
        pltpu.make_async_copy(extra[0].at[lax.div(me, PAIRS)], extra[1].at[me], extra[3]).start()
    lax.fori_loop(1, count, send, 0)


def send_home(me, count, pieces, src, home, send_sem, recv_sem):
    mine = lax.div(me, PAIRS)
    pair = lax.rem(me, PAIRS)

    def send(k, carry):
        to = partner_of(me, k)
        for j in range(pieces):
            remote(src.at[to, :, pl.ds(128 * j, 128)], home.at[mine, :, lanes(j, pair)],
                   send_sem, recv_sem, to).start()
        return carry

    for j in range(pieces):
        pltpu.make_async_copy(src.at[me, :, pl.ds(128 * j, 128)], home.at[mine, :, lanes(j, pair)], recv_sem).start()
    lax.fori_loop(1, count, send, 0)


def await_bytes(ref, sem):
    pltpu.make_async_copy(ref, ref, sem).wait()


def build_sorter(table, sorter):
    n = sorter.shape[0]
    for c in range(n // 128):
        ids = lax.broadcasted_iota(jnp.int32, (n, 128), 0)
        sorter[:, pl.ds(128 * c, 128)] = jnp.where(ids == table[c : c + 1, :] - 1, 1.0, 0.0).astype(BF16)


def sort_blocks(cap, recv, wide32, gathered, sorter, out):
    count = recv.shape[0]
    span = cap * SEG

    def widen(d, carry):
        for j in range(wide32.shape[0]):
            part = recv[d, :, pl.ds(128 * j, 128)]
            wide32[j, pl.ds(pl.multiple_of(d * span, 8), span), :] = part.astype(F32)
        return carry

    lax.fori_loop(0, count, widen, 0)

    for r in range(SEG):
        for s in range(cap):
            for j in range(wide32.shape[0]):
                part = wide32[j, pl.ds(s * SEG + r, count, stride=span), :]
                gathered[pl.ds(s * count, count), pl.ds(128 * j, 128)] = part.astype(BF16)
        out[r] = dot(sorter[...], gathered[...], NN).astype(BF16)


def unsort_blocks(cap, src, wide32, sorter, out):
    count = out.shape[0]
    span = cap * SEG
    for r in range(SEG):
        back = dot(sorter[...], src[r], TN)
        for s in range(cap):
            for j in range(wide32.shape[0]):
                part = back[s * count : (s + 1) * count, 128 * j : 128 * (j + 1)]
                wide32[j, pl.ds(s * SEG + r, count, stride=span), :] = part

    def narrow(d, carry):
        for j in range(wide32.shape[0]):
            part = wide32[j, pl.ds(pl.multiple_of(d * span, 8), span), :]
            out[d, :, pl.ds(128 * j, 128)] = part.astype(BF16)
        return carry

    lax.fori_loop(0, count, narrow, 0)


TILE = 32


def same_line():
    n = TILE * SEG
    a = lax.div(lax.rem(lax.broadcasted_iota(jnp.int32, (n, n), 0), TILE), FRAG)
    b = lax.div(lax.rem(lax.broadcasted_iota(jnp.int32, (n, n), 1), TILE), FRAG)
    return a == b


def head_probs(q, k, first, mask, scale):
    q = jnp.where(first, q, jnp.zeros_like(q))
    expo = jnp.where(mask, jnp.exp(dot(q, k, NT) * scale), 0.0)
    return expo / jnp.sum(expo, axis=-1, keepdims=True)


def forward_kernel(cap, scale, proj, tagt, mixed, lines, table, recv, trecv, wide32, gathered, sorter,
                   attended, wide128, back, sems):
    me = lax.axis_index("space")
    count = recv.shape[0]
    greet_all(me, count)
    send_to_lines(me, count, 3, proj, recv, sems.at[0], sems.at[1], (tagt, trecv, sems.at[2], sems.at[3]))
    await_bytes(trecv, sems.at[3])
    table[...] = jnp.sum(trecv[...], axis=0)
    build_sorter(table[...], sorter)
    await_bytes(recv, sems.at[1])
    sort_blocks(cap, recv, wide32, gathered, sorter, lines)
    n = TILE * SEG
    mask = same_line()
    low = lax.broadcasted_iota(jnp.int32, (n, 128), 1) < 64

    def attend(t, carry):
        part = pl.ds(pl.multiple_of(t * TILE, TILE), TILE)
        x = lines[:, part, :].reshape(n, 384)
        q, k, v = x[:, :128], x[:, 128:256], x[:, 256:]
        outs = []
        for first in (low, ~low):
            w = head_probs(q, k, first, mask, scale).astype(BF16)
            outs.append(dot(w, v, NN))
        attended[:, part, :] = jnp.where(low, outs[0], outs[1]).astype(BF16).reshape(SEG, TILE, 128)
        return carry

    lax.fori_loop(0, cap * count // TILE, attend, 0)
    unsort_blocks(cap, attended, wide128, sorter, back)
    send_home(me, count, 1, back, mixed, sems.at[4], sems.at[5])
    await_bytes(recv.at[pl.ds(0, count - 1)], sems.at[0])
    await_bytes(trecv.at[pl.ds(0, count - 1)], sems.at[2])
    await_bytes(back.at[pl.ds(0, count - 1)], sems.at[4])
    await_bytes(mixed, sems.at[5])


VM = pl.BlockSpec(memory_space=pltpu.VMEM)


class Reducer:
    def __init__(self, me, g, out, pair, s0, r1, s1, r2, s2, r3, send, recv):
        self.me, self.g, self.out, self.pair, self.s0, self.r1, self.s1 = me, g, out, pair, s0, r1, s1
        self.r2, self.s2, self.r3, self.send, self.recv = r2, s2, r3, send, recv
        self.core = lax.axis_index("dp")
        self.place = (lax.div(me, 16), lax.rem(lax.div(me, 4), 4), lax.rem(me, 4))

    def peers(self, axis):
        step = (16, 4, 1)[axis]
        mine = self.place[axis]
        for k in (1, 2, 3):
            there = lax.rem(mine + k, 4)
            yield k - 1, there, self.me + (there - mine) * step

    def copy(self, stage, p, src, dst, device):
        pltpu.make_async_remote_copy(
            src_ref=src, dst_ref=dst, send_sem=self.send.at[stage, p], recv_sem=self.recv.at[stage, p],
            device_id=device, device_id_type=MESH,
        ).start()

    def wait(self, stage, p):
        await_bytes(self.sized(stage, p), self.recv.at[stage, p])

    def sized(self, stage, p):
        return (self.pair, self.r1, self.r2, self.r3, self.r3, self.r2, self.r1, self.pair)[stage].at[p]

    def start(self):
        for p in range(3):
            self.copy(0, p, self.g.at[1 - self.core, p], self.pair.at[p], {"dp": 1 - self.core})

    def step(self, stage):
        for p in range(3):
            self.wait(stage, p)
            a, b, c = p, (p + 1) % 3, (p + 2) % 3
            ia, ib, ic = self.place[a], self.place[b], self.place[c]
            shard = pl.ds(pl.multiple_of(ic * 128, 128), 128)
            own = self.out.at[self.core, p]
            if stage == 0:

                def add(i, carry):
                    u, v = lax.div(i, 4), lax.rem(i, 4)
                    self.s0[p, u, v] = (self.g[self.core, p, u, v].astype(F32) + self.pair[p, u, v].astype(F32)).astype(BF16)
                    return carry

                lax.fori_loop(0, 16, add, 0)
                for k, there, device in self.peers(a):
                    self.copy(1, p, self.s0.at[p, there], self.r1.at[p, k], {"space": device})
            elif stage == 1:

                def add4(u, carry):
                    total = self.s0[p, ia, u].astype(F32)
                    for k in range(3):
                        total += self.r1[p, k, u].astype(F32)
                    self.s1[p, u] = total.astype(BF16)
                    return carry

                lax.fori_loop(0, 4, add4, 0)
                for k, there, device in self.peers(b):
                    self.copy(2, p, self.s1.at[p, there], self.r2.at[p, k], {"space": device})
            elif stage == 2:
                total = self.s1[p, ib].astype(F32)
                for k in range(3):
                    total += self.r2[p, k].astype(F32)
                self.s2[p] = total.astype(BF16)
                for k, there, device in self.peers(c):
                    part = pl.ds(pl.multiple_of(there * 128, 128), 128)
                    self.copy(3, p, self.s2.at[p, :, part], self.r3.at[p, k], {"space": device})
            elif stage == 3:
                total = self.s2[p, :, shard].astype(F32)
                for k in range(3):
                    total += self.r3[p, k].astype(F32)
                own[ia, ib, :, shard] = total.astype(BF16)
                for k, there, device in self.peers(c):
                    piece = own.at[ia, ib, :, shard]
                    self.copy(4, p, piece, piece, {"space": device})
            elif stage == 4:
                for k, there, device in self.peers(b):
                    self.copy(5, p, own.at[ia, ib], own.at[ia, ib], {"space": device})
            elif stage == 5:
                for k, there, device in self.peers(a):
                    self.copy(6, p, own.at[ia], own.at[ia], {"space": device})
            elif stage == 6:
                self.copy(7, p, own, own, {"dp": 1 - self.core})

    def finish(self):
        for stage in range(8):
            for p in range(3):
                await_bytes(self.sized(stage, p), self.send.at[stage, p])


def reducer_scratch(q):
    return [
        pltpu.VMEM((3, 4, 4, q, 512), BF16),
        pltpu.VMEM((3, 4, 4, q, 512), BF16),
        pltpu.VMEM((3, 3, 4, q, 512), BF16),
        pltpu.VMEM((3, 4, q, 512), BF16),
        pltpu.VMEM((3, 3, q, 512), BF16),
        pltpu.VMEM((3, q, 512), BF16),
        pltpu.VMEM((3, 3, q, 128), BF16),
        pltpu.SemaphoreType.DMA((8, 3)),
        pltpu.SemaphoreType.DMA((8, 3)),
    ]


def sum_gains(stage, reducer, got, sems):
    slots, held, send, recv = got, sems[0], sems[1], sems[2]
    count = 2 if stage == 0 else 4
    mine = reducer.core if stage == 0 else reducer.place[stage - 1]
    slots[stage, mine] = held[stage]
    if stage == 0:
        pltpu.make_async_remote_copy(
            src_ref=held.at[0], dst_ref=slots.at[0, mine], send_sem=send.at[0], recv_sem=recv.at[0],
            device_id={"dp": 1 - mine}, device_id_type=MESH,
        ).start()
    else:
        for k, there, device in reducer.peers(stage - 1):
            remote(held.at[stage], slots.at[stage, mine], send.at[stage], recv.at[stage], device).start()


def gather_gains(stage, got, sems):
    slots, held, send, recv = got, sems[0], sems[1], sems[2]
    count = 2 if stage == 0 else 4
    await_bytes(slots.at[stage, pl.ds(0, count - 1)], recv.at[stage])
    total = slots[stage, 0]
    for k in range(1, count):
        total += slots[stage, k]
    return total


def tail_kernel(g, gains, out, gains_out, *scratch):
    me = lax.axis_index("space")
    red = Reducer(me, g, out, *scratch[:9])
    slots, held, gsend, grecv = scratch[9:]
    sems = (held, gsend, grecv)
    barrier = pltpu.get_barrier_semaphore()
    pl.semaphore_signal(barrier, inc=1, device_id={"dp": 1 - red.core}, device_id_type=MESH)
    for axis in range(3):
        for k, there, device in red.peers(axis):
            pl.semaphore_signal(barrier, inc=1, device_id={"space": device}, device_id_type=MESH)
    pl.semaphore_wait(barrier, 10)
    red.start()
    held[0] = gains[...]
    sum_gains(0, red, slots, sems)
    for stage in range(7):
        red.step(stage)
        if stage < 4:
            total = gather_gains(stage, slots, sems)
            if stage < 3:
                held[stage + 1] = total
                sum_gains(stage + 1, red, slots, sems)
            else:
                gains_out[...] = total
    for p in range(3):
        red.wait(7, p)
    red.finish()
    for stage in range(4):
        await_bytes(slots.at[stage, pl.ds(0, 1 if stage == 0 else 3)], gsend.at[stage])


def reduce_tail(cap, g, gains):
    q = g.shape[0] // 96
    out, gains = pl.pallas_call(
        tail_kernel,
        out_shape=(
            jax.ShapeDtypeStruct((2, 3, 4, 4, q, 512), BF16),
            jax.ShapeDtypeStruct((8, 128), F32),
        ),
        in_specs=[VM] * 2,
        out_specs=(VM,) * 2,
        scratch_shapes=reducer_scratch(q)
        + [
            pltpu.VMEM((4, 4, 8, 128), F32),
            pltpu.VMEM((4, 8, 128), F32),
            pltpu.SemaphoreType.DMA((4,)),
            pltpu.SemaphoreType.DMA((4,)),
        ],
        compiler_params=pltpu.CompilerParams(collective_id=20 + cap, has_side_effects=True, vmem_limit_bytes=60 << 20),
        name="reduce_tail",
    )(g.reshape(2, 3, 4, 4, q, 512), gains)
    return out.reshape(g.shape), gains


def backward_kernel(cap, scale, dmixed, lines, table, g, dproj, out, recv, wide128, gathered, sorter, dlines_in,
                    dlines, wide32, back, sems, *scratch):
    me = lax.axis_index("space")
    count = recv.shape[0]
    red = Reducer(me, g, out, *scratch)
    greet_all(me, count, True)
    send_to_lines(me, count, 1, dmixed, recv, sems.at[0], sems.at[1])
    red.start()
    build_sorter(table[...], sorter)
    await_bytes(recv, sems.at[1])
    red.step(0)
    sort_blocks(cap, recv, wide128, gathered, sorter, dlines_in)
    n = TILE * SEG
    mask = same_line()
    low = lax.broadcasted_iota(jnp.int32, (n, 128), 1) < 64

    def attend(t, carry):
        part = pl.ds(pl.multiple_of(t * TILE, TILE), TILE)
        x = lines[:, part, :].reshape(n, 384)
        up = dlines_in[:, part, :].reshape(n, 128)
        q, k, v = x[:, :128], x[:, 128:256], x[:, 256:]
        outs = []
        for first in (low, ~low):
            p = head_probs(q, k, first, mask, scale)
            g = dot(jnp.where(first, up, jnp.zeros_like(up)), v, NT)
            ds = (p * (g - jnp.sum(g * p, axis=-1, keepdims=True)) * scale).astype(BF16)
            outs.append((dot(ds, k, NN), dot(ds, q, TN), dot(p.astype(BF16), up, TN)))
        for j in range(3):
            dlines[:, part, pl.ds(128 * j, 128)] = (
                jnp.where(low, outs[0][j], outs[1][j]).astype(BF16).reshape(SEG, TILE, 128)
            )
        return carry

    tiles = cap * count // TILE
    lax.fori_loop(0, tiles // 2, attend, 0)
    red.step(1)
    lax.fori_loop(tiles // 2, tiles, attend, 0)
    red.step(2)
    unsort_blocks(cap, dlines, wide32, sorter, back)
    send_home(me, count, 3, back, dproj, sems.at[2], sems.at[3])
    for stage in range(3, 7):
        red.step(stage)
    await_bytes(recv.at[pl.ds(0, count - 1)], sems.at[0])
    await_bytes(back.at[pl.ds(0, count - 1)], sems.at[2])
    await_bytes(dproj, sems.at[3])
    for p in range(3):
        red.wait(7, p)
    red.finish()


def forward_lines(proj, tagt, cap, count, scale):
    n = cap * count
    span = cap * SEG
    return pl.pallas_call(
        functools.partial(forward_kernel, cap, scale),
        out_shape=(
            jax.ShapeDtypeStruct((BINS, span, 512), BF16),
            jax.ShapeDtypeStruct((SEG, n, 384), BF16),
            jax.ShapeDtypeStruct((8, 128), jnp.int32),
        ),
        in_specs=[VM] * 2,
        out_specs=(VM,) * 3,
        scratch_shapes=[
            pltpu.VMEM((count, span, 384), BF16),
            pltpu.VMEM((count, 8, 128), jnp.int32),
            pltpu.VMEM((3, count * span, 128), F32),
            pltpu.VMEM((n, 384), BF16),
            pltpu.VMEM((n, n), BF16),
            pltpu.VMEM((SEG, n, 128), BF16),
            pltpu.VMEM((1, count * span, 128), F32),
            pltpu.VMEM((count, span, 128), BF16),
            pltpu.SemaphoreType.DMA((6,)),
        ],
        compiler_params=pltpu.CompilerParams(collective_id=cap, has_side_effects=True, vmem_limit_bytes=60 << 20),
        name="forward_lines",
    )(proj, tagt)


def backward_lines(dmixed, lines, table, g, cap, count, scale):
    q = g.shape[0] // 96
    n = cap * count
    span = cap * SEG
    dproj, out = pl.pallas_call(
        functools.partial(backward_kernel, cap, scale),
        out_shape=(
            jax.ShapeDtypeStruct((BINS, span, 1536), BF16),
            jax.ShapeDtypeStruct((2, 3, 4, 4, q, 512), BF16),
        ),
        in_specs=[VM] * 4,
        out_specs=(VM,) * 2,
        scratch_shapes=[
            pltpu.VMEM((count, span, 128), BF16),
            pltpu.VMEM((1, count * span, 128), F32),
            pltpu.VMEM((n, 128), BF16),
            pltpu.VMEM((n, n), BF16),
            pltpu.VMEM((SEG, n, 128), BF16),
            pltpu.VMEM((SEG, n, 384), BF16),
            pltpu.VMEM((3, count * span, 128), F32),
            pltpu.VMEM((count, span, 384), BF16),
            pltpu.SemaphoreType.DMA((4,)),
        ]
        + reducer_scratch(q),
        compiler_params=pltpu.CompilerParams(collective_id=10 + cap, has_side_effects=True, vmem_limit_bytes=60 << 20),
        name="backward_lines",
    )(dmixed, lines, table, g.reshape(2, 3, 4, 4, q, 512))
    return dproj, out.reshape(g.shape)


def fits_four(owner):
    same = owner[:, None] == owner[None, :]
    load = jnp.sum(same, axis=1, dtype=jnp.int32)
    threes = jnp.sum(load == 3, dtype=jnp.int32)
    twos = jnp.sum(load == 2, dtype=jnp.int32)
    return 4 * threes + 3 * twos <= 3 * owner.shape[0]


def per_device(*args):
    return lax.cond(fits_four(args[2]), functools.partial(block, 4), functools.partial(block, 6), *args)


def block(
    cap, states, cotangent, send_owner, line_place, gain_attn, w_qkv, w_out, gain_mlp, w_up, w_down
):
    width = states.shape[2]
    rows = states.shape[1]
    nspace = lax.axis_size("space")
    total_rows = rows * nspace * lax.axis_size("dp")
    nblocks = send_owner.shape[0]
    slots = BINS * cap
    wide = 2 * (width // HEADS)
    head_dim = width // HEADS
    scale = head_dim ** (-0.5)
    slot, tag = routing(send_owner, line_place, cap)
    me = lax.axis_index("space")
    hit = slot[None, :] == jnp.arange(slots, dtype=jnp.int32)[:, None]
    tags = jnp.sum(jnp.where(hit, tag[None, :] + 1, 0), axis=1).reshape(BINS, cap // 2, 2)
    tags = jnp.pad(tags, ((0, 0), (0, 8 - cap // 2), (0, 0)))
    at_me = jnp.arange(nspace, dtype=jnp.int32) == me
    tagt = jnp.where(at_me[None, None, None, :], tags[..., None], 0).reshape(BINS, 8, 2 * nspace)
    target = (slot[:, None] * SEG + jnp.arange(SEG, dtype=jnp.int32)[None, :]).reshape(rows)
    pack = (jnp.arange(slots * SEG, dtype=jnp.int32)[:, None] == target[None, :]).astype(BF16)

    flat_b = dot(pack, states[0], NN).astype(BF16)
    upstream = dot(pack, cotangent[0], NN).astype(BF16)
    flat = flat_b.astype(F32)
    unit_a, inv_a = norm_stats(flat)
    normed = (unit_a * gain_attn).astype(BF16)
    projected = dot(normed, w_qkv, NN).astype(BF16)
    span = cap * SEG
    mixed, lines, table = forward_lines(projected.reshape(BINS, span, 3 * width), tagt, cap, nspace, scale)
    mixed = mixed.reshape(BINS * span, width)

    hidden = (flat + dot(mixed, w_out, NN)).astype(BF16)
    hidden32 = hidden.astype(F32)
    unit_m, inv_m = norm_stats(hidden32)
    normed_mlp = (unit_m * gain_mlp).astype(BF16)
    act32, slope = gelu_parts(dot(normed_mlp, w_up, NN))
    activated = act32.astype(BF16)
    output = (hidden32 + dot(activated, w_down, NN)).astype(BF16)
    dpre = (slope * dot(upstream, w_down, NT)).astype(BF16)
    dnormed_mlp = dot(dpre, w_up, NT)
    grad_gain_mlp = jnp.sum(unit_m * dnormed_mlp, axis=0)
    dhidden = upstream.astype(F32) + norm_back(unit_m, inv_m, gain_mlp, dnormed_mlp)
    dhidden_b = dhidden.astype(BF16)
    dmixed = dot(dhidden_b, w_out, NT).astype(BF16)
    early = [dot(activated, upstream, TN)]
    early += [dot(normed_mlp, dpre[:, j * width : (j + 1) * width], TN) for j in range(4)]
    early += [dot(mixed, dhidden_b, TN)]
    early = jnp.concatenate([v.astype(BF16) for v in early], axis=0)

    dprojected, early = backward_lines(dmixed.reshape(BINS, span, width), lines, table, early, cap, nspace, scale)
    dprojected = dprojected.reshape(BINS * span, 3 * width)
    late = [dot(normed, dprojected[:, j * width : (j + 1) * width], TN) for j in range(3)]
    late = jnp.concatenate([v.astype(BF16) for v in late], axis=0)
    dnormed = dot(dprojected, w_qkv, NT).astype(BF16).astype(F32)
    grad_gain_attn = jnp.sum(unit_a * dnormed, axis=0)
    grad_states = (dhidden + norm_back(unit_a, inv_a, gain_attn, dnormed)).astype(BF16)
    output = dot(pack, output, TN).astype(BF16)
    grad_states = dot(pack, grad_states, TN).astype(BF16)
    late, gains = reduce_tail(cap, late, jnp.concatenate([grad_gain_attn, grad_gain_mlp]).reshape(8, 128))
    factor = 1.0 / math.sqrt(total_rows)
    gains = gains.reshape(2, width) * factor
    hidden_units = w_up.shape[1]

    def columns(blocks):
        blocks = blocks.reshape(-1, width, width)
        return jnp.concatenate([blocks[j].astype(F32) * factor for j in range(blocks.shape[0])], axis=1)

    return (
        output[None],
        grad_states[None],
        gains[0],
        columns(late),
        early[2 * hidden_units :].astype(F32) * factor,
        gains[1],
        columns(early[hidden_units : 2 * hidden_units]),
        early[:hidden_units].astype(F32) * factor,
    )


def solution(mesh):
    placed = (
        P("dp", "space", None),
        P("dp", "space", None),
        P("space"),
        P("space"),
        P(),
        P(),
        P(),
        P(),
        P(),
        P(),
    )
    return jax.shard_map(
        per_device,
        mesh=mesh,
        in_specs=placed,
        out_specs=(P("dp", "space", None), P("dp", "space", None), P(), P(), P(), P(), P(), P()),
        check_vma=False,
    )
```

```python
import functools
import math

import jax
import jax.numpy as jnp
from jax import lax
from jax.experimental import pallas as pl
from jax.experimental.pallas import tpu as pltpu
from jax.sharding import PartitionSpec as P

HEADS = 8
SEG = 8
FRAG = 4
BINS = 16
PAIRS = 4

EPSILON = 1e-05
F32 = jnp.float32
BF16 = jnp.bfloat16
MESH = pl.DeviceIdType.MESH


def dot(a, b, dims):
    return lax.dot_general(a, b, (dims, ((), ())), preferred_element_type=F32)


NN = ((1,), (0,))
NT = ((1,), (1,))
TN = ((0,), (0,))


def norm_stats(v):
    center = v - jnp.mean(v, axis=-1, keepdims=True)
    inv = lax.rsqrt(jnp.mean(center * center, axis=-1, keepdims=True) + EPSILON)
    return center * inv, inv


def norm_back(unit, inv, gain, upstream):
    g = upstream * gain
    m1 = jnp.mean(g, axis=-1, keepdims=True)
    m2 = jnp.mean(g * unit, axis=-1, keepdims=True)
    return inv * (g - m1 - unit * m2)


GELU_C = math.sqrt(2.0 / math.pi)


def gelu_parts(v):
    t = jnp.tanh(GELU_C * (v + 0.044715 * (v * v * v)))
    value = 0.5 * v * (1.0 + t)
    slope = 0.5 * (1.0 + t) + 0.5 * v * (1.0 - t * t) * (GELU_C * (1.0 + 3 * 0.044715 * (v * v)))
    return value, slope


def routing(owner, place, cap):
    n = owner.shape[0]
    ids = jnp.arange(n, dtype=jnp.int32)
    same = owner[:, None] == owner[None, :]
    rank = jnp.sum(same & (ids[None, :] < ids[:, None]), axis=1, dtype=jnp.int32)
    load = jnp.sum(same, axis=1, dtype=jnp.int32)
    first = rank == 0
    ahead = first[None, :] & (load[None, :] == load[:, None]) & (owner[None, :] < owner[:, None])
    index = jnp.sum(ahead, axis=1, dtype=jnp.int32)
    n3 = jnp.sum(first & (load == 3), dtype=jnp.int32)
    n2 = jnp.sum(first & (load == 2), dtype=jnp.int32)
    if cap == 4:
        spare = index < n3
        base1 = jnp.where(spare, 4 * index + 3, 3 * n3 + 2 * n2 + index)
        base = jnp.where(load == 3, 4 * index, jnp.where(load == 2, 4 * n3 + 2 * index, base1))
        return base + rank, (base % cap) * n + place
    odd = (n3 % 2) == 1
    base3 = 3 * index
    base2 = 3 * n3 + 2 * index + jnp.where(odd & (index >= 1), 1, 0)
    base1 = 3 * n3 + 2 * n2 + jnp.where(odd & (n2 >= 2), 1, 0) + index
    base = jnp.where(load == 3, base3, jnp.where(load == 2, base2, base1))
    return base + rank, (base % cap) * n + place


def partner_of(me, k):
    ys = lax.rem(lax.div(me, 16) + lax.div(k, 16), 4)
    zs = lax.rem(lax.div(lax.rem(me, 16), 4) + lax.div(lax.rem(k, 16), 4), 4)
    xs = lax.rem(lax.rem(me, 4) + lax.rem(k, 4), 4)
    return ys * 16 + zs * 4 + xs


def greet_all(me, count, pair=False):
    barrier = pltpu.get_barrier_semaphore()

    def greet(k, carry):
        pl.semaphore_signal(barrier, inc=1, device_id={"space": partner_of(me, k)}, device_id_type=MESH)
        return carry

    lax.fori_loop(1, count, greet, 0)
    if pair:
        pl.semaphore_signal(barrier, inc=1, device_id={"dp": 1 - lax.axis_index("dp")}, device_id_type=MESH)
    pl.semaphore_wait(barrier, count if pair else count - 1)


def remote(src, dst, send_sem, recv_sem, device):
    return pltpu.make_async_remote_copy(
        src_ref=src, dst_ref=dst, send_sem=send_sem, recv_sem=recv_sem,
        device_id={"space": device}, device_id_type=MESH,
    )


def lanes(j, pair):
    return pl.ds(pl.multiple_of(j * 512 + pair * 128, 128), 128)


def send_to_lines(me, count, pieces, src, recv, send_sem, recv_sem, extra=None):
    def send(k, carry):
        to = partner_of(me, k)
        for j in range(pieces):
            remote(src.at[lax.div(to, PAIRS), :, lanes(j, lax.rem(to, PAIRS))],
                   recv.at[me, :, pl.ds(128 * j, 128)], send_sem, recv_sem, to).start()
        if extra is not None:
            remote(extra[0].at[lax.div(to, PAIRS)], extra[1].at[me], extra[2], extra[3], to).start()
        return carry

    for j in range(pieces):
        pltpu.make_async_copy(src.at[lax.div(me, PAIRS), :, lanes(j, lax.rem(me, PAIRS))],
                              recv.at[me, :, pl.ds(128 * j, 128)], recv_sem).start()
    if extra is not None:
        pltpu.make_async_copy(extra[0].at[lax.div(me, PAIRS)], extra[1].at[me], extra[3]).start()
    lax.fori_loop(1, count, send, 0)


def send_home(me, count, pieces, src, home, send_sem, recv_sem):
    mine = lax.div(me, PAIRS)
    pair = lax.rem(me, PAIRS)

    def send(k, carry):
        to = partner_of(me, k)
        for j in range(pieces):
            remote(src.at[to, :, pl.ds(128 * j, 128)], home.at[mine, :, lanes(j, pair)],
                   send_sem, recv_sem, to).start()
        return carry

    for j in range(pieces):
        pltpu.make_async_copy(src.at[me, :, pl.ds(128 * j, 128)], home.at[mine, :, lanes(j, pair)], recv_sem).start()
    lax.fori_loop(1, count, send, 0)


def await_bytes(ref, sem):
    pltpu.make_async_copy(ref, ref, sem).wait()


def build_sorter(table, sorter):
    n = sorter.shape[0]
    for c in range(n // 128):
        ids = lax.broadcasted_iota(jnp.int32, (n, 128), 0)
        sorter[:, pl.ds(128 * c, 128)] = jnp.where(ids == table[c : c + 1, :] - 1, 1.0, 0.0).astype(BF16)


def sort_blocks(cap, recv, wide32, gathered, sorter, out):
    count = recv.shape[0]
    span = cap * SEG

    def widen(d, carry):
        for j in range(wide32.shape[0]):
            part = recv[d, :, pl.ds(128 * j, 128)]
            wide32[j, pl.ds(pl.multiple_of(d * span, 8), span), :] = part.astype(F32)
        return carry

    lax.fori_loop(0, count, widen, 0)

    for r in range(SEG):
        for s in range(cap):
            for j in range(wide32.shape[0]):
                part = wide32[j, pl.ds(s * SEG + r, count, stride=span), :]
                gathered[pl.ds(s * count, count), pl.ds(128 * j, 128)] = part.astype(BF16)
        out[r] = dot(sorter[...], gathered[...], NN).astype(BF16)


def unsort_blocks(cap, src, wide32, sorter, out):
    count = out.shape[0]
    span = cap * SEG
    for r in range(SEG):
        back = dot(sorter[...], src[r], TN)
        for s in range(cap):
            for j in range(wide32.shape[0]):
                part = back[s * count : (s + 1) * count, 128 * j : 128 * (j + 1)]
                wide32[j, pl.ds(s * SEG + r, count, stride=span), :] = part

    def narrow(d, carry):
        for j in range(wide32.shape[0]):
            part = wide32[j, pl.ds(pl.multiple_of(d * span, 8), span), :]
            out[d, :, pl.ds(128 * j, 128)] = part.astype(BF16)
        return carry

    lax.fori_loop(0, count, narrow, 0)


TILE = 32


def same_line():
    n = TILE * SEG
    a = lax.div(lax.rem(lax.broadcasted_iota(jnp.int32, (n, n), 0), TILE), FRAG)
    b = lax.div(lax.rem(lax.broadcasted_iota(jnp.int32, (n, n), 1), TILE), FRAG)
    return a == b


def head_probs(q, k, first, mask, scale):
    q = jnp.where(first, q, jnp.zeros_like(q))
    expo = jnp.where(mask, jnp.exp(dot(q, k, NT) * scale), 0.0)
    return expo / jnp.sum(expo, axis=-1, keepdims=True)


def forward_kernel(cap, scale, proj, tagt, mixed, lines, table, recv, trecv, wide32, gathered, sorter,
                   attended, wide128, back, sems):
    me = lax.axis_index("space")
    count = recv.shape[0]
    greet_all(me, count)
    send_to_lines(me, count, 3, proj, recv, sems.at[0], sems.at[1], (tagt, trecv, sems.at[2], sems.at[3]))
    await_bytes(trecv, sems.at[3])
    table[...] = jnp.sum(trecv[...], axis=0)
    build_sorter(table[...], sorter)
    await_bytes(recv, sems.at[1])
    sort_blocks(cap, recv, wide32, gathered, sorter, lines)
    n = TILE * SEG
    mask = same_line()
    low = lax.broadcasted_iota(jnp.int32, (n, 128), 1) < 64

    def attend(t, carry):
        part = pl.ds(pl.multiple_of(t * TILE, TILE), TILE)
        x = lines[:, part, :].reshape(n, 384)
        q, k, v = x[:, :128], x[:, 128:256], x[:, 256:]
        outs = []
        for first in (low, ~low):
            w = head_probs(q, k, first, mask, scale).astype(BF16)
            outs.append(dot(w, v, NN))
        attended[:, part, :] = jnp.where(low, outs[0], outs[1]).astype(BF16).reshape(SEG, TILE, 128)
        return carry

    lax.fori_loop(0, cap * count // TILE, attend, 0)
    unsort_blocks(cap, attended, wide128, sorter, back)
    send_home(me, count, 1, back, mixed, sems.at[4], sems.at[5])
    await_bytes(recv.at[pl.ds(0, count - 1)], sems.at[0])
    await_bytes(trecv.at[pl.ds(0, count - 1)], sems.at[2])
    await_bytes(back.at[pl.ds(0, count - 1)], sems.at[4])
    await_bytes(mixed, sems.at[5])


VM = pl.BlockSpec(memory_space=pltpu.VMEM)


class Reducer:
    def __init__(self, me, g, out, pair, s0, r1, s1, r2, s2, r3, send, recv):
        self.me, self.g, self.out, self.pair, self.s0, self.r1, self.s1 = me, g, out, pair, s0, r1, s1
        self.r2, self.s2, self.r3, self.send, self.recv = r2, s2, r3, send, recv
        self.q = s2.shape[1]
        self.core = lax.axis_index("dp")
        self.place = (lax.div(me, 16), lax.rem(lax.div(me, 4), 4), lax.rem(me, 4))

    def peers(self, axis):
        step = (16, 4, 1)[axis]
        mine = self.place[axis]
        for k in (1, 2, 3):
            there = lax.rem(mine + k, 4)
            yield k - 1, there, self.me + (there - mine) * step

    def rows(self, half, p, u=None, v=None):
        q = self.q
        start, size = (half * 3 + p) * 16 * q, 16 * q
        if u is not None:
            start, size = start + u * 4 * q, 4 * q
        if v is not None:
            start, size = start + v * q, q
        return pl.ds(pl.multiple_of(start, 16), size)

    def copy(self, stage, p, src, dst, device):
        pltpu.make_async_remote_copy(
            src_ref=src, dst_ref=dst, send_sem=self.send.at[stage, p], recv_sem=self.recv.at[stage, p],
            device_id=device, device_id_type=MESH,
        ).start()

    def wait(self, stage, p):
        await_bytes(self.sized(stage, p), self.recv.at[stage, p])

    def sized(self, stage, p):
        return (self.pair, self.r1, self.r2, self.r3, self.r3, self.r2, self.r1, self.pair)[stage].at[p]

    def start(self):
        for p in range(3):
            self.copy(0, p, self.g.at[self.rows(1 - self.core, p)], self.pair.at[p], {"dp": 1 - self.core})

    def step(self, stage):
        for p in range(3):
            self.wait(stage, p)
            a, b, c = p, (p + 1) % 3, (p + 2) % 3
            ia, ib, ic = self.place[a], self.place[b], self.place[c]
            shard = pl.ds(pl.multiple_of(ic * 128, 128), 128)
            if stage == 0:

                def add(i, carry):
                    u, v = lax.div(i, 4), lax.rem(i, 4)
                    both = self.g[self.rows(self.core, p, u, v)].astype(F32)
                    both += self.pair[p, pl.ds(pl.multiple_of(i * self.q, 16), self.q)].astype(F32)
                    self.s0[p, u, v] = both.astype(BF16)
                    return carry

                lax.fori_loop(0, 16, add, 0)
                for k, there, device in self.peers(a):
                    self.copy(1, p, self.s0.at[p, there], self.r1.at[p, k], {"space": device})
            elif stage == 1:

                def add4(u, carry):
                    total = self.s0[p, ia, u].astype(F32)
                    for k in range(3):
                        total += self.r1[p, k, u].astype(F32)
                    self.s1[p, u] = total.astype(BF16)
                    return carry

                lax.fori_loop(0, 4, add4, 0)
                for k, there, device in self.peers(b):
                    self.copy(2, p, self.s1.at[p, there], self.r2.at[p, k], {"space": device})
            elif stage == 2:
                total = self.s1[p, ib].astype(F32)
                for k in range(3):
                    total += self.r2[p, k].astype(F32)
                self.s2[p] = total.astype(BF16)
                for k, there, device in self.peers(c):
                    part = pl.ds(pl.multiple_of(there * 128, 128), 128)
                    self.copy(3, p, self.s2.at[p, :, part], self.r3.at[p, k], {"space": device})
            elif stage == 3:
                total = self.s2[p, :, shard].astype(F32)
                for k in range(3):
                    total += self.r3[p, k].astype(F32)
                self.out[self.rows(self.core, p, ia, ib), shard] = total.astype(BF16)
                for k, there, device in self.peers(c):
                    piece = self.out.at[self.rows(self.core, p, ia, ib), shard]
                    self.copy(4, p, piece, piece, {"space": device})
            elif stage == 4:
                for k, there, device in self.peers(b):
                    piece = self.out.at[self.rows(self.core, p, ia, ib)]
                    self.copy(5, p, piece, piece, {"space": device})
            elif stage == 5:
                for k, there, device in self.peers(a):
                    piece = self.out.at[self.rows(self.core, p, ia)]
                    self.copy(6, p, piece, piece, {"space": device})
            elif stage == 6:
                piece = self.out.at[self.rows(self.core, p)]
                self.copy(7, p, piece, piece, {"dp": 1 - self.core})

    def finish(self):
        for stage in range(8):
            for p in range(3):
                await_bytes(self.sized(stage, p), self.send.at[stage, p])


def reducer_scratch(q):
    return [
        pltpu.VMEM((3, 16 * q, 512), BF16),
        pltpu.VMEM((3, 4, 4, q, 512), BF16),
        pltpu.VMEM((3, 3, 4, q, 512), BF16),
        pltpu.VMEM((3, 4, q, 512), BF16),
        pltpu.VMEM((3, 3, q, 512), BF16),
        pltpu.VMEM((3, q, 512), BF16),
        pltpu.VMEM((3, 3, q, 128), BF16),
        pltpu.SemaphoreType.DMA((8, 3)),
        pltpu.SemaphoreType.DMA((8, 3)),
    ]


def sum_gains(stage, reducer, got, sems):
    slots, held, send, recv = got, sems[0], sems[1], sems[2]
    count = 2 if stage == 0 else 4
    mine = reducer.core if stage == 0 else reducer.place[stage - 1]
    slots[stage, mine] = held[stage]
    if stage == 0:
        pltpu.make_async_remote_copy(
            src_ref=held.at[0], dst_ref=slots.at[0, mine], send_sem=send.at[0], recv_sem=recv.at[0],
            device_id={"dp": 1 - mine}, device_id_type=MESH,
        ).start()
    else:
        for k, there, device in reducer.peers(stage - 1):
            remote(held.at[stage], slots.at[stage, mine], send.at[stage], recv.at[stage], device).start()


def gather_gains(stage, got, sems):
    slots, held, send, recv = got, sems[0], sems[1], sems[2]
    count = 2 if stage == 0 else 4
    await_bytes(slots.at[stage, pl.ds(0, count - 1)], recv.at[stage])
    total = slots[stage, 0]
    for k in range(1, count):
        total += slots[stage, k]
    return total


def tail_kernel(g, gains, out, gains_out, *scratch):
    me = lax.axis_index("space")
    red = Reducer(me, g, out, *scratch[:9])
    slots, held, gsend, grecv = scratch[9:]
    sems = (held, gsend, grecv)
    barrier = pltpu.get_barrier_semaphore()
    pl.semaphore_signal(barrier, inc=1, device_id={"dp": 1 - red.core}, device_id_type=MESH)
    for axis in range(3):
        for k, there, device in red.peers(axis):
            pl.semaphore_signal(barrier, inc=1, device_id={"space": device}, device_id_type=MESH)
    pl.semaphore_wait(barrier, 10)
    red.start()
    held[0] = gains[...]
    sum_gains(0, red, slots, sems)
    for stage in range(7):
        red.step(stage)
        if stage < 4:
            total = gather_gains(stage, slots, sems)
            if stage < 3:
                held[stage + 1] = total
                sum_gains(stage + 1, red, slots, sems)
            else:
                gains_out[...] = total
    for p in range(3):
        red.wait(7, p)
    red.finish()
    for stage in range(4):
        await_bytes(slots.at[stage, pl.ds(0, 1 if stage == 0 else 3)], gsend.at[stage])


def reduce_tail(cap, g, gains):
    q = g.shape[0] // 96
    out, gains = pl.pallas_call(
        tail_kernel,
        out_shape=(
            jax.ShapeDtypeStruct(g.shape, BF16),
            jax.ShapeDtypeStruct((8, 128), F32),
        ),
        in_specs=[VM] * 2,
        out_specs=(VM,) * 2,
        scratch_shapes=reducer_scratch(q)
        + [
            pltpu.VMEM((4, 4, 8, 128), F32),
            pltpu.VMEM((4, 8, 128), F32),
            pltpu.SemaphoreType.DMA((4,)),
            pltpu.SemaphoreType.DMA((4,)),
        ],
        compiler_params=pltpu.CompilerParams(collective_id=20 + cap, has_side_effects=True, vmem_limit_bytes=60 << 20),
        name="reduce_tail",
    )(g, gains)
    return out, gains


def backward_tiles(scale, lines, dlines_in, dlines):
    n = TILE * SEG
    mask = same_line()
    low = lax.broadcasted_iota(jnp.int32, (n, 128), 1) < 64

    def attend(t, carry):
        part = pl.ds(pl.multiple_of(t * TILE, TILE), TILE)
        x = lines[:, part, :].reshape(n, 384)
        up = dlines_in[:, part, :].reshape(n, 128)
        q, k, v = x[:, :128], x[:, 128:256], x[:, 256:]
        outs = []
        for first in (low, ~low):
            p = head_probs(q, k, first, mask, scale)
            g = dot(jnp.where(first, up, jnp.zeros_like(up)), v, NT)
            ds = (p * (g - jnp.sum(g * p, axis=-1, keepdims=True)) * scale).astype(BF16)
            outs.append((dot(ds, k, NN), dot(ds, q, TN), dot(p.astype(BF16), up, TN)))
        for j in range(3):
            dlines[:, part, pl.ds(128 * j, 128)] = (
                jnp.where(low, outs[0][j], outs[1][j]).astype(BF16).reshape(SEG, TILE, 128)
            )
        return carry

    return attend


def backward_kernel(cap, scale, dmixed, lines, table, g, dproj, out, recv, wide128, gathered, sorter, dlines_in,
                    dlines, wide32, back, sems, *scratch):
    me = lax.axis_index("space")
    count = recv.shape[0]
    red = Reducer(me, g, out, *scratch)
    greet_all(me, count, True)
    send_to_lines(me, count, 1, dmixed, recv, sems.at[0], sems.at[1])
    red.start()
    build_sorter(table[...], sorter)
    await_bytes(recv, sems.at[1])
    red.step(0)
    sort_blocks(cap, recv, wide128, gathered, sorter, dlines_in)
    attend = backward_tiles(scale, lines, dlines_in, dlines)
    tiles = cap * count // TILE
    lax.fori_loop(0, tiles // 2, attend, 0)
    red.step(1)
    lax.fori_loop(tiles // 2, tiles, attend, 0)
    red.step(2)
    unsort_blocks(cap, dlines, wide32, sorter, back)
    send_home(me, count, 3, back, dproj, sems.at[2], sems.at[3])
    for stage in range(3, 7):
        red.step(stage)
    await_bytes(recv.at[pl.ds(0, count - 1)], sems.at[0])
    await_bytes(back.at[pl.ds(0, count - 1)], sems.at[2])
    await_bytes(dproj, sems.at[3])
    for p in range(3):
        red.wait(7, p)
    red.finish()


def forward_lines(proj, tagt, cap, count, scale):
    n = cap * count
    span = cap * SEG
    return pl.pallas_call(
        functools.partial(forward_kernel, cap, scale),
        out_shape=(
            jax.ShapeDtypeStruct((BINS, span, 512), BF16),
            jax.ShapeDtypeStruct((SEG, n, 384), BF16),
            jax.ShapeDtypeStruct((8, 128), jnp.int32),
        ),
        in_specs=[VM] * 2,
        out_specs=(VM,) * 3,
        scratch_shapes=[
            pltpu.VMEM((count, span, 384), BF16),
            pltpu.VMEM((count, 8, 128), jnp.int32),
            pltpu.VMEM((3, count * span, 128), F32),
            pltpu.VMEM((n, 384), BF16),
            pltpu.VMEM((n, n), BF16),
            pltpu.VMEM((SEG, n, 128), BF16),
            pltpu.VMEM((1, count * span, 128), F32),
            pltpu.VMEM((count, span, 128), BF16),
            pltpu.SemaphoreType.DMA((6,)),
        ],
        compiler_params=pltpu.CompilerParams(collective_id=cap, has_side_effects=True, vmem_limit_bytes=60 << 20),
        name="forward_lines",
    )(proj, tagt)


def backward_lines(dmixed, lines, table, g, cap, count, scale):
    q = g.shape[0] // 96
    n = cap * count
    span = cap * SEG
    dproj, out = pl.pallas_call(
        functools.partial(backward_kernel, cap, scale),
        out_shape=(
            jax.ShapeDtypeStruct((BINS, span, 1536), BF16),
            jax.ShapeDtypeStruct(g.shape, BF16),
        ),
        in_specs=[VM] * 4,
        out_specs=(VM,) * 2,
        scratch_shapes=[
            pltpu.VMEM((count, span, 128), BF16),
            pltpu.VMEM((1, count * span, 128), F32),
            pltpu.VMEM((n, 128), BF16),
            pltpu.VMEM((n, n), BF16),
            pltpu.VMEM((SEG, n, 128), BF16),
            pltpu.VMEM((SEG, n, 384), BF16),
            pltpu.VMEM((3, count * span, 128), F32),
            pltpu.VMEM((count, span, 384), BF16),
            pltpu.SemaphoreType.DMA((4,)),
        ]
        + reducer_scratch(q),
        compiler_params=pltpu.CompilerParams(collective_id=10 + cap, has_side_effects=True, vmem_limit_bytes=60 << 20),
        name="backward_lines",
    )(dmixed, lines, table, g)
    return dproj, out


def step_back_kernel(scale, dmixed, lines, table, activated, upstream, normed_mlp, dpre, mixed, dhidden_b, normed, w_qkv,
                     unit, inv, dhidden, gain, mlp_gain_sum, pack, grad_states, early, late, gains_out,
                     recv, wide128, gathered, sorter, dlines_in, dlines, wide32, back, dproj, g, g_late, shifted, sems, *scratch):
    me = lax.axis_index("space")
    cap = 4
    count = recv.shape[0]
    red = Reducer(me, g, early, *scratch[:9])
    red_late = Reducer(me, g_late, late, *scratch[9:18])
    slots, held, gsend, grecv = scratch[18:]
    gain_refs = (held, gsend, grecv)
    greet_all(me, count, True)
    send_to_lines(me, count, 1, dmixed, recv, sems.at[0], sems.at[1])

    def blocks(j, width=512):
        return pl.ds(pl.multiple_of(j * width, width), width)

    def down_sum(j, carry):
        g[blocks(j), :] = dot(activated[:, blocks(j)], upstream[...], TN).astype(BF16)
        return carry

    def up_sum(j, carry):
        g[blocks(j + 4), :] = dot(normed_mlp[...], dpre[:, blocks(j)], TN).astype(BF16)
        return carry

    lax.fori_loop(0, 4, down_sum, 0)
    lax.fori_loop(0, 4, up_sum, 0)
    g[pl.ds(4096, 512), :] = dot(mixed[...], dhidden_b[...], TN).astype(BF16)
    red.start()
    build_sorter(table[...], sorter)
    await_bytes(recv, sems.at[1])
    sort_blocks(cap, recv, wide128, gathered, sorter, dlines_in)
    attend = backward_tiles(scale, lines, dlines_in, dlines)
    tiles = cap * count // TILE
    lax.fori_loop(0, tiles // 2, attend, 0)
    red.step(0)
    lax.fori_loop(tiles // 2, tiles, attend, 0)
    unsort_blocks(cap, dlines, wide32, sorter, back)
    send_home(me, count, 3, back, dproj, sems.at[2], sems.at[3])
    red.step(1)
    red.step(2)
    await_bytes(dproj, sems.at[3])
    rows = BINS * cap * SEG

    def late_sum(j, carry):
        rhs = dproj[:, :, blocks(j)].reshape(rows, 512)
        g_late[blocks(j), :] = dot(normed[...], rhs, TN).astype(BF16)
        return carry

    lax.fori_loop(0, 3, late_sum, 0)
    red_late.start()

    def norm_chunk(i, total):
        part = pl.ds(pl.multiple_of(i * 128, 128), 128)
        dn = dot(dproj[pl.ds(i * 4, 4)].reshape(128, 1536), w_qkv[...], NT).astype(BF16).astype(F32)
        u = unit[part, :]
        shifted[part, :] = (dhidden[part, :] + norm_back(u, inv[part, :], gain[...], dn)).astype(BF16)
        return total + jnp.sum(u * dn, axis=0, keepdims=True)

    total = lax.fori_loop(0, rows // 128, norm_chunk, jnp.zeros((1, 512), F32))
    for j in range(4):
        held[0, pl.ds(j, 1), :] = total[:, 128 * j : 128 * (j + 1)]
    held[0, pl.ds(4, 4), :] = mlp_gain_sum[...]
    sum_gains(0, red, slots, gain_refs)
    red_late.step(0)
    grad_states[...] = dot(pack[...], shifted[...], TN).astype(BF16)
    for stage in range(7):
        if stage > 0:
            red_late.step(stage)
        if stage == 0:
            red.step(3)
        if stage == 1:
            red.step(4)
        if stage == 2:
            red.step(5)
        if stage == 5:
            red.step(6)
        if stage < 4:
            some = gather_gains(stage, slots, gain_refs)
            if stage < 3:
                held[stage + 1] = some
                sum_gains(stage + 1, red, slots, gain_refs)
            else:
                gains_out[...] = some
    for p in range(3):
        red.wait(7, p)
        red_late.wait(7, p)
    red.finish()
    red_late.finish()
    for stage in range(4):
        await_bytes(slots.at[stage, pl.ds(0, 1 if stage == 0 else 3)], gsend.at[stage])
    await_bytes(recv.at[pl.ds(0, count - 1)], sems.at[0])
    await_bytes(back.at[pl.ds(0, count - 1)], sems.at[2])


def step_back(scale, *args):
    cap, count = 4, 64
    n = cap * count
    span = cap * SEG
    rows = BINS * span
    out = pl.pallas_call(
        functools.partial(step_back_kernel, scale),
        out_shape=(
            jax.ShapeDtypeStruct((512, 512), BF16),
            jax.ShapeDtypeStruct((4608, 512), BF16),
            jax.ShapeDtypeStruct((1536, 512), BF16),
            jax.ShapeDtypeStruct((8, 128), F32),
        ),
        in_specs=[VM] * len(args),
        out_specs=(VM,) * 4,
        scratch_shapes=[
            pltpu.VMEM((count, span, 128), BF16),
            pltpu.VMEM((1, count * span, 128), F32),
            pltpu.VMEM((n, 128), BF16),
            pltpu.VMEM((n, n), BF16),
            pltpu.VMEM((SEG, n, 128), BF16),
            pltpu.VMEM((SEG, n, 384), BF16),
            pltpu.VMEM((3, count * span, 128), F32),
            pltpu.VMEM((count, span, 384), BF16),
            pltpu.VMEM((BINS, span, 1536), BF16),
            pltpu.VMEM((4608, 512), BF16),
            pltpu.VMEM((1536, 512), BF16),
            pltpu.VMEM((rows, 512), BF16),
            pltpu.SemaphoreType.DMA((4,)),
        ]
        + reducer_scratch(48)
        + reducer_scratch(16)
        + [
            pltpu.VMEM((4, 4, 8, 128), F32),
            pltpu.VMEM((4, 8, 128), F32),
            pltpu.SemaphoreType.DMA((4,)),
            pltpu.SemaphoreType.DMA((4,)),
        ],
        compiler_params=pltpu.CompilerParams(collective_id=30, has_side_effects=True, vmem_limit_bytes=62 << 20),
        name="step_back",
    )(*args)
    return out


def fits_four(owner):
    same = owner[:, None] == owner[None, :]
    load = jnp.sum(same, axis=1, dtype=jnp.int32)
    threes = jnp.sum(load == 3, dtype=jnp.int32)
    twos = jnp.sum(load == 2, dtype=jnp.int32)
    return 4 * threes + 3 * twos <= 3 * owner.shape[0]


def per_device(*args):
    return lax.cond(fits_four(args[2]), functools.partial(block, 4), functools.partial(block, 6), *args)


def block(
    cap, states, cotangent, send_owner, line_place, gain_attn, w_qkv, w_out, gain_mlp, w_up, w_down
):
    width = states.shape[2]
    rows = states.shape[1]
    nspace = lax.axis_size("space")
    total_rows = rows * nspace * lax.axis_size("dp")
    nblocks = send_owner.shape[0]
    slots = BINS * cap
    wide = 2 * (width // HEADS)
    head_dim = width // HEADS
    scale = head_dim ** (-0.5)
    slot, tag = routing(send_owner, line_place, cap)
    me = lax.axis_index("space")
    hit = slot[None, :] == jnp.arange(slots, dtype=jnp.int32)[:, None]
    tags = jnp.sum(jnp.where(hit, tag[None, :] + 1, 0), axis=1).reshape(BINS, cap // 2, 2)
    tags = jnp.pad(tags, ((0, 0), (0, 8 - cap // 2), (0, 0)))
    at_me = jnp.arange(nspace, dtype=jnp.int32) == me
    tagt = jnp.where(at_me[None, None, None, :], tags[..., None], 0).reshape(BINS, 8, 2 * nspace)
    target = (slot[:, None] * SEG + jnp.arange(SEG, dtype=jnp.int32)[None, :]).reshape(rows)
    pack = (jnp.arange(slots * SEG, dtype=jnp.int32)[:, None] == target[None, :]).astype(BF16)

    flat_b = dot(pack, states[0], NN).astype(BF16)
    upstream = dot(pack, cotangent[0], NN).astype(BF16)
    flat = flat_b.astype(F32)
    unit_a, inv_a = norm_stats(flat)
    normed = (unit_a * gain_attn).astype(BF16)
    projected = dot(normed, w_qkv, NN).astype(BF16)
    span = cap * SEG
    mixed, lines, table = forward_lines(projected.reshape(BINS, span, 3 * width), tagt, cap, nspace, scale)
    mixed = mixed.reshape(BINS * span, width)

    hidden = (flat + dot(mixed, w_out, NN)).astype(BF16)
    hidden32 = hidden.astype(F32)
    unit_m, inv_m = norm_stats(hidden32)
    normed_mlp = (unit_m * gain_mlp).astype(BF16)
    act32, slope = gelu_parts(dot(normed_mlp, w_up, NN))
    activated = act32.astype(BF16)
    output = (hidden32 + dot(activated, w_down, NN)).astype(BF16)
    dpre = (slope * dot(upstream, w_down, NT)).astype(BF16)
    dnormed_mlp = dot(dpre, w_up, NT)
    grad_gain_mlp = jnp.sum(unit_m * dnormed_mlp, axis=0)
    dhidden = upstream.astype(F32) + norm_back(unit_m, inv_m, gain_mlp, dnormed_mlp)
    dhidden_b = dhidden.astype(BF16)
    dmixed = dot(dhidden_b, w_out, NT).astype(BF16)
    output = dot(pack, output, TN).astype(BF16)
    if cap == 4:
        grad_states, early, late, gains = step_back(
            scale, dmixed.reshape(BINS, span, width), lines, table, activated, upstream, normed_mlp, dpre, mixed, dhidden_b,
            normed, w_qkv, unit_a, inv_a, dhidden, gain_attn[None], grad_gain_mlp.reshape(4, 128), pack,
        )
    else:
        early = [dot(activated, upstream, TN)]
        early += [dot(normed_mlp, dpre[:, j * width : (j + 1) * width], TN) for j in range(4)]
        early += [dot(mixed, dhidden_b, TN)]
        early = jnp.concatenate([v.astype(BF16) for v in early], axis=0)

        dprojected, early = backward_lines(dmixed.reshape(BINS, span, width), lines, table, early, cap, nspace, scale)
        dprojected = dprojected.reshape(BINS * span, 3 * width)
        late = [dot(normed, dprojected[:, j * width : (j + 1) * width], TN) for j in range(3)]
        late = jnp.concatenate([v.astype(BF16) for v in late], axis=0)
        dnormed = dot(dprojected, w_qkv, NT).astype(BF16).astype(F32)
        grad_gain_attn = jnp.sum(unit_a * dnormed, axis=0)
        grad_states = (dhidden + norm_back(unit_a, inv_a, gain_attn, dnormed)).astype(BF16)
        grad_states = dot(pack, grad_states, TN).astype(BF16)
        late, gains = reduce_tail(cap, late, jnp.concatenate([grad_gain_attn, grad_gain_mlp]).reshape(8, 128))
    factor = 1.0 / math.sqrt(total_rows)
    gains = gains.reshape(2, width) * factor
    hidden_units = w_up.shape[1]

    def columns(blocks):
        blocks = blocks.reshape(-1, width, width)
        return jnp.concatenate([blocks[j].astype(F32) * factor for j in range(blocks.shape[0])], axis=1)

    return (
        output[None],
        grad_states[None],
        gains[0],
        columns(late),
        early[2 * hidden_units :].astype(F32) * factor,
        gains[1],
        columns(early[hidden_units : 2 * hidden_units]),
        early[:hidden_units].astype(F32) * factor,
    )


def solution(mesh):
    placed = (
        P("dp", "space", None),
        P("dp", "space", None),
        P("space"),
        P("space"),
        P(),
        P(),
        P(),
        P(),
        P(),
        P(),
    )
    return jax.shard_map(
        per_device,
        mesh=mesh,
        in_specs=placed,
        out_specs=(P("dp", "space", None), P("dp", "space", None), P(), P(), P(), P(), P(), P()),
        check_vma=False,
    )
```

```python
import functools
import math

import jax
import jax.numpy as jnp
from jax import lax
from jax.experimental import pallas as pl
from jax.experimental.pallas import tpu as pltpu
from jax.sharding import PartitionSpec as P

HEADS = 8
SEG = 8
FRAG = 4
BINS = 16
PAIRS = 4

EPSILON = 1e-05
F32 = jnp.float32
BF16 = jnp.bfloat16
MESH = pl.DeviceIdType.MESH


def dot(a, b, dims):
    return lax.dot_general(a, b, (dims, ((), ())), preferred_element_type=F32)


NN = ((1,), (0,))
NT = ((1,), (1,))
TN = ((0,), (0,))


def norm_stats(v):
    center = v - jnp.mean(v, axis=-1, keepdims=True)
    inv = lax.rsqrt(jnp.mean(center * center, axis=-1, keepdims=True) + EPSILON)
    return center * inv, inv


def norm_back(unit, inv, gain, upstream):
    g = upstream * gain
    m1 = jnp.mean(g, axis=-1, keepdims=True)
    m2 = jnp.mean(g * unit, axis=-1, keepdims=True)
    return inv * (g - m1 - unit * m2)


GELU_C = math.sqrt(2.0 / math.pi)


def gelu_parts(v):
    t = jnp.tanh(GELU_C * (v + 0.044715 * (v * v * v)))
    value = 0.5 * v * (1.0 + t)
    slope = 0.5 * (1.0 + t) + 0.5 * v * (1.0 - t * t) * (GELU_C * (1.0 + 3 * 0.044715 * (v * v)))
    return value, slope


def routing(owner, place, cap):
    n = owner.shape[0]
    ids = jnp.arange(n, dtype=jnp.int32)
    same = owner[:, None] == owner[None, :]
    rank = jnp.sum(same & (ids[None, :] < ids[:, None]), axis=1, dtype=jnp.int32)
    load = jnp.sum(same, axis=1, dtype=jnp.int32)
    first = rank == 0
    ahead = first[None, :] & (load[None, :] == load[:, None]) & (owner[None, :] < owner[:, None])
    index = jnp.sum(ahead, axis=1, dtype=jnp.int32)
    n3 = jnp.sum(first & (load == 3), dtype=jnp.int32)
    n2 = jnp.sum(first & (load == 2), dtype=jnp.int32)
    if cap == 4:
        spare = index < n3
        base1 = jnp.where(spare, 4 * index + 3, 3 * n3 + 2 * n2 + index)
        base = jnp.where(load == 3, 4 * index, jnp.where(load == 2, 4 * n3 + 2 * index, base1))
        return base + rank, (base % cap) * n + place
    odd = (n3 % 2) == 1
    base3 = 3 * index
    base2 = 3 * n3 + 2 * index + jnp.where(odd & (index >= 1), 1, 0)
    base1 = 3 * n3 + 2 * n2 + jnp.where(odd & (n2 >= 2), 1, 0) + index
    base = jnp.where(load == 3, base3, jnp.where(load == 2, base2, base1))
    return base + rank, (base % cap) * n + place


def partner_of(me, k):
    ys = lax.rem(lax.div(me, 16) + lax.div(k, 16), 4)
    zs = lax.rem(lax.div(lax.rem(me, 16), 4) + lax.div(lax.rem(k, 16), 4), 4)
    xs = lax.rem(lax.rem(me, 4) + lax.rem(k, 4), 4)
    return ys * 16 + zs * 4 + xs


def greet_all(me, count, pair=False, work=None):
    barrier = pltpu.get_barrier_semaphore()

    def greet(k, carry):
        pl.semaphore_signal(barrier, inc=1, device_id={"space": partner_of(me, k)}, device_id_type=MESH)
        return carry

    lax.fori_loop(1, count, greet, 0)
    if pair:
        pl.semaphore_signal(barrier, inc=1, device_id={"dp": 1 - lax.axis_index("dp")}, device_id_type=MESH)
    if work is not None:
        work()
    pl.semaphore_wait(barrier, count if pair else count - 1)


def remote(src, dst, send_sem, recv_sem, device):
    return pltpu.make_async_remote_copy(
        src_ref=src, dst_ref=dst, send_sem=send_sem, recv_sem=recv_sem,
        device_id={"space": device}, device_id_type=MESH,
    )


def lanes(j, pair):
    return pl.ds(pl.multiple_of(j * 512 + pair * 128, 128), 128)


def send_to_lines(me, count, pieces, src, recv, send_sem, recv_sem, extra=None):
    def send(k, carry):
        to = partner_of(me, k)
        for j in range(pieces):
            remote(src.at[lax.div(to, PAIRS), :, lanes(j, lax.rem(to, PAIRS))],
                   recv.at[me, :, pl.ds(128 * j, 128)], send_sem, recv_sem, to).start()
        if extra is not None:
            remote(extra[0].at[lax.div(to, PAIRS)], extra[1].at[me], extra[2], extra[3], to).start()
        return carry

    for j in range(pieces):
        pltpu.make_async_copy(src.at[lax.div(me, PAIRS), :, lanes(j, lax.rem(me, PAIRS))],
                              recv.at[me, :, pl.ds(128 * j, 128)], recv_sem).start()
    if extra is not None:
        pltpu.make_async_copy(extra[0].at[lax.div(me, PAIRS)], extra[1].at[me], extra[3]).start()
    lax.fori_loop(1, count, send, 0)


def send_home(me, count, pieces, src, home, send_sem, recv_sem):
    mine = lax.div(me, PAIRS)
    pair = lax.rem(me, PAIRS)

    def send(k, carry):
        to = partner_of(me, k)
        for j in range(pieces):
            remote(src.at[to, :, pl.ds(128 * j, 128)], home.at[mine, :, lanes(j, pair)],
                   send_sem, recv_sem, to).start()
        return carry

    for j in range(pieces):
        pltpu.make_async_copy(src.at[me, :, pl.ds(128 * j, 128)], home.at[mine, :, lanes(j, pair)], recv_sem).start()
    lax.fori_loop(1, count, send, 0)


def await_bytes(ref, sem):
    pltpu.make_async_copy(ref, ref, sem).wait()


def build_sorter(table, sorter):
    n = sorter.shape[0]
    for c in range(n // 128):
        ids = lax.broadcasted_iota(jnp.int32, (n, 128), 0)
        sorter[:, pl.ds(128 * c, 128)] = jnp.where(ids == table[c : c + 1, :] - 1, 1.0, 0.0).astype(BF16)


def sort_blocks(cap, recv, wide32, gathered, sorter, out):
    count = recv.shape[0]
    span = cap * SEG

    def widen(d, carry):
        for j in range(wide32.shape[0]):
            part = recv[d, :, pl.ds(128 * j, 128)]
            wide32[j, pl.ds(pl.multiple_of(d * span, 8), span), :] = part.astype(F32)
        return carry

    lax.fori_loop(0, count, widen, 0)

    for r in range(SEG):
        for s in range(cap):
            for j in range(wide32.shape[0]):
                part = wide32[j, pl.ds(s * SEG + r, count, stride=span), :]
                gathered[pl.ds(s * count, count), pl.ds(128 * j, 128)] = part.astype(BF16)
        out[r] = dot(sorter[...], gathered[...], NN).astype(BF16)


def unsort_blocks(cap, src, wide32, sorter, out):
    count = out.shape[0]
    span = cap * SEG
    for r in range(SEG):
        back = dot(sorter[...], src[r], TN)
        for s in range(cap):
            for j in range(wide32.shape[0]):
                part = back[s * count : (s + 1) * count, 128 * j : 128 * (j + 1)]
                wide32[j, pl.ds(s * SEG + r, count, stride=span), :] = part

    def narrow(d, carry):
        for j in range(wide32.shape[0]):
            part = wide32[j, pl.ds(pl.multiple_of(d * span, 8), span), :]
            out[d, :, pl.ds(128 * j, 128)] = part.astype(BF16)
        return carry

    lax.fori_loop(0, count, narrow, 0)


TILE = 32


def same_line():
    n = TILE * SEG
    a = lax.div(lax.rem(lax.broadcasted_iota(jnp.int32, (n, n), 0), TILE), FRAG)
    b = lax.div(lax.rem(lax.broadcasted_iota(jnp.int32, (n, n), 1), TILE), FRAG)
    return a == b


def head_probs(q, k, first, mask, scale):
    q = jnp.where(first, q, jnp.zeros_like(q))
    expo = jnp.where(mask, jnp.exp(dot(q, k, NT) * scale), 0.0)
    return expo / jnp.sum(expo, axis=-1, keepdims=True)


def forward_kernel(cap, scale, proj, tagt, mixed, lines, table, recv, trecv, wide32, gathered, sorter,
                   attended, wide128, back, sems, work=None):
    me = lax.axis_index("space")
    count = recv.shape[0]
    greet_all(me, count, work=work)
    send_to_lines(me, count, 3, proj, recv, sems.at[0], sems.at[1], (tagt, trecv, sems.at[2], sems.at[3]))
    await_bytes(trecv, sems.at[3])
    table[...] = jnp.sum(trecv[...], axis=0)
    build_sorter(table[...], sorter)
    await_bytes(recv, sems.at[1])
    sort_blocks(cap, recv, wide32, gathered, sorter, lines)
    n = TILE * SEG
    mask = same_line()
    low = lax.broadcasted_iota(jnp.int32, (n, 128), 1) < 64

    def attend(t, carry):
        part = pl.ds(pl.multiple_of(t * TILE, TILE), TILE)
        x = lines[:, part, :].reshape(n, 384)
        q, k, v = x[:, :128], x[:, 128:256], x[:, 256:]
        outs = []
        for first in (low, ~low):
            w = head_probs(q, k, first, mask, scale).astype(BF16)
            outs.append(dot(w, v, NN))
        attended[:, part, :] = jnp.where(low, outs[0], outs[1]).astype(BF16).reshape(SEG, TILE, 128)
        return carry

    lax.fori_loop(0, cap * count // TILE, attend, 0)
    unsort_blocks(cap, attended, wide128, sorter, back)
    send_home(me, count, 1, back, mixed, sems.at[4], sems.at[5])
    await_bytes(recv.at[pl.ds(0, count - 1)], sems.at[0])
    await_bytes(trecv.at[pl.ds(0, count - 1)], sems.at[2])
    await_bytes(back.at[pl.ds(0, count - 1)], sems.at[4])
    await_bytes(mixed, sems.at[5])


VM = pl.BlockSpec(memory_space=pltpu.VMEM)


class Reducer:
    def __init__(self, me, g, out, pair, s0, r1, s1, r2, s2, r3, send, recv):
        self.me, self.g, self.out, self.pair, self.s0, self.r1, self.s1 = me, g, out, pair, s0, r1, s1
        self.r2, self.s2, self.r3, self.send, self.recv = r2, s2, r3, send, recv
        self.q = s2.shape[1]
        self.core = lax.axis_index("dp")
        self.place = (lax.div(me, 16), lax.rem(lax.div(me, 4), 4), lax.rem(me, 4))

    def peers(self, axis):
        step = (16, 4, 1)[axis]
        mine = self.place[axis]
        for k in (1, 2, 3):
            there = lax.rem(mine + k, 4)
            yield k - 1, there, self.me + (there - mine) * step

    def rows(self, half, p, u=None, v=None):
        q = self.q
        start, size = (half * 3 + p) * 16 * q, 16 * q
        if u is not None:
            start, size = start + u * 4 * q, 4 * q
        if v is not None:
            start, size = start + v * q, q
        return pl.ds(pl.multiple_of(start, 16), size)

    def copy(self, stage, p, src, dst, device):
        pltpu.make_async_remote_copy(
            src_ref=src, dst_ref=dst, send_sem=self.send.at[stage, p], recv_sem=self.recv.at[stage, p],
            device_id=device, device_id_type=MESH,
        ).start()

    def wait(self, stage, p):
        await_bytes(self.sized(stage, p), self.recv.at[stage, p])

    def sized(self, stage, p):
        return (self.pair, self.r1, self.r2, self.r3, self.r3, self.r2, self.r1, self.pair)[stage].at[p]

    def start(self):
        for p in range(3):
            self.copy(0, p, self.g.at[self.rows(1 - self.core, p)], self.pair.at[p], {"dp": 1 - self.core})

    def step(self, stage):
        for p in range(3):
            self.wait(stage, p)
            a, b, c = p, (p + 1) % 3, (p + 2) % 3
            ia, ib, ic = self.place[a], self.place[b], self.place[c]
            shard = pl.ds(pl.multiple_of(ic * 128, 128), 128)
            if stage == 0:

                def add(i, carry):
                    u, v = lax.div(i, 4), lax.rem(i, 4)
                    both = self.g[self.rows(self.core, p, u, v)].astype(F32)
                    both += self.pair[p, pl.ds(pl.multiple_of(i * self.q, 16), self.q)].astype(F32)
                    self.s0[p, u, v] = both.astype(BF16)
                    return carry

                lax.fori_loop(0, 16, add, 0)
                for k, there, device in self.peers(a):
                    self.copy(1, p, self.s0.at[p, there], self.r1.at[p, k], {"space": device})
            elif stage == 1:

                def add4(u, carry):
                    total = self.s0[p, ia, u].astype(F32)
                    for k in range(3):
                        total += self.r1[p, k, u].astype(F32)
                    self.s1[p, u] = total.astype(BF16)
                    return carry

                lax.fori_loop(0, 4, add4, 0)
                for k, there, device in self.peers(b):
                    self.copy(2, p, self.s1.at[p, there], self.r2.at[p, k], {"space": device})
            elif stage == 2:
                total = self.s1[p, ib].astype(F32)
                for k in range(3):
                    total += self.r2[p, k].astype(F32)
                self.s2[p] = total.astype(BF16)
                for k, there, device in self.peers(c):
                    part = pl.ds(pl.multiple_of(there * 128, 128), 128)
                    self.copy(3, p, self.s2.at[p, :, part], self.r3.at[p, k], {"space": device})
            elif stage == 3:
                total = self.s2[p, :, shard].astype(F32)
                for k in range(3):
                    total += self.r3[p, k].astype(F32)
                self.out[self.rows(self.core, p, ia, ib), shard] = total.astype(BF16)
                for k, there, device in self.peers(c):
                    piece = self.out.at[self.rows(self.core, p, ia, ib), shard]
                    self.copy(4, p, piece, piece, {"space": device})
            elif stage == 4:
                for k, there, device in self.peers(b):
                    piece = self.out.at[self.rows(self.core, p, ia, ib)]
                    self.copy(5, p, piece, piece, {"space": device})
            elif stage == 5:
                for k, there, device in self.peers(a):
                    piece = self.out.at[self.rows(self.core, p, ia)]
                    self.copy(6, p, piece, piece, {"space": device})
            elif stage == 6:
                piece = self.out.at[self.rows(self.core, p)]
                self.copy(7, p, piece, piece, {"dp": 1 - self.core})

    def finish(self):
        for stage in range(8):
            for p in range(3):
                await_bytes(self.sized(stage, p), self.send.at[stage, p])


def reducer_scratch(q):
    return [
        pltpu.VMEM((3, 16 * q, 512), BF16),
        pltpu.VMEM((3, 4, 4, q, 512), BF16),
        pltpu.VMEM((3, 3, 4, q, 512), BF16),
        pltpu.VMEM((3, 4, q, 512), BF16),
        pltpu.VMEM((3, 3, q, 512), BF16),
        pltpu.VMEM((3, q, 512), BF16),
        pltpu.VMEM((3, 3, q, 128), BF16),
        pltpu.SemaphoreType.DMA((8, 3)),
        pltpu.SemaphoreType.DMA((8, 3)),
    ]


def sum_gains(stage, reducer, got, sems):
    slots, held, send, recv = got, sems[0], sems[1], sems[2]
    count = 2 if stage == 0 else 4
    mine = reducer.core if stage == 0 else reducer.place[stage - 1]
    slots[stage, mine] = held[stage]
    if stage == 0:
        pltpu.make_async_remote_copy(
            src_ref=held.at[0], dst_ref=slots.at[0, mine], send_sem=send.at[0], recv_sem=recv.at[0],
            device_id={"dp": 1 - mine}, device_id_type=MESH,
        ).start()
    else:
        for k, there, device in reducer.peers(stage - 1):
            remote(held.at[stage], slots.at[stage, mine], send.at[stage], recv.at[stage], device).start()


def gather_gains(stage, got, sems):
    slots, held, send, recv = got, sems[0], sems[1], sems[2]
    count = 2 if stage == 0 else 4
    await_bytes(slots.at[stage, pl.ds(0, count - 1)], recv.at[stage])
    total = slots[stage, 0]
    for k in range(1, count):
        total += slots[stage, k]
    return total


def tail_kernel(g, gains, out, gains_out, *scratch):
    me = lax.axis_index("space")
    red = Reducer(me, g, out, *scratch[:9])
    slots, held, gsend, grecv = scratch[9:]
    sems = (held, gsend, grecv)
    barrier = pltpu.get_barrier_semaphore()
    pl.semaphore_signal(barrier, inc=1, device_id={"dp": 1 - red.core}, device_id_type=MESH)
    for axis in range(3):
        for k, there, device in red.peers(axis):
            pl.semaphore_signal(barrier, inc=1, device_id={"space": device}, device_id_type=MESH)
    pl.semaphore_wait(barrier, 10)
    red.start()
    held[0] = gains[...]
    sum_gains(0, red, slots, sems)
    for stage in range(7):
        red.step(stage)
        if stage < 4:
            total = gather_gains(stage, slots, sems)
            if stage < 3:
                held[stage + 1] = total
                sum_gains(stage + 1, red, slots, sems)
            else:
                gains_out[...] = total
    for p in range(3):
        red.wait(7, p)
    red.finish()
    for stage in range(4):
        await_bytes(slots.at[stage, pl.ds(0, 1 if stage == 0 else 3)], gsend.at[stage])


def reduce_tail(cap, g, gains):
    q = g.shape[0] // 96
    out, gains = pl.pallas_call(
        tail_kernel,
        out_shape=(
            jax.ShapeDtypeStruct(g.shape, BF16),
            jax.ShapeDtypeStruct((8, 128), F32),
        ),
        in_specs=[VM] * 2,
        out_specs=(VM,) * 2,
        scratch_shapes=reducer_scratch(q)
        + [
            pltpu.VMEM((4, 4, 8, 128), F32),
            pltpu.VMEM((4, 8, 128), F32),
            pltpu.SemaphoreType.DMA((4,)),
            pltpu.SemaphoreType.DMA((4,)),
        ],
        compiler_params=pltpu.CompilerParams(collective_id=20 + cap, has_side_effects=True, vmem_limit_bytes=60 << 20),
        name="reduce_tail",
    )(g, gains)
    return out, gains


def backward_tiles(scale, lines, dlines_in, dlines):
    n = TILE * SEG
    mask = same_line()
    low = lax.broadcasted_iota(jnp.int32, (n, 128), 1) < 64

    def attend(t, carry):
        part = pl.ds(pl.multiple_of(t * TILE, TILE), TILE)
        x = lines[:, part, :].reshape(n, 384)
        up = dlines_in[:, part, :].reshape(n, 128)
        q, k, v = x[:, :128], x[:, 128:256], x[:, 256:]
        outs = []
        for first in (low, ~low):
            p = head_probs(q, k, first, mask, scale)
            g = dot(jnp.where(first, up, jnp.zeros_like(up)), v, NT)
            ds = (p * (g - jnp.sum(g * p, axis=-1, keepdims=True)) * scale).astype(BF16)
            outs.append((dot(ds, k, NN), dot(ds, q, TN), dot(p.astype(BF16), up, TN)))
        for j in range(3):
            dlines[:, part, pl.ds(128 * j, 128)] = (
                jnp.where(low, outs[0][j], outs[1][j]).astype(BF16).reshape(SEG, TILE, 128)
            )
        return carry

    return attend


def backward_kernel(cap, scale, dmixed, lines, table, g, dproj, out, recv, wide128, gathered, sorter, dlines_in,
                    dlines, wide32, back, sems, *scratch):
    me = lax.axis_index("space")
    count = recv.shape[0]
    red = Reducer(me, g, out, *scratch)
    greet_all(me, count, True)
    send_to_lines(me, count, 1, dmixed, recv, sems.at[0], sems.at[1])
    red.start()
    build_sorter(table[...], sorter)
    await_bytes(recv, sems.at[1])
    red.step(0)
    sort_blocks(cap, recv, wide128, gathered, sorter, dlines_in)
    attend = backward_tiles(scale, lines, dlines_in, dlines)
    tiles = cap * count // TILE
    lax.fori_loop(0, tiles // 2, attend, 0)
    red.step(1)
    lax.fori_loop(tiles // 2, tiles, attend, 0)
    red.step(2)
    unsort_blocks(cap, dlines, wide32, sorter, back)
    send_home(me, count, 3, back, dproj, sems.at[2], sems.at[3])
    for stage in range(3, 7):
        red.step(stage)
    await_bytes(recv.at[pl.ds(0, count - 1)], sems.at[0])
    await_bytes(back.at[pl.ds(0, count - 1)], sems.at[2])
    await_bytes(dproj, sems.at[3])
    for p in range(3):
        red.wait(7, p)
    red.finish()


def forward_scratch(cap, count):
    n = cap * count
    span = cap * SEG
    return [
        pltpu.VMEM((count, span, 384), BF16),
        pltpu.VMEM((count, 8, 128), jnp.int32),
        pltpu.VMEM((3, count * span, 128), F32),
        pltpu.VMEM((n, 384), BF16),
        pltpu.VMEM((n, n), BF16),
        pltpu.VMEM((SEG, n, 128), BF16),
        pltpu.VMEM((1, count * span, 128), F32),
        pltpu.VMEM((count, span, 128), BF16),
        pltpu.SemaphoreType.DMA((6,)),
    ]


def forward_lines(proj, tagt, cap, count, scale):
    n = cap * count
    span = cap * SEG
    return pl.pallas_call(
        functools.partial(forward_kernel, cap, scale),
        out_shape=(
            jax.ShapeDtypeStruct((BINS, span, 512), BF16),
            jax.ShapeDtypeStruct((SEG, n, 384), BF16),
            jax.ShapeDtypeStruct((8, 128), jnp.int32),
        ),
        in_specs=[VM] * 2,
        out_specs=(VM,) * 3,
        scratch_shapes=forward_scratch(cap, count),
        compiler_params=pltpu.CompilerParams(collective_id=cap, has_side_effects=True, vmem_limit_bytes=60 << 20),
        name="forward_lines",
    )(proj, tagt)


def backward_lines(dmixed, lines, table, g, cap, count, scale):
    q = g.shape[0] // 96
    n = cap * count
    span = cap * SEG
    dproj, out = pl.pallas_call(
        functools.partial(backward_kernel, cap, scale),
        out_shape=(
            jax.ShapeDtypeStruct((BINS, span, 1536), BF16),
            jax.ShapeDtypeStruct(g.shape, BF16),
        ),
        in_specs=[VM] * 4,
        out_specs=(VM,) * 2,
        scratch_shapes=[
            pltpu.VMEM((count, span, 128), BF16),
            pltpu.VMEM((1, count * span, 128), F32),
            pltpu.VMEM((n, 128), BF16),
            pltpu.VMEM((n, n), BF16),
            pltpu.VMEM((SEG, n, 128), BF16),
            pltpu.VMEM((SEG, n, 384), BF16),
            pltpu.VMEM((3, count * span, 128), F32),
            pltpu.VMEM((count, span, 384), BF16),
            pltpu.SemaphoreType.DMA((4,)),
        ]
        + reducer_scratch(q),
        compiler_params=pltpu.CompilerParams(collective_id=10 + cap, has_side_effects=True, vmem_limit_bytes=60 << 20),
        name="backward_lines",
    )(dmixed, lines, table, g)
    return dproj, out


def step_back_kernel(scale, dmixed, lines, table, activated, upstream, normed_mlp, dpre, mixed, dhidden_b, normed, w_qkv,
                     unit, inv, dhidden, gain, mlp_gain_sum, pack, grad_states, early, late, gains_out,
                     recv, wide128, gathered, sorter, dlines_in, dlines, wide32, back, dproj, g, g_late, shifted, sems, *scratch):
    me = lax.axis_index("space")
    cap = 4
    count = recv.shape[0]
    red = Reducer(me, g, early, *scratch[:9])
    red_late = Reducer(me, g_late, late, *scratch[9:18])
    slots, held, gsend, grecv = scratch[18:]
    gain_refs = (held, gsend, grecv)

    def blocks(j, width=512):
        return pl.ds(pl.multiple_of(j * width, width), width)

    def down_sum(j, carry):
        g[blocks(j), :] = dot(activated[:, blocks(j)], upstream[...], TN).astype(BF16)
        return carry

    def up_sum(j, carry):
        g[blocks(j + 4), :] = dot(normed_mlp[...], dpre[:, blocks(j)], TN).astype(BF16)
        return carry

    def work():
        lax.fori_loop(0, 4, down_sum, 0)
        lax.fori_loop(0, 4, up_sum, 0)
        g[pl.ds(4096, 512), :] = dot(mixed[...], dhidden_b[...], TN).astype(BF16)

    greet_all(me, count, True, work)
    send_to_lines(me, count, 1, dmixed, recv, sems.at[0], sems.at[1])
    red.start()
    build_sorter(table[...], sorter)
    await_bytes(recv, sems.at[1])
    sort_blocks(cap, recv, wide128, gathered, sorter, dlines_in)
    attend = backward_tiles(scale, lines, dlines_in, dlines)
    tiles = cap * count // TILE
    lax.fori_loop(0, tiles // 2, attend, 0)
    red.step(0)
    lax.fori_loop(tiles // 2, tiles, attend, 0)
    unsort_blocks(cap, dlines, wide32, sorter, back)
    send_home(me, count, 3, back, dproj, sems.at[2], sems.at[3])
    red.step(1)
    red.step(2)
    await_bytes(dproj, sems.at[3])
    rows = BINS * cap * SEG

    def late_sum(j, carry):
        rhs = dproj[:, :, blocks(j)].reshape(rows, 512)
        g_late[blocks(j), :] = dot(normed[...], rhs, TN).astype(BF16)
        return carry

    lax.fori_loop(0, 3, late_sum, 0)
    red_late.start()

    def norm_chunk(i, total):
        part = pl.ds(pl.multiple_of(i * 128, 128), 128)
        dn = dot(dproj[pl.ds(i * 4, 4)].reshape(128, 1536), w_qkv[...], NT).astype(BF16).astype(F32)
        u = unit[part, :]
        shifted[part, :] = (dhidden[part, :] + norm_back(u, inv[part, :], gain[...], dn)).astype(BF16)
        return total + jnp.sum(u * dn, axis=0, keepdims=True)

    total = lax.fori_loop(0, rows // 128, norm_chunk, jnp.zeros((1, 512), F32))
    for j in range(4):
        held[0, pl.ds(j, 1), :] = total[:, 128 * j : 128 * (j + 1)]
    held[0, pl.ds(4, 4), :] = mlp_gain_sum[...]
    sum_gains(0, red, slots, gain_refs)
    red_late.step(0)
    grad_states[...] = dot(pack[...], shifted[...], TN).astype(BF16)
    for stage in range(7):
        if stage > 0:
            red_late.step(stage)
        if stage == 0:
            red.step(3)
        if stage == 1:
            red.step(4)
        if stage == 2:
            red.step(5)
        if stage == 5:
            red.step(6)
        if stage < 4:
            some = gather_gains(stage, slots, gain_refs)
            if stage < 3:
                held[stage + 1] = some
                sum_gains(stage + 1, red, slots, gain_refs)
            else:
                gains_out[...] = some
    for p in range(3):
        red.wait(7, p)
        red_late.wait(7, p)
    red.finish()
    red_late.finish()
    for stage in range(4):
        await_bytes(slots.at[stage, pl.ds(0, 1 if stage == 0 else 3)], gsend.at[stage])
    await_bytes(recv.at[pl.ds(0, count - 1)], sems.at[0])
    await_bytes(back.at[pl.ds(0, count - 1)], sems.at[2])


def step_back(scale, *args):
    cap, count = 4, 64
    n = cap * count
    span = cap * SEG
    rows = BINS * span
    out = pl.pallas_call(
        functools.partial(step_back_kernel, scale),
        out_shape=(
            jax.ShapeDtypeStruct((512, 512), BF16),
            jax.ShapeDtypeStruct((4608, 512), BF16),
            jax.ShapeDtypeStruct((1536, 512), BF16),
            jax.ShapeDtypeStruct((8, 128), F32),
        ),
        in_specs=[VM] * len(args),
        out_specs=(VM,) * 4,
        scratch_shapes=[
            pltpu.VMEM((count, span, 128), BF16),
            pltpu.VMEM((1, count * span, 128), F32),
            pltpu.VMEM((n, 128), BF16),
            pltpu.VMEM((n, n), BF16),
            pltpu.VMEM((SEG, n, 128), BF16),
            pltpu.VMEM((SEG, n, 384), BF16),
            pltpu.VMEM((3, count * span, 128), F32),
            pltpu.VMEM((count, span, 384), BF16),
            pltpu.VMEM((BINS, span, 1536), BF16),
            pltpu.VMEM((4608, 512), BF16),
            pltpu.VMEM((1536, 512), BF16),
            pltpu.VMEM((rows, 512), BF16),
            pltpu.SemaphoreType.DMA((4,)),
        ]
        + reducer_scratch(48)
        + reducer_scratch(16)
        + [
            pltpu.VMEM((4, 4, 8, 128), F32),
            pltpu.VMEM((4, 8, 128), F32),
            pltpu.SemaphoreType.DMA((4,)),
            pltpu.SemaphoreType.DMA((4,)),
        ],
        compiler_params=pltpu.CompilerParams(collective_id=30, has_side_effects=True, vmem_limit_bytes=62 << 20),
        name="step_back",
    )(*args)
    return out


def route_four(me, owner_c, owner_r, place_r, pack, tagt):
    n = 64
    owner_c, owner_r, place_r = owner_c.astype(F32), owner_r.astype(F32), place_r.astype(F32)
    rows = lax.broadcasted_iota(jnp.int32, (n, n), 0)
    cols = lax.broadcasted_iota(jnp.int32, (n, n), 1)

    def one(mask):
        return jnp.where(mask, 1.0, 0.0)

    same = one(owner_c == owner_r)
    rank_r = jnp.sum(same * one(rows < cols), axis=0, keepdims=True)
    rank_c = jnp.sum(same * one(cols < rows), axis=1, keepdims=True)
    load_r = jnp.sum(same, axis=0, keepdims=True)
    load_c = jnp.sum(same, axis=1, keepdims=True)
    first = one(rank_c == 0.0)
    index = jnp.sum(first * one(load_c == load_r) * one(owner_c < owner_r), axis=0, keepdims=True)
    n3 = jnp.sum(first * one(load_c == 3.0), axis=0, keepdims=True)
    n2 = jnp.sum(first * one(load_c == 2.0), axis=0, keepdims=True)
    base1 = jnp.where(index < n3, 4.0 * index + 3.0, 3.0 * n3 + 2.0 * n2 + index)
    base = jnp.where(load_r == 3.0, 4.0 * index, jnp.where(load_r == 2.0, 4.0 * n3 + 2.0 * index, base1))
    slot = base + rank_r
    tag = (base - 4.0 * jnp.floor(base * 0.25)) * n + place_r + 1.0
    spread = one(lax.div(lax.broadcasted_iota(jnp.int32, (n, 512), 1), SEG) == lax.broadcasted_iota(jnp.int32, (n, 512), 0))
    target = dot(jnp.broadcast_to(slot, (8, n)).astype(BF16), spread.astype(BF16), NN)[0:1]
    target = target * SEG + lax.rem(lax.broadcasted_iota(jnp.int32, (1, 512), 1), SEG).astype(F32)
    ids = lax.broadcasted_iota(jnp.int32, (512, 512), 0).astype(F32)
    pack[...] = one(ids == target).astype(BF16)
    tags = jnp.sum(one(rows.astype(F32) == slot) * tag, axis=1, keepdims=True)
    lane = lax.broadcasted_iota(jnp.int32, (1, 128), 1)
    tagt[...] = jnp.zeros_like(tagt)
    for b in range(BINS):
        for s in range(2):
            i = 4 * b + 2 * s
            row = jnp.where(lane == me, tags[i : i + 1], jnp.where(lane == me + n, tags[i + 1 : i + 2], 0.0))
            tagt[b, pl.ds(s, 1), :] = row.astype(jnp.int32)


def step_forward_kernel(scale, states, cotangent, owner_c, owner_r, place_r, gain, w_qkv, mixed, lines, table, pack, upstream,
                        flat_b, normed, unit, inv, proj, tagt, *scratch):
    me = lax.axis_index("space")

    def work():
        route_four(me, owner_c[...], owner_r[...], place_r[...], pack, tagt)

        def chunk(i, carry):
            part = pl.ds(pl.multiple_of(i * 128, 128), 128)
            f = dot(pack[part, :], states[...], NN).astype(BF16)
            flat_b[part, :] = f
            u, v = norm_stats(f.astype(F32))
            unit[part, :] = u
            inv[part, :] = v
            x = (u * gain[...]).astype(BF16)
            normed[part, :] = x
            proj[pl.ds(i * 4, 4)] = dot(x, w_qkv[...], NN).astype(BF16).reshape(4, 32, 1536)
            upstream[part, :] = dot(pack[part, :], cotangent[...], NN).astype(BF16)
            return carry

        lax.fori_loop(0, 4, chunk, 0)

    forward_kernel(4, scale, proj, tagt, mixed, lines, table, *scratch, work=work)


def step_forward(scale, *args):
    cap, count = 4, 64
    n = cap * count
    span = cap * SEG
    return pl.pallas_call(
        functools.partial(step_forward_kernel, scale),
        out_shape=(
            jax.ShapeDtypeStruct((BINS, span, 512), BF16),
            jax.ShapeDtypeStruct((SEG, n, 384), BF16),
            jax.ShapeDtypeStruct((8, 128), jnp.int32),
            jax.ShapeDtypeStruct((512, 512), BF16),
            jax.ShapeDtypeStruct((512, 512), BF16),
            jax.ShapeDtypeStruct((512, 512), BF16),
            jax.ShapeDtypeStruct((512, 512), BF16),
            jax.ShapeDtypeStruct((512, 512), F32),
            jax.ShapeDtypeStruct((512, 1), F32),
        ),
        in_specs=[VM] * len(args),
        out_specs=(VM,) * 9,
        scratch_shapes=[pltpu.VMEM((BINS, span, 1536), BF16), pltpu.VMEM((BINS, 8, 128), jnp.int32)]
        + forward_scratch(cap, count),
        compiler_params=pltpu.CompilerParams(collective_id=31, has_side_effects=True, vmem_limit_bytes=60 << 20),
        name="step_forward",
    )(*args)


def fits_four(owner):
    same = owner[:, None] == owner[None, :]
    load = jnp.sum(same, axis=1, dtype=jnp.int32)
    threes = jnp.sum(load == 3, dtype=jnp.int32)
    twos = jnp.sum(load == 2, dtype=jnp.int32)
    return 4 * threes + 3 * twos <= 3 * owner.shape[0]


def per_device(*args):
    return lax.cond(fits_four(args[2]), functools.partial(block, 4), functools.partial(block, 6), *args)


def block(
    cap, states, cotangent, send_owner, line_place, gain_attn, w_qkv, w_out, gain_mlp, w_up, w_down
):
    width = states.shape[2]
    rows = states.shape[1]
    nspace = lax.axis_size("space")
    total_rows = rows * nspace * lax.axis_size("dp")
    nblocks = send_owner.shape[0]
    slots = BINS * cap
    wide = 2 * (width // HEADS)
    head_dim = width // HEADS
    scale = head_dim ** (-0.5)
    span = cap * SEG
    if cap == 4:
        mixed, lines, table, pack, upstream, flat_b, normed, unit_a, inv_a = step_forward(
            scale, states[0], cotangent[0], send_owner[:, None], send_owner[None], line_place[None], gain_attn[None], w_qkv
        )
        flat = flat_b.astype(F32)
        mixed = mixed.reshape(BINS * span, width)
    else:
        slot, tag = routing(send_owner, line_place, cap)
        me = lax.axis_index("space")
        hit = slot[None, :] == jnp.arange(slots, dtype=jnp.int32)[:, None]
        tags = jnp.sum(jnp.where(hit, tag[None, :] + 1, 0), axis=1).reshape(BINS, cap // 2, 2)
        tags = jnp.pad(tags, ((0, 0), (0, 8 - cap // 2), (0, 0)))
        at_me = jnp.arange(nspace, dtype=jnp.int32) == me
        tagt = jnp.where(at_me[None, None, None, :], tags[..., None], 0).reshape(BINS, 8, 2 * nspace)
        target = (slot[:, None] * SEG + jnp.arange(SEG, dtype=jnp.int32)[None, :]).reshape(rows)
        pack = (jnp.arange(slots * SEG, dtype=jnp.int32)[:, None] == target[None, :]).astype(BF16)

        flat_b = dot(pack, states[0], NN).astype(BF16)
        upstream = dot(pack, cotangent[0], NN).astype(BF16)
        flat = flat_b.astype(F32)
        unit_a, inv_a = norm_stats(flat)
        normed = (unit_a * gain_attn).astype(BF16)
        projected = dot(normed, w_qkv, NN).astype(BF16)
        mixed, lines, table = forward_lines(projected.reshape(BINS, span, 3 * width), tagt, cap, nspace, scale)
        mixed = mixed.reshape(BINS * span, width)

    hidden = (flat + dot(mixed, w_out, NN)).astype(BF16)
    hidden32 = hidden.astype(F32)
    unit_m, inv_m = norm_stats(hidden32)
    normed_mlp = (unit_m * gain_mlp).astype(BF16)
    act32, slope = gelu_parts(dot(normed_mlp, w_up, NN))
    activated = act32.astype(BF16)
    output = (hidden32 + dot(activated, w_down, NN)).astype(BF16)
    dpre = (slope * dot(upstream, w_down, NT)).astype(BF16)
    dnormed_mlp = dot(dpre, w_up, NT)
    grad_gain_mlp = jnp.sum(unit_m * dnormed_mlp, axis=0)
    dhidden = upstream.astype(F32) + norm_back(unit_m, inv_m, gain_mlp, dnormed_mlp)
    dhidden_b = dhidden.astype(BF16)
    dmixed = dot(dhidden_b, w_out, NT).astype(BF16)
    output = dot(pack, output, TN).astype(BF16)
    if cap == 4:
        grad_states, early, late, gains = step_back(
            scale, dmixed.reshape(BINS, span, width), lines, table, activated, upstream, normed_mlp, dpre, mixed, dhidden_b,
            normed, w_qkv, unit_a, inv_a, dhidden, gain_attn[None], grad_gain_mlp.reshape(4, 128), pack,
        )
    else:
        early = [dot(activated, upstream, TN)]
        early += [dot(normed_mlp, dpre[:, j * width : (j + 1) * width], TN) for j in range(4)]
        early += [dot(mixed, dhidden_b, TN)]
        early = jnp.concatenate([v.astype(BF16) for v in early], axis=0)

        dprojected, early = backward_lines(dmixed.reshape(BINS, span, width), lines, table, early, cap, nspace, scale)
        dprojected = dprojected.reshape(BINS * span, 3 * width)
        late = [dot(normed, dprojected[:, j * width : (j + 1) * width], TN) for j in range(3)]
        late = jnp.concatenate([v.astype(BF16) for v in late], axis=0)
        dnormed = dot(dprojected, w_qkv, NT).astype(BF16).astype(F32)
        grad_gain_attn = jnp.sum(unit_a * dnormed, axis=0)
        grad_states = (dhidden + norm_back(unit_a, inv_a, gain_attn, dnormed)).astype(BF16)
        grad_states = dot(pack, grad_states, TN).astype(BF16)
        late, gains = reduce_tail(cap, late, jnp.concatenate([grad_gain_attn, grad_gain_mlp]).reshape(8, 128))
    factor = 1.0 / math.sqrt(total_rows)
    gains = gains.reshape(2, width) * factor
    hidden_units = w_up.shape[1]

    def columns(blocks):
        blocks = blocks.reshape(-1, width, width)
        return jnp.concatenate([blocks[j].astype(F32) * factor for j in range(blocks.shape[0])], axis=1)

    return (
        output[None],
        grad_states[None],
        gains[0],
        columns(late),
        early[2 * hidden_units :].astype(F32) * factor,
        gains[1],
        columns(early[hidden_units : 2 * hidden_units]),
        early[:hidden_units].astype(F32) * factor,
    )


def solution(mesh):
    placed = (
        P("dp", "space", None),
        P("dp", "space", None),
        P("space"),
        P("space"),
        P(),
        P(),
        P(),
        P(),
        P(),
        P(),
    )
    return jax.shard_map(
        per_device,
        mesh=mesh,
        in_specs=placed,
        out_specs=(P("dp", "space", None), P("dp", "space", None), P(), P(), P(), P(), P(), P()),
        check_vma=False,
    )
```

```python
import functools
import math

import jax
import jax.numpy as jnp
from jax import lax
from jax.experimental import pallas as pl
from jax.experimental.pallas import tpu as pltpu
from jax.sharding import PartitionSpec as P

HEADS = 8
SEG = 8
FRAG = 4
BINS = 16
PAIRS = 4

EPSILON = 1e-05
F32 = jnp.float32
BF16 = jnp.bfloat16
MESH = pl.DeviceIdType.MESH


def dot(a, b, dims):
    return lax.dot_general(a, b, (dims, ((), ())), preferred_element_type=F32)


NN = ((1,), (0,))
NT = ((1,), (1,))
TN = ((0,), (0,))


def norm_stats(v):
    center = v - jnp.mean(v, axis=-1, keepdims=True)
    inv = lax.rsqrt(jnp.mean(center * center, axis=-1, keepdims=True) + EPSILON)
    return center * inv, inv


def norm_back(unit, inv, gain, upstream):
    g = upstream * gain
    m1 = jnp.mean(g, axis=-1, keepdims=True)
    m2 = jnp.mean(g * unit, axis=-1, keepdims=True)
    return inv * (g - m1 - unit * m2)


GELU_C = math.sqrt(2.0 / math.pi)


def gelu_parts(v):
    t = jnp.tanh(GELU_C * (v + 0.044715 * (v * v * v)))
    value = 0.5 * v * (1.0 + t)
    slope = 0.5 * (1.0 + t) + 0.5 * v * (1.0 - t * t) * (GELU_C * (1.0 + 3 * 0.044715 * (v * v)))
    return value, slope


def routing(owner, place, cap):
    n = owner.shape[0]
    ids = jnp.arange(n, dtype=jnp.int32)
    same = owner[:, None] == owner[None, :]
    rank = jnp.sum(same & (ids[None, :] < ids[:, None]), axis=1, dtype=jnp.int32)
    load = jnp.sum(same, axis=1, dtype=jnp.int32)
    first = rank == 0
    ahead = first[None, :] & (load[None, :] == load[:, None]) & (owner[None, :] < owner[:, None])
    index = jnp.sum(ahead, axis=1, dtype=jnp.int32)
    n3 = jnp.sum(first & (load == 3), dtype=jnp.int32)
    n2 = jnp.sum(first & (load == 2), dtype=jnp.int32)
    if cap == 4:
        spare = index < n3
        base1 = jnp.where(spare, 4 * index + 3, 3 * n3 + 2 * n2 + index)
        base = jnp.where(load == 3, 4 * index, jnp.where(load == 2, 4 * n3 + 2 * index, base1))
        return base + rank, (base % cap) * n + place
    odd = (n3 % 2) == 1
    base3 = 3 * index
    base2 = 3 * n3 + 2 * index + jnp.where(odd & (index >= 1), 1, 0)
    base1 = 3 * n3 + 2 * n2 + jnp.where(odd & (n2 >= 2), 1, 0) + index
    base = jnp.where(load == 3, base3, jnp.where(load == 2, base2, base1))
    return base + rank, (base % cap) * n + place


def partner_of(me, k):
    ys = lax.rem(lax.div(me, 16) + lax.div(k, 16), 4)
    zs = lax.rem(lax.div(lax.rem(me, 16), 4) + lax.div(lax.rem(k, 16), 4), 4)
    xs = lax.rem(lax.rem(me, 4) + lax.rem(k, 4), 4)
    return ys * 16 + zs * 4 + xs


def greet_all(me, count, pair=False, work=None):
    barrier = pltpu.get_barrier_semaphore()

    def greet(k, carry):
        pl.semaphore_signal(barrier, inc=1, device_id={"space": partner_of(me, k)}, device_id_type=MESH)
        return carry

    lax.fori_loop(1, count, greet, 0)
    if pair:
        pl.semaphore_signal(barrier, inc=1, device_id={"dp": 1 - lax.axis_index("dp")}, device_id_type=MESH)
    if work is not None:
        work()
    pl.semaphore_wait(barrier, count if pair else count - 1)


def remote(src, dst, send_sem, recv_sem, device):
    return pltpu.make_async_remote_copy(
        src_ref=src, dst_ref=dst, send_sem=send_sem, recv_sem=recv_sem,
        device_id={"space": device}, device_id_type=MESH,
    )


def lanes(j, pair):
    return pl.ds(pl.multiple_of(j * 512 + pair * 128, 128), 128)


def send_to_lines(me, count, pieces, src, recv, send_sem, recv_sem, extra=None):
    def send(k, carry):
        to = partner_of(me, k)
        for j in range(pieces):
            remote(src.at[lax.div(to, PAIRS), :, lanes(j, lax.rem(to, PAIRS))],
                   recv.at[me, :, pl.ds(128 * j, 128)], send_sem, recv_sem, to).start()
        if extra is not None:
            remote(extra[0].at[lax.div(to, PAIRS)], extra[1].at[me], extra[2], extra[3], to).start()
        return carry

    for j in range(pieces):
        pltpu.make_async_copy(src.at[lax.div(me, PAIRS), :, lanes(j, lax.rem(me, PAIRS))],
                              recv.at[me, :, pl.ds(128 * j, 128)], recv_sem).start()
    if extra is not None:
        pltpu.make_async_copy(extra[0].at[lax.div(me, PAIRS)], extra[1].at[me], extra[3]).start()
    lax.fori_loop(1, count, send, 0)


def send_home(me, count, pieces, src, home, send_sem, recv_sem):
    mine = lax.div(me, PAIRS)
    pair = lax.rem(me, PAIRS)

    def send(k, carry):
        to = partner_of(me, k)
        for j in range(pieces):
            remote(src.at[to, :, pl.ds(128 * j, 128)], home.at[mine, :, lanes(j, pair)],
                   send_sem, recv_sem, to).start()
        return carry

    for j in range(pieces):
        pltpu.make_async_copy(src.at[me, :, pl.ds(128 * j, 128)], home.at[mine, :, lanes(j, pair)], recv_sem).start()
    lax.fori_loop(1, count, send, 0)


def await_bytes(ref, sem):
    pltpu.make_async_copy(ref, ref, sem).wait()


def build_sorter(table, sorter):
    n = sorter.shape[0]
    for c in range(n // 128):
        ids = lax.broadcasted_iota(jnp.int32, (n, 128), 0)
        sorter[:, pl.ds(128 * c, 128)] = jnp.where(ids == table[c : c + 1, :] - 1, 1.0, 0.0).astype(BF16)


def sort_blocks(cap, recv, wide32, gathered, sorter, out):
    count = recv.shape[0]
    span = cap * SEG

    def widen(d, carry):
        for j in range(wide32.shape[0]):
            part = recv[d, :, pl.ds(128 * j, 128)]
            wide32[j, pl.ds(pl.multiple_of(d * span, 8), span), :] = part.astype(F32)
        return carry

    lax.fori_loop(0, count, widen, 0)

    def sort(r, carry):
        for s in range(cap):
            for j in range(wide32.shape[0]):
                part = wide32[j, pl.ds(s * SEG + r, count, stride=span), :]
                gathered[pl.ds(s * count, count), pl.ds(128 * j, 128)] = part.astype(BF16)
        out[r] = dot(sorter[...], gathered[...], NN).astype(BF16)
        return carry

    lax.fori_loop(0, SEG, sort, 0, unroll=cap == 4)


def unsort_blocks(cap, src, wide32, sorter, out):
    count = out.shape[0]
    span = cap * SEG
    def unsort(r, carry):
        back = dot(sorter[...], src[r], TN)
        for s in range(cap):
            for j in range(wide32.shape[0]):
                part = back[s * count : (s + 1) * count, 128 * j : 128 * (j + 1)]
                wide32[j, pl.ds(s * SEG + r, count, stride=span), :] = part
        return carry

    lax.fori_loop(0, SEG, unsort, 0, unroll=cap == 4)

    def narrow(d, carry):
        for j in range(wide32.shape[0]):
            part = wide32[j, pl.ds(pl.multiple_of(d * span, 8), span), :]
            out[d, :, pl.ds(128 * j, 128)] = part.astype(BF16)
        return carry

    lax.fori_loop(0, count, narrow, 0)


TILE = 32


def same_line():
    n = TILE * SEG
    a = lax.div(lax.rem(lax.broadcasted_iota(jnp.int32, (n, n), 0), TILE), FRAG)
    b = lax.div(lax.rem(lax.broadcasted_iota(jnp.int32, (n, n), 1), TILE), FRAG)
    return a == b


def head_probs(q, k, first, mask, scale):
    q = jnp.where(first, q, jnp.zeros_like(q))
    expo = jnp.where(mask, jnp.exp(dot(q, k, NT) * scale), 0.0)
    return expo / jnp.sum(expo, axis=-1, keepdims=True)


def forward_kernel(cap, scale, proj, tagt, mixed, lines, table, recv, trecv, wide32, gathered, sorter,
                   attended, wide128, back, sems, work=None):
    me = lax.axis_index("space")
    count = recv.shape[0]
    greet_all(me, count, work=work)
    send_to_lines(me, count, 3, proj, recv, sems.at[0], sems.at[1], (tagt, trecv, sems.at[2], sems.at[3]))
    await_bytes(trecv, sems.at[3])
    table[...] = jnp.sum(trecv[...], axis=0)
    build_sorter(table[...], sorter)
    await_bytes(recv, sems.at[1])
    sort_blocks(cap, recv, wide32, gathered, sorter, lines)
    n = TILE * SEG
    mask = same_line()
    low = lax.broadcasted_iota(jnp.int32, (n, 128), 1) < 64

    def attend(t, carry):
        part = pl.ds(pl.multiple_of(t * TILE, TILE), TILE)
        x = lines[:, part, :].reshape(n, 384)
        q, k, v = x[:, :128], x[:, 128:256], x[:, 256:]
        outs = []
        for first in (low, ~low):
            w = head_probs(q, k, first, mask, scale).astype(BF16)
            outs.append(dot(w, v, NN))
        attended[:, part, :] = jnp.where(low, outs[0], outs[1]).astype(BF16).reshape(SEG, TILE, 128)
        return carry

    lax.fori_loop(0, cap * count // TILE, attend, 0, unroll=2 if cap == 4 else 1)
    unsort_blocks(cap, attended, wide128, sorter, back)
    send_home(me, count, 1, back, mixed, sems.at[4], sems.at[5])
    await_bytes(recv.at[pl.ds(0, count - 1)], sems.at[0])
    await_bytes(trecv.at[pl.ds(0, count - 1)], sems.at[2])
    await_bytes(back.at[pl.ds(0, count - 1)], sems.at[4])
    await_bytes(mixed, sems.at[5])


VM = pl.BlockSpec(memory_space=pltpu.VMEM)


class Reducer:
    def __init__(self, me, g, out, pair, s0, r1, s1, r2, s2, r3, send, recv):
        self.me, self.g, self.out, self.pair, self.s0, self.r1, self.s1 = me, g, out, pair, s0, r1, s1
        self.r2, self.s2, self.r3, self.send, self.recv = r2, s2, r3, send, recv
        self.q = s2.shape[1]
        self.core = lax.axis_index("dp")
        self.place = (lax.div(me, 16), lax.rem(lax.div(me, 4), 4), lax.rem(me, 4))

    def peers(self, axis):
        step = (16, 4, 1)[axis]
        mine = self.place[axis]
        for k in (1, 2, 3):
            there = lax.rem(mine + k, 4)
            yield k - 1, there, self.me + (there - mine) * step

    def rows(self, half, p, u=None, v=None):
        q = self.q
        start, size = (half * 3 + p) * 16 * q, 16 * q
        if u is not None:
            start, size = start + u * 4 * q, 4 * q
        if v is not None:
            start, size = start + v * q, q
        return pl.ds(pl.multiple_of(start, 16), size)

    def copy(self, stage, p, src, dst, device):
        pltpu.make_async_remote_copy(
            src_ref=src, dst_ref=dst, send_sem=self.send.at[stage, p], recv_sem=self.recv.at[stage, p],
            device_id=device, device_id_type=MESH,
        ).start()

    def wait(self, stage, p):
        await_bytes(self.sized(stage, p), self.recv.at[stage, p])

    def sized(self, stage, p):
        return (self.pair, self.r1, self.r2, self.r3, self.r3, self.r2, self.r1, self.pair)[stage].at[p]

    def start(self):
        for p in range(3):
            self.copy(0, p, self.g.at[self.rows(1 - self.core, p)], self.pair.at[p], {"dp": 1 - self.core})

    def step(self, stage):
        for p in range(3):
            self.wait(stage, p)
            a, b, c = p, (p + 1) % 3, (p + 2) % 3
            ia, ib, ic = self.place[a], self.place[b], self.place[c]
            shard = pl.ds(pl.multiple_of(ic * 128, 128), 128)
            if stage == 0:

                def add(i, carry):
                    u, v = lax.div(i, 4), lax.rem(i, 4)
                    both = self.g[self.rows(self.core, p, u, v)].astype(F32)
                    both += self.pair[p, pl.ds(pl.multiple_of(i * self.q, 16), self.q)].astype(F32)
                    self.s0[p, u, v] = both.astype(BF16)
                    return carry

                lax.fori_loop(0, 16, add, 0)
                for k, there, device in self.peers(a):
                    self.copy(1, p, self.s0.at[p, there], self.r1.at[p, k], {"space": device})
            elif stage == 1:

                def add4(u, carry):
                    total = self.s0[p, ia, u].astype(F32)
                    for k in range(3):
                        total += self.r1[p, k, u].astype(F32)
                    self.s1[p, u] = total.astype(BF16)
                    return carry

                lax.fori_loop(0, 4, add4, 0)
                for k, there, device in self.peers(b):
                    self.copy(2, p, self.s1.at[p, there], self.r2.at[p, k], {"space": device})
            elif stage == 2:
                total = self.s1[p, ib].astype(F32)
                for k in range(3):
                    total += self.r2[p, k].astype(F32)
                self.s2[p] = total.astype(BF16)
                for k, there, device in self.peers(c):
                    part = pl.ds(pl.multiple_of(there * 128, 128), 128)
                    self.copy(3, p, self.s2.at[p, :, part], self.r3.at[p, k], {"space": device})
            elif stage == 3:
                total = self.s2[p, :, shard].astype(F32)
                for k in range(3):
                    total += self.r3[p, k].astype(F32)
                self.out[self.rows(self.core, p, ia, ib), shard] = total.astype(BF16)
                for k, there, device in self.peers(c):
                    piece = self.out.at[self.rows(self.core, p, ia, ib), shard]
                    self.copy(4, p, piece, piece, {"space": device})
            elif stage == 4:
                for k, there, device in self.peers(b):
                    piece = self.out.at[self.rows(self.core, p, ia, ib)]
                    self.copy(5, p, piece, piece, {"space": device})
            elif stage == 5:
                for k, there, device in self.peers(a):
                    piece = self.out.at[self.rows(self.core, p, ia)]
                    self.copy(6, p, piece, piece, {"space": device})
            elif stage == 6:
                piece = self.out.at[self.rows(self.core, p)]
                self.copy(7, p, piece, piece, {"dp": 1 - self.core})

    def finish(self):
        for stage in range(8):
            for p in range(3):
                await_bytes(self.sized(stage, p), self.send.at[stage, p])


def reducer_scratch(q):
    return [
        pltpu.VMEM((3, 16 * q, 512), BF16),
        pltpu.VMEM((3, 4, 4, q, 512), BF16),
        pltpu.VMEM((3, 3, 4, q, 512), BF16),
        pltpu.VMEM((3, 4, q, 512), BF16),
        pltpu.VMEM((3, 3, q, 512), BF16),
        pltpu.VMEM((3, q, 512), BF16),
        pltpu.VMEM((3, 3, q, 128), BF16),
        pltpu.SemaphoreType.DMA((8, 3)),
        pltpu.SemaphoreType.DMA((8, 3)),
    ]


def sum_gains(stage, reducer, got, sems):
    slots, held, send, recv = got, sems[0], sems[1], sems[2]
    count = 2 if stage == 0 else 4
    mine = reducer.core if stage == 0 else reducer.place[stage - 1]
    slots[stage, mine] = held[stage]
    if stage == 0:
        pltpu.make_async_remote_copy(
            src_ref=held.at[0], dst_ref=slots.at[0, mine], send_sem=send.at[0], recv_sem=recv.at[0],
            device_id={"dp": 1 - mine}, device_id_type=MESH,
        ).start()
    else:
        for k, there, device in reducer.peers(stage - 1):
            remote(held.at[stage], slots.at[stage, mine], send.at[stage], recv.at[stage], device).start()


def gather_gains(stage, got, sems):
    slots, held, send, recv = got, sems[0], sems[1], sems[2]
    count = 2 if stage == 0 else 4
    await_bytes(slots.at[stage, pl.ds(0, count - 1)], recv.at[stage])
    total = slots[stage, 0]
    for k in range(1, count):
        total += slots[stage, k]
    return total


def tail_kernel(g, gains, out, gains_out, *scratch):
    me = lax.axis_index("space")
    red = Reducer(me, g, out, *scratch[:9])
    slots, held, gsend, grecv = scratch[9:]
    sems = (held, gsend, grecv)
    barrier = pltpu.get_barrier_semaphore()
    pl.semaphore_signal(barrier, inc=1, device_id={"dp": 1 - red.core}, device_id_type=MESH)
    for axis in range(3):
        for k, there, device in red.peers(axis):
            pl.semaphore_signal(barrier, inc=1, device_id={"space": device}, device_id_type=MESH)
    pl.semaphore_wait(barrier, 10)
    red.start()
    held[0] = gains[...]
    sum_gains(0, red, slots, sems)
    for stage in range(7):
        red.step(stage)
        if stage < 4:
            total = gather_gains(stage, slots, sems)
            if stage < 3:
                held[stage + 1] = total
                sum_gains(stage + 1, red, slots, sems)
            else:
                gains_out[...] = total
    for p in range(3):
        red.wait(7, p)
    red.finish()
    for stage in range(4):
        await_bytes(slots.at[stage, pl.ds(0, 1 if stage == 0 else 3)], gsend.at[stage])


def reduce_tail(cap, g, gains):
    q = g.shape[0] // 96
    out, gains = pl.pallas_call(
        tail_kernel,
        out_shape=(
            jax.ShapeDtypeStruct(g.shape, BF16),
            jax.ShapeDtypeStruct((8, 128), F32),
        ),
        in_specs=[VM] * 2,
        out_specs=(VM,) * 2,
        scratch_shapes=reducer_scratch(q)
        + [
            pltpu.VMEM((4, 4, 8, 128), F32),
            pltpu.VMEM((4, 8, 128), F32),
            pltpu.SemaphoreType.DMA((4,)),
            pltpu.SemaphoreType.DMA((4,)),
        ],
        compiler_params=pltpu.CompilerParams(collective_id=20 + cap, has_side_effects=True, vmem_limit_bytes=60 << 20),
        name="reduce_tail",
    )(g, gains)
    return out, gains


def backward_tiles(scale, lines, dlines_in, dlines):
    n = TILE * SEG
    mask = same_line()
    low = lax.broadcasted_iota(jnp.int32, (n, 128), 1) < 64

    def attend(t, carry):
        part = pl.ds(pl.multiple_of(t * TILE, TILE), TILE)
        x = lines[:, part, :].reshape(n, 384)
        up = dlines_in[:, part, :].reshape(n, 128)
        q, k, v = x[:, :128], x[:, 128:256], x[:, 256:]
        outs = []
        for first in (low, ~low):
            p = head_probs(q, k, first, mask, scale)
            g = dot(jnp.where(first, up, jnp.zeros_like(up)), v, NT)
            ds = (p * (g - jnp.sum(g * p, axis=-1, keepdims=True)) * scale).astype(BF16)
            outs.append((dot(ds, k, NN), dot(ds, q, TN), dot(p.astype(BF16), up, TN)))
        for j in range(3):
            dlines[:, part, pl.ds(128 * j, 128)] = (
                jnp.where(low, outs[0][j], outs[1][j]).astype(BF16).reshape(SEG, TILE, 128)
            )
        return carry

    return attend


def backward_kernel(cap, scale, dmixed, lines, table, g, dproj, out, recv, wide128, gathered, sorter, dlines_in,
                    dlines, wide32, back, sems, *scratch):
    me = lax.axis_index("space")
    count = recv.shape[0]
    red = Reducer(me, g, out, *scratch)
    greet_all(me, count, True)
    send_to_lines(me, count, 1, dmixed, recv, sems.at[0], sems.at[1])
    red.start()
    build_sorter(table[...], sorter)
    await_bytes(recv, sems.at[1])
    red.step(0)
    sort_blocks(cap, recv, wide128, gathered, sorter, dlines_in)
    attend = backward_tiles(scale, lines, dlines_in, dlines)
    tiles = cap * count // TILE
    lax.fori_loop(0, tiles // 2, attend, 0)
    red.step(1)
    lax.fori_loop(tiles // 2, tiles, attend, 0)
    red.step(2)
    unsort_blocks(cap, dlines, wide32, sorter, back)
    send_home(me, count, 3, back, dproj, sems.at[2], sems.at[3])
    for stage in range(3, 7):
        red.step(stage)
    await_bytes(recv.at[pl.ds(0, count - 1)], sems.at[0])
    await_bytes(back.at[pl.ds(0, count - 1)], sems.at[2])
    await_bytes(dproj, sems.at[3])
    for p in range(3):
        red.wait(7, p)
    red.finish()


def forward_scratch(cap, count):
    n = cap * count
    span = cap * SEG
    return [
        pltpu.VMEM((count, span, 384), BF16),
        pltpu.VMEM((count, 8, 128), jnp.int32),
        pltpu.VMEM((3, count * span, 128), F32),
        pltpu.VMEM((n, 384), BF16),
        pltpu.VMEM((n, n), BF16),
        pltpu.VMEM((SEG, n, 128), BF16),
        pltpu.VMEM((1, count * span, 128), F32),
        pltpu.VMEM((count, span, 128), BF16),
        pltpu.SemaphoreType.DMA((6,)),
    ]


def forward_lines(proj, tagt, cap, count, scale):
    n = cap * count
    span = cap * SEG
    return pl.pallas_call(
        functools.partial(forward_kernel, cap, scale),
        out_shape=(
            jax.ShapeDtypeStruct((BINS, span, 512), BF16),
            jax.ShapeDtypeStruct((SEG, n, 384), BF16),
            jax.ShapeDtypeStruct((8, 128), jnp.int32),
        ),
        in_specs=[VM] * 2,
        out_specs=(VM,) * 3,
        scratch_shapes=forward_scratch(cap, count),
        compiler_params=pltpu.CompilerParams(collective_id=cap, has_side_effects=True, vmem_limit_bytes=60 << 20),
        name="forward_lines",
    )(proj, tagt)


def backward_lines(dmixed, lines, table, g, cap, count, scale):
    q = g.shape[0] // 96
    n = cap * count
    span = cap * SEG
    dproj, out = pl.pallas_call(
        functools.partial(backward_kernel, cap, scale),
        out_shape=(
            jax.ShapeDtypeStruct((BINS, span, 1536), BF16),
            jax.ShapeDtypeStruct(g.shape, BF16),
        ),
        in_specs=[VM] * 4,
        out_specs=(VM,) * 2,
        scratch_shapes=[
            pltpu.VMEM((count, span, 128), BF16),
            pltpu.VMEM((1, count * span, 128), F32),
            pltpu.VMEM((n, 128), BF16),
            pltpu.VMEM((n, n), BF16),
            pltpu.VMEM((SEG, n, 128), BF16),
            pltpu.VMEM((SEG, n, 384), BF16),
            pltpu.VMEM((3, count * span, 128), F32),
            pltpu.VMEM((count, span, 384), BF16),
            pltpu.SemaphoreType.DMA((4,)),
        ]
        + reducer_scratch(q),
        compiler_params=pltpu.CompilerParams(collective_id=10 + cap, has_side_effects=True, vmem_limit_bytes=60 << 20),
        name="backward_lines",
    )(dmixed, lines, table, g)
    return dproj, out


def step_back_kernel(scale, dmixed, lines, table, activated, upstream, normed_mlp, dpre, mixed, dhidden_b, normed, w_qkv,
                     unit, inv, dhidden, gain, mlp_gain_sum, pack, grad_states, early, late, gains_out,
                     recv, wide128, gathered, sorter, dlines_in, dlines, wide32, back, dproj, g, g_late, shifted, sems, *scratch):
    me = lax.axis_index("space")
    cap = 4
    count = recv.shape[0]
    red = Reducer(me, g, early, *scratch[:9])
    red_late = Reducer(me, g_late, late, *scratch[9:18])
    slots, held, gsend, grecv = scratch[18:]
    gain_refs = (held, gsend, grecv)

    def blocks(j, width=512):
        return pl.ds(pl.multiple_of(j * width, width), width)

    def down_sum(j, carry):
        g[blocks(j), :] = dot(activated[:, blocks(j)], upstream[...], TN).astype(BF16)
        return carry

    def up_sum(j, carry):
        g[blocks(j + 4), :] = dot(normed_mlp[...], dpre[:, blocks(j)], TN).astype(BF16)
        return carry

    def work():
        lax.fori_loop(0, 4, down_sum, 0)
        lax.fori_loop(0, 4, up_sum, 0)
        g[pl.ds(4096, 512), :] = dot(mixed[...], dhidden_b[...], TN).astype(BF16)

    greet_all(me, count, True)
    send_to_lines(me, count, 1, dmixed, recv, sems.at[0], sems.at[1])
    work()
    red.start()
    build_sorter(table[...], sorter)
    await_bytes(recv, sems.at[1])
    sort_blocks(cap, recv, wide128, gathered, sorter, dlines_in)
    attend = backward_tiles(scale, lines, dlines_in, dlines)
    tiles = cap * count // TILE
    lax.fori_loop(0, tiles // 2, attend, 0, unroll=2)
    red.step(0)
    lax.fori_loop(tiles // 2, tiles, attend, 0, unroll=2)
    unsort_blocks(cap, dlines, wide32, sorter, back)
    send_home(me, count, 3, back, dproj, sems.at[2], sems.at[3])
    red.step(1)
    red.step(2)
    await_bytes(dproj, sems.at[3])
    rows = BINS * cap * SEG

    def late_sum(j, carry):
        rhs = dproj[:, :, blocks(j)].reshape(rows, 512)
        g_late[blocks(j), :] = dot(normed[...], rhs, TN).astype(BF16)
        return carry

    lax.fori_loop(0, 3, late_sum, 0)
    red_late.start()

    def norm_chunk(i, total):
        part = pl.ds(pl.multiple_of(i * 128, 128), 128)
        dn = dot(dproj[pl.ds(i * 4, 4)].reshape(128, 1536), w_qkv[...], NT).astype(BF16).astype(F32)
        u = unit[part, :]
        shifted[part, :] = (dhidden[part, :] + norm_back(u, inv[part, :], gain[...], dn)).astype(BF16)
        return total + jnp.sum(u * dn, axis=0, keepdims=True)

    total = lax.fori_loop(0, rows // 128, norm_chunk, jnp.zeros((1, 512), F32))
    for j in range(4):
        held[0, pl.ds(j, 1), :] = total[:, 128 * j : 128 * (j + 1)]
    held[0, pl.ds(4, 4), :] = mlp_gain_sum[...]
    sum_gains(0, red, slots, gain_refs)
    red_late.step(0)
    grad_states[...] = dot(pack[...], shifted[...], TN).astype(BF16)
    for stage in range(7):
        if stage > 0:
            red_late.step(stage)
        if stage == 0:
            red.step(3)
        if stage == 1:
            red.step(4)
        if stage == 2:
            red.step(5)
        if stage == 5:
            red.step(6)
        if stage < 4:
            some = gather_gains(stage, slots, gain_refs)
            if stage < 3:
                held[stage + 1] = some
                sum_gains(stage + 1, red, slots, gain_refs)
            else:
                gains_out[...] = some
    for p in range(3):
        red.wait(7, p)
        red_late.wait(7, p)
    red.finish()
    red_late.finish()
    for stage in range(4):
        await_bytes(slots.at[stage, pl.ds(0, 1 if stage == 0 else 3)], gsend.at[stage])
    await_bytes(recv.at[pl.ds(0, count - 1)], sems.at[0])
    await_bytes(back.at[pl.ds(0, count - 1)], sems.at[2])


def step_back(scale, *args):
    cap, count = 4, 64
    n = cap * count
    span = cap * SEG
    rows = BINS * span
    out = pl.pallas_call(
        functools.partial(step_back_kernel, scale),
        out_shape=(
            jax.ShapeDtypeStruct((512, 512), BF16),
            jax.ShapeDtypeStruct((4608, 512), BF16),
            jax.ShapeDtypeStruct((1536, 512), BF16),
            jax.ShapeDtypeStruct((8, 128), F32),
        ),
        in_specs=[VM] * len(args),
        out_specs=(VM,) * 4,
        scratch_shapes=[
            pltpu.VMEM((count, span, 128), BF16),
            pltpu.VMEM((1, count * span, 128), F32),
            pltpu.VMEM((n, 128), BF16),
            pltpu.VMEM((n, n), BF16),
            pltpu.VMEM((SEG, n, 128), BF16),
            pltpu.VMEM((SEG, n, 384), BF16),
            pltpu.VMEM((3, count * span, 128), F32),
            pltpu.VMEM((count, span, 384), BF16),
            pltpu.VMEM((BINS, span, 1536), BF16),
            pltpu.VMEM((4608, 512), BF16),
            pltpu.VMEM((1536, 512), BF16),
            pltpu.VMEM((rows, 512), BF16),
            pltpu.SemaphoreType.DMA((4,)),
        ]
        + reducer_scratch(48)
        + reducer_scratch(16)
        + [
            pltpu.VMEM((4, 4, 8, 128), F32),
            pltpu.VMEM((4, 8, 128), F32),
            pltpu.SemaphoreType.DMA((4,)),
            pltpu.SemaphoreType.DMA((4,)),
        ],
        compiler_params=pltpu.CompilerParams(collective_id=30, has_side_effects=True, vmem_limit_bytes=62 << 20),
        name="step_back",
    )(*args)
    return out


def route_four(me, owner_r, place_r, pack, tagt):
    n = 64
    owner_r, place_r = owner_r.astype(F32), place_r.astype(F32)
    rows = lax.broadcasted_iota(jnp.int32, (n, n), 0)
    cols = lax.broadcasted_iota(jnp.int32, (n, n), 1)

    def one(mask):
        return jnp.where(mask, 1.0, 0.0)

    owner_c = jnp.sum(one(rows == cols) * owner_r, axis=1, keepdims=True)
    same = one(owner_c == owner_r)
    rank_r = jnp.sum(same * one(rows < cols), axis=0, keepdims=True)
    rank_c = jnp.sum(same * one(cols < rows), axis=1, keepdims=True)
    load_r = jnp.sum(same, axis=0, keepdims=True)
    load_c = jnp.sum(same, axis=1, keepdims=True)
    first = one(rank_c == 0.0)
    index = jnp.sum(first * one(load_c == load_r) * one(owner_c < owner_r), axis=0, keepdims=True)
    n3 = jnp.sum(first * one(load_c == 3.0), axis=0, keepdims=True)
    n2 = jnp.sum(first * one(load_c == 2.0), axis=0, keepdims=True)
    base1 = jnp.where(index < n3, 4.0 * index + 3.0, 3.0 * n3 + 2.0 * n2 + index)
    base = jnp.where(load_r == 3.0, 4.0 * index, jnp.where(load_r == 2.0, 4.0 * n3 + 2.0 * index, base1))
    slot = base + rank_r
    tag = (base - 4.0 * jnp.floor(base * 0.25)) * n + place_r + 1.0
    spread = one(lax.div(lax.broadcasted_iota(jnp.int32, (n, 512), 1), SEG) == lax.broadcasted_iota(jnp.int32, (n, 512), 0))
    target = dot(jnp.broadcast_to(slot, (8, n)).astype(BF16), spread.astype(BF16), NN)[0:1]
    target = target * SEG + lax.rem(lax.broadcasted_iota(jnp.int32, (1, 512), 1), SEG).astype(F32)
    ids = lax.broadcasted_iota(jnp.int32, (512, 512), 0).astype(F32)
    pack[...] = one(ids == target).astype(BF16)
    tags = jnp.sum(one(rows.astype(F32) == slot) * tag, axis=1, keepdims=True)
    lane = lax.broadcasted_iota(jnp.int32, (1, 128), 1)
    tagt[...] = jnp.zeros_like(tagt)
    for b in range(BINS):
        for s in range(2):
            i = 4 * b + 2 * s
            row = jnp.where(lane == me, tags[i : i + 1], jnp.where(lane == me + n, tags[i + 1 : i + 2], 0.0))
            tagt[b, pl.ds(s, 1), :] = row.astype(jnp.int32)


def step_forward_kernel(scale, states, cotangent, owner_r, place_r, gain, w_qkv, mixed, lines, table, pack, upstream,
                        flat_b, normed, unit, inv, proj, tagt, *scratch):
    me = lax.axis_index("space")

    def work():
        route_four(me, owner_r[...], place_r[...], pack, tagt)

        def chunk(i, carry):
            part = pl.ds(pl.multiple_of(i * 128, 128), 128)
            f = dot(pack[part, :], states[...], NN).astype(BF16)
            flat_b[part, :] = f
            u, v = norm_stats(f.astype(F32))
            unit[part, :] = u
            inv[part, :] = v
            x = (u * gain[...]).astype(BF16)
            normed[part, :] = x
            proj[pl.ds(i * 4, 4)] = dot(x, w_qkv[...], NN).astype(BF16).reshape(4, 32, 1536)
            upstream[part, :] = dot(pack[part, :], cotangent[...], NN).astype(BF16)
            return carry

        lax.fori_loop(0, 4, chunk, 0)

    forward_kernel(4, scale, proj, tagt, mixed, lines, table, *scratch, work=work)


def step_forward(scale, *args):
    cap, count = 4, 64
    n = cap * count
    span = cap * SEG
    return pl.pallas_call(
        functools.partial(step_forward_kernel, scale),
        out_shape=(
            jax.ShapeDtypeStruct((BINS, span, 512), BF16),
            jax.ShapeDtypeStruct((SEG, n, 384), BF16),
            jax.ShapeDtypeStruct((8, 128), jnp.int32),
            jax.ShapeDtypeStruct((512, 512), BF16),
            jax.ShapeDtypeStruct((512, 512), BF16),
            jax.ShapeDtypeStruct((512, 512), BF16),
            jax.ShapeDtypeStruct((512, 512), BF16),
            jax.ShapeDtypeStruct((512, 512), F32),
            jax.ShapeDtypeStruct((512, 1), F32),
        ),
        in_specs=[VM] * len(args),
        out_specs=(VM,) * 9,
        scratch_shapes=[pltpu.VMEM((BINS, span, 1536), BF16), pltpu.VMEM((BINS, 8, 128), jnp.int32)]
        + forward_scratch(cap, count),
        compiler_params=pltpu.CompilerParams(collective_id=31, has_side_effects=True, vmem_limit_bytes=60 << 20),
        name="step_forward",
    )(*args)


def fits_four(owner):
    same = owner[:, None] == owner[None, :]
    load = jnp.sum(same, axis=1, dtype=jnp.int32)
    threes = jnp.sum(load == 3, dtype=jnp.int32)
    twos = jnp.sum(load == 2, dtype=jnp.int32)
    return 4 * threes + 3 * twos <= 3 * owner.shape[0]


def per_device(*args):
    return lax.cond(fits_four(args[2]), functools.partial(block, 4), functools.partial(block, 6), *args)


def block(
    cap, states, cotangent, send_owner, line_place, gain_attn, w_qkv, w_out, gain_mlp, w_up, w_down
):
    width = states.shape[2]
    rows = states.shape[1]
    nspace = lax.axis_size("space")
    total_rows = rows * nspace * lax.axis_size("dp")
    nblocks = send_owner.shape[0]
    slots = BINS * cap
    wide = 2 * (width // HEADS)
    head_dim = width // HEADS
    scale = head_dim ** (-0.5)
    span = cap * SEG
    if cap == 4:
        mixed, lines, table, pack, upstream, flat_b, normed, unit_a, inv_a = step_forward(
            scale, states[0], cotangent[0], send_owner[None], line_place[None], gain_attn[None], w_qkv
        )
        flat = flat_b.astype(F32)
        mixed = mixed.reshape(BINS * span, width)
    else:
        slot, tag = routing(send_owner, line_place, cap)
        me = lax.axis_index("space")
        hit = slot[None, :] == jnp.arange(slots, dtype=jnp.int32)[:, None]
        tags = jnp.sum(jnp.where(hit, tag[None, :] + 1, 0), axis=1).reshape(BINS, cap // 2, 2)
        tags = jnp.pad(tags, ((0, 0), (0, 8 - cap // 2), (0, 0)))
        at_me = jnp.arange(nspace, dtype=jnp.int32) == me
        tagt = jnp.where(at_me[None, None, None, :], tags[..., None], 0).reshape(BINS, 8, 2 * nspace)
        target = (slot[:, None] * SEG + jnp.arange(SEG, dtype=jnp.int32)[None, :]).reshape(rows)
        pack = (jnp.arange(slots * SEG, dtype=jnp.int32)[:, None] == target[None, :]).astype(BF16)

        flat_b = dot(pack, states[0], NN).astype(BF16)
        upstream = dot(pack, cotangent[0], NN).astype(BF16)
        flat = flat_b.astype(F32)
        unit_a, inv_a = norm_stats(flat)
        normed = (unit_a * gain_attn).astype(BF16)
        projected = dot(normed, w_qkv, NN).astype(BF16)
        mixed, lines, table = forward_lines(projected.reshape(BINS, span, 3 * width), tagt, cap, nspace, scale)
        mixed = mixed.reshape(BINS * span, width)

    hidden = (flat + dot(mixed, w_out, NN)).astype(BF16)
    hidden32 = hidden.astype(F32)
    unit_m, inv_m = norm_stats(hidden32)
    normed_mlp = (unit_m * gain_mlp).astype(BF16)
    act32, slope = gelu_parts(dot(normed_mlp, w_up, NN))
    activated = act32.astype(BF16)
    output = (hidden32 + dot(activated, w_down, NN)).astype(BF16)
    dpre = (slope * dot(upstream, w_down, NT)).astype(BF16)
    dnormed_mlp = dot(dpre, w_up, NT)
    grad_gain_mlp = jnp.sum(unit_m * dnormed_mlp, axis=0)
    dhidden = upstream.astype(F32) + norm_back(unit_m, inv_m, gain_mlp, dnormed_mlp)
    dhidden_b = dhidden.astype(BF16)
    dmixed = dot(dhidden_b, w_out, NT).astype(BF16)
    output = dot(pack, output, TN).astype(BF16)
    if cap == 4:
        grad_states, early, late, gains = step_back(
            scale, dmixed.reshape(BINS, span, width), lines, table, activated, upstream, normed_mlp, dpre, mixed, dhidden_b,
            normed, w_qkv, unit_a, inv_a, dhidden, gain_attn[None], grad_gain_mlp.reshape(4, 128), pack,
        )
    else:
        early = [dot(activated, upstream, TN)]
        early += [dot(normed_mlp, dpre[:, j * width : (j + 1) * width], TN) for j in range(4)]
        early += [dot(mixed, dhidden_b, TN)]
        early = jnp.concatenate([v.astype(BF16) for v in early], axis=0)

        dprojected, early = backward_lines(dmixed.reshape(BINS, span, width), lines, table, early, cap, nspace, scale)
        dprojected = dprojected.reshape(BINS * span, 3 * width)
        late = [dot(normed, dprojected[:, j * width : (j + 1) * width], TN) for j in range(3)]
        late = jnp.concatenate([v.astype(BF16) for v in late], axis=0)
        dnormed = dot(dprojected, w_qkv, NT).astype(BF16).astype(F32)
        grad_gain_attn = jnp.sum(unit_a * dnormed, axis=0)
        grad_states = (dhidden + norm_back(unit_a, inv_a, gain_attn, dnormed)).astype(BF16)
        grad_states = dot(pack, grad_states, TN).astype(BF16)
        late, gains = reduce_tail(cap, late, jnp.concatenate([grad_gain_attn, grad_gain_mlp]).reshape(8, 128))
    factor = 1.0 / math.sqrt(total_rows)
    gains = gains.reshape(2, width) * factor
    hidden_units = w_up.shape[1]

    def columns(blocks):
        blocks = blocks.reshape(-1, width, width)
        return jnp.concatenate([blocks[j].astype(F32) * factor for j in range(blocks.shape[0])], axis=1)

    return (
        output[None],
        grad_states[None],
        gains[0],
        columns(late),
        early[2 * hidden_units :].astype(F32) * factor,
        gains[1],
        columns(early[hidden_units : 2 * hidden_units]),
        early[:hidden_units].astype(F32) * factor,
    )


def solution(mesh):
    placed = (
        P("dp", "space", None),
        P("dp", "space", None),
        P("space"),
        P("space"),
        P(),
        P(),
        P(),
        P(),
        P(),
        P(),
    )
    return jax.shard_map(
        per_device,
        mesh=mesh,
        in_specs=placed,
        out_specs=(P("dp", "space", None), P("dp", "space", None), P(), P(), P(), P(), P(), P()),
        check_vma=False,
    )
```
